256 devices in a mesh: load: 8 (over z), dom: 32 (over x, y, core).
Axes of the slice: x: 4, y: 4, z: 8, core: 2. Of those that a mesh axis runs over, the one named last changes fastest.
Arguments:
- displacement: float32 [8, 6, 262144], P('load', None, 'dom'), may hold values from -6 to 6
- adjoint: float32 [8, 6, 262144], P('load', None, 'dom'), may hold values from -0.12 to 0.12
- send_list: int32 [32, 32, 512], P('dom'), may hold values from 0 to 8191
- connect: int32 [4, 262144], P(None, 'dom'), may hold values from 0 to 11263, as said below
- elem_comp: int32 [262144], P('dom'), may hold values from 0 to 399, as said below
- elem_dv: int32 [262144], P('dom'), may hold values from 0 to 65535, as said below
- thickness: float32 [65536], P('dom'), may hold values from 0.5 to 1.5
- multiplier: float32 [8, 400], P('load'), may hold values from 0.2 to 2
- k_memb: float32 [24, 24], replicated, may hold values from -1.25 to 1.25
- k_bend: float32 [24, 24], replicated, may hold values from -1.25 to 1.25
- s_memb: float32 [8, 24], replicated, may hold values from -1.25 to 1.25
- s_bend: float32 [8, 24], replicated, may hold values from -1.25 to 1.25
Outputs:
- ks_value: float32 [8, 400], P('load')
- sensitivity: float32 [65536], P('dom')
The draws below stay inside these ranges and needn't reach their ends.
Inputs may be any that keep to these rules, and one draw needn't show every extreme that they name: `connect`: an entry below 8192 is an own node of the element's partition; an entry v of 8192 or more refers to row (v - 8192) % 512 of the interface block received from a partition at most 3 places away in cyclic partition order. Some block is referenced up to its last row. `elem_comp`: every component has elements. `elem_dv`: in each aligned block of 1024 elements, at most 64 elements name variables of one owner partition (variables d with the same d // 2048); in every block some owner has exactly 64.
All inputs are finite; a program needn't handle non-finite values.
Results may differ from the reference program's by a relative error of at most 0.0003.
Values sent between devices are 32-bit elements; how exact they have to be, the bound alone decides.
No kernel may reach another device: no remote copies, remote signals or barrier semaphores. Data moves between devices by JAX's collectives and lax.ppermute only.
A program may use at most 64 MiB of HBM per device.

```python
import math
import jax
import jax.numpy as jnp
from jax import lax

DOF = 6
NPE = 4
STR = 8
NBR = 3
COMP = 400
NODE_DEV = 8192
ELEM_DEV = 8192
IFACE = 512
DV_DEV = 2048
LOADS = 8
NODES = 262144
ELEMS = 262144
NDV = 65536
SLICE = 1024
CAP = 64
N_DOM = 32


def draw_connect(key, part):
    domains = ELEMS // ELEM_DEV
    slots = 2 * NBR
    levels = jax.random.randint(jax.random.fold_in(key, 11), (domains, slots), 0, 3)
    counts = IFACE // jnp.array([1, 2, 4], dtype=jnp.int32)[levels]
    pick = jax.random.randint(jax.random.fold_in(key, 12), (), 0, domains * slots)
    flat = jnp.arange(domains * slots, dtype=jnp.int32).reshape(domains, slots)
    counts = jnp.where(flat == pick, IFACE, counts)
    owner = (jnp.arange(ELEMS, dtype=jnp.int32) // ELEM_DEV)[None, :]
    shape = (NPE, ELEMS)
    ghost = jax.random.randint(jax.random.fold_in(key, 13), shape, 0, 8) == 0
    local = jax.random.randint(jax.random.fold_in(key, 14), shape, 0, NODE_DEV)
    slot = jax.random.randint(jax.random.fold_in(key, 15), shape, 0, slots)
    limit = counts[jnp.broadcast_to(owner, shape), slot]
    row = jax.random.randint(jax.random.fold_in(key, 16), shape, 0, 1 << 20) % limit
    value = jnp.where(ghost, NODE_DEV + slot * IFACE + row, local)
    corner = pick // slots * ELEM_DEV
    value = value.at[0, corner].set(NODE_DEV + pick % slots * IFACE + IFACE - 1)
    return value.astype(jnp.int32)


def draw_elem_comp(key, part):
    domains = ELEMS // ELEM_DEV
    index = jnp.arange(ELEMS, dtype=jnp.int32)
    owner = index // ELEM_DEV
    spread = max(3 * COMP // domains, 4)
    base = owner * COMP // domains
    comp = (base + jax.random.randint(jax.random.fold_in(key, 21), (ELEMS,), 0, spread)) % COMP
    comp = jnp.where(index < COMP, index, comp)
    return comp.astype(jnp.int32)


def draw_elem_dv(key, part):
    domains = NDV // DV_DEV
    blocks = ELEMS // SLICE
    width = domains * CAP

    def one_block(block_key):
        values = jax.random.permutation(jax.random.fold_in(block_key, 1), width).astype(jnp.int32)
        owners = values // CAP
        full = jax.random.randint(jax.random.fold_in(block_key, 2), (), 0, domains)
        score = jnp.where(owners == full, 0, 1) * width + jnp.arange(width, dtype=jnp.int32)
        order = jnp.argsort(score)
        chosen = owners[order][:SLICE]
        mixing = jax.random.permutation(jax.random.fold_in(block_key, 3), SLICE)
        chosen = chosen[mixing]
        within = jax.random.randint(jax.random.fold_in(block_key, 4), (SLICE,), 0, DV_DEV)
        return (chosen * DV_DEV + within).astype(jnp.int32)
    block_keys = jax.random.split(jax.random.fold_in(key, 31), blocks)
    return jax.vmap(one_block)(block_keys).reshape(ELEMS).astype(jnp.int32)


def set_ends(entries, key, least, largest):
    dims = entries.shape
    spot = [jax.random.randint(jax.random.fold_in(key, axis), (), 0, dims[axis]) for axis in range(len(dims))]
    entries = entries.at[tuple(spot)].set(least)
    longest = dims.index(max(dims))
    spot[longest] = (spot[longest] + 1) % dims[longest]
    return entries.at[tuple(spot)].set(largest)


def block_scale(key, shape, cuts, smallest, top_value):
    gain = 1.0
    for position, shards_of in cuts:
        draws = jax.random.uniform(jax.random.fold_in(jax.random.fold_in(key, 6), position), (shards_of,), jnp.float32, smallest / len(cuts), top_value / len(cuts))
        gain = gain * jnp.repeat(jnp.exp(draws), shape[position] // shards_of).reshape((-1,) + (1,) * (len(shape) - 1 - position))
    return gain


def scatter_about(stream_key, extent, scale, most, cuts=(), kind=jnp.bfloat16):
    entries = jax.random.normal(stream_key, extent, jnp.float32) * scale
    if len(cuts) > 0:
        entries = block_scale(stream_key, extent, cuts, -0.22, 0.18) * entries
    return jnp.clip(entries, min=-most, max=most).astype(kind)


def setup_inputs(seed: int = 0) -> dict:
    splits = jax.random.split(jax.random.key(seed), 13)
    displacement = scatter_about(splits[0], (LOADS, DOF, NODES), 1.0, 6.0, ((0, 8), (2, 32)), jnp.float32)
    adjoint = scatter_about(splits[1], (LOADS, DOF, NODES), 0.02, 0.12, ((0, 8), (2, 32)), jnp.float32)
    send_list = set_ends(jax.random.randint(splits[2], (N_DOM, N_DOM, IFACE), 0, NODE_DEV), jax.random.fold_in(splits[2], 1), 0, NODE_DEV - 1).astype(jnp.int32)
    connect = draw_connect(jax.random.fold_in(splits[12], 71), 0)
    elem_comp = draw_elem_comp(jax.random.fold_in(splits[12], 71), 0)
    elem_dv = draw_elem_dv(jax.random.fold_in(splits[12], 71), 0)
    thickness = jnp.clip(jnp.exp(math.log(1.5) - 1.0986123 * jax.random.uniform(splits[6], (NDV,), jnp.float32) ** block_scale(splits[6], (NDV,), ((0, 32),), -0.2, 0.2)), 0.5, 1.5)
    multiplier = jnp.clip(jnp.exp(math.log(2.0) - 2.3025851 * jax.random.uniform(splits[7], (LOADS, COMP), jnp.float32) ** block_scale(splits[7], (LOADS, COMP), ((0, 8),), -0.2, 0.2)), 0.2, 2.0)
    k_memb = scatter_about(splits[8], (DOF * NPE, DOF * NPE), (DOF * NPE) ** -0.5, 1.25, (), jnp.float32)
    k_bend = scatter_about(splits[9], (DOF * NPE, DOF * NPE), (DOF * NPE) ** -0.5, 1.25, (), jnp.float32)
    s_memb = scatter_about(splits[10], (STR, DOF * NPE), (DOF * NPE) ** -0.5, 1.25, (), jnp.float32)
    s_bend = scatter_about(splits[11], (STR, DOF * NPE), (DOF * NPE) ** -0.5, 1.25, (), jnp.float32)
    return {"displacement": displacement, "adjoint": adjoint, "send_list": send_list, "connect": connect, "elem_comp": elem_comp, "elem_dv": elem_dv, "thickness": thickness, "multiplier": multiplier, "k_memb": k_memb, "k_bend": k_bend, "s_memb": s_memb, "s_bend": s_bend}


def cycle_offsets(reach):
    return [j - reach if j < reach else j - reach + 1 for j in range(2 * reach)]


def reference(displacement, adjoint, send_list, connect, elem_comp, elem_dv, thickness, multiplier, k_memb, k_bend, s_memb, s_bend):
    offsets = jnp.array(cycle_offsets(NBR), dtype=jnp.int32)
    owner = (jnp.arange(ELEMS, dtype=jnp.int32) // ELEM_DEV)[None, :]
    owners = jnp.broadcast_to(owner, connect.shape).astype(jnp.int32)
    ghost = connect >= NODE_DEV
    spot = jnp.maximum(connect - NODE_DEV, 0).astype(jnp.int32)
    source = ((owners + offsets[spot // IFACE]) % N_DOM).astype(jnp.int32)
    remote = send_list[source, owners, spot % IFACE]
    node_of = jnp.where(ghost, source * NODE_DEV + remote, owners * NODE_DEV + connect).astype(jnp.int32)
    panel = thickness[elem_dv]
    high = lax.Precision.HIGHEST

    def one_load(inputs):
        disp, adj, weights = inputs
        states = jnp.concatenate([disp, adj], axis=0)
        local = jnp.take(states, node_of, axis=1).reshape(2, -1, ELEMS)
        motion = local[0]
        costate = local[1]
        bending = jnp.dot(s_bend, motion, precision=high)
        stress = jnp.dot(s_memb, motion, precision=high) + panel * bending
        failure = jnp.sum(stress * stress, axis=0) / STR
        peak = jax.ops.segment_max(failure, elem_comp, num_segments=COMP)
        scaled = jnp.exp(50.0 * (failure - peak[elem_comp]))
        total = jax.ops.segment_sum(scaled, elem_comp, num_segments=COMP)
        ks = peak + jnp.log(total) / 50.0
        explicit = weights[elem_comp] * scaled / total[elem_comp] * (2.0 / STR) * jnp.sum(stress * bending, axis=0)
        stiff = jnp.dot(k_memb, motion, precision=high) + 3.0 * panel * panel * jnp.dot(k_bend, motion, precision=high)
        implicit = jnp.sum(costate * stiff, axis=0)
        partial_sum = jax.ops.segment_sum(explicit + implicit, elem_dv, num_segments=NDV)
        return ks, partial_sum

    ks_all, partials = lax.map(one_load, (displacement, adjoint, multiplier))
    return ks_all, jnp.sum(partials, axis=0)
```

```python
import functools

import jax
import jax.numpy as jnp
from jax import lax
from jax.experimental import pallas as pl
from jax.experimental.pallas import tpu as pltpu
from jax.sharding import PartitionSpec as P

NBR = 3
SHARP = 50.0
LOW = -1e30
LANES = 128
DISP_TOP = 8388600.0
ADJ_TOP = 131000.0
ADJ_MID = 131072
OFFSETS = tuple(j - NBR if j < NBR else j - NBR + 1 for j in range(2 * NBR))
I32 = jnp.int32
F32 = jnp.float32


def from_everyone(x, axis):
    count = lax.axis_size(axis)
    return lax.all_to_all(jnp.broadcast_to(x[None], (count, *x.shape)), axis, 0, 0, tiled=True)


def lane_pick(table, index):
    return jnp.take_along_axis(table, index, axis=1, mode="promise_in_bounds")


def row_shifts(rows):
    row = lax.broadcasted_iota(I32, (rows, LANES), 0)
    return (row % 3) * 10


def scales_of(x_of, count, top):
    best = jnp.abs(x_of(0))
    for h in range(1, count):
        best = jnp.maximum(best, jnp.abs(x_of(h)))
    most = jnp.maximum(jnp.max(best, axis=1, keepdims=True), 1e-30)
    return top / most, most / top


def pack_tile(x, y, x_inv, y_inv, store):
    q = jnp.floor(x * x_inv + 0.5).astype(I32)
    u = jnp.floor(y * y_inv + 0.5).astype(I32) + ADJ_MID
    store(0, 6, (q << 8) | (u & 255))
    high = (u >> 8) << row_shifts(6)
    store(6, 1, high[0:1] + high[1:2] + high[2:3])
    store(7, 1, high[3:4] + high[4:5] + high[5:6])


def unpack_tile(word, x_scale, y_scale):
    x = (word >> 8).astype(F32) * x_scale
    row = lax.broadcasted_iota(I32, (8, LANES), 0)
    first = jnp.broadcast_to(word[6:7], (8, LANES))
    second = jnp.broadcast_to(word[7:8], (8, LANES))
    high = (jnp.where(row < 3, first, second) >> row_shifts(8)) & 1023
    y = (((high << 8) | (word & 255)) - ADJ_MID).astype(F32) * y_scale
    return x, y


def pad_rows(column):
    return jnp.concatenate([jnp.broadcast_to(column, (6, LANES)), jnp.zeros((2, LANES), F32)], axis=0)


def pick_pair(table_of, count, first_high, indices, starts):
    lows = [i & 127 for i in indices]
    highs = [(i >> 7) - first_high for i in indices]
    found = list(starts)
    for h in range(count):
        tile = table_of(h)
        for u in range(len(indices)):
            found[u] = jnp.where(highs[u] == h, lane_pick(tile, lows[u]), found[u])
    return found


def send_kernel(here_ref, disp_ref, adj_ref, list_ref, thick_ref, packed_ref, scale_ref, send_ref, *, chunks, domains, iface):
    rows = iface // LANES
    cut = lambda ref, h: ref[:, h * LANES : (h + 1) * LANES]
    x_inv, x_scale = scales_of(lambda h: cut(disp_ref, h), chunks, DISP_TOP)
    y_inv, y_scale = scales_of(lambda h: cut(adj_ref, h), chunks, ADJ_TOP)
    scale_ref[0:8] = jnp.zeros((8, LANES), F32)
    scale_ref[8:16] = jnp.zeros((8, LANES), F32)
    scale_ref[0:6] = jnp.broadcast_to(x_scale, (6, LANES))
    scale_ref[8:14] = jnp.broadcast_to(y_scale, (6, LANES))
    xs = scale_ref[0:8]
    ys = scale_ref[8:16]
    x_inv = jnp.broadcast_to(x_inv, (6, LANES))
    y_inv = jnp.broadcast_to(y_inv, (6, LANES))
    for h in range(chunks):

        def store(row, many, value, h=h):
            packed_ref[h * 8 + row : h * 8 + row + many] = value

        pack_tile(cut(disp_ref, h), cut(adj_ref, h), x_inv, y_inv, store)

    def thickness_rows(k, half):
        return thick_ref[k * 4 + half * 2 : k * 4 + half * 2 + 2]

    @pl.loop(0, domains)
    def _(d):
        for k in range(rows):
            for half in range(2):
                at = k * 16 + half * 8
                send_ref[d, at : at + 6] = jnp.zeros((6, LANES), F32)
                send_ref[d, at + 6 : at + 8] = thickness_rows(k, half)

    here = here_ref[0]
    row_ids = lax.broadcasted_iota(I32, (8, LANES), 0)

    def listed(target, k):
        base = pl.multiple_of(target // 8 * 8, 8)
        tile = list_ref[pl.ds(base, 8), k * LANES : (k + 1) * LANES]
        row = jnp.sum(jnp.where(row_ids == target - base, tile, 0), axis=0, keepdims=True)
        return jnp.broadcast_to(row, (8, LANES))

    for offset in OFFSETS:
        target = lax.rem(here - offset + domains, domains)
        for k in range(0, rows, 2):
            picked = pick_pair(
                lambda h: packed_ref[h * 8 : h * 8 + 8],
                chunks,
                0,
                [listed(target, k + u) for u in range(2)],
                [jnp.zeros((8, LANES), I32)] * 2,
            )
            for u in range(2):
                x, y = unpack_tile(picked[u], xs, ys)
                at = (k + u) * 16
                send_ref[target, at : at + 6] = x[0:6]
                send_ref[target, at + 8 : at + 14] = y[0:6]


def own_kernel(packed_ref, connect_ref, got_ref, *, chunks, groups):
    @pl.loop(0, groups)
    def _(b):
        lanes = pl.ds(pl.multiple_of(b * LANES, LANES), LANES)
        for a in range(0, 4, 2):
            found = pick_pair(
                lambda h: packed_ref[h * 8 : h * 8 + 8],
                chunks,
                0,
                [jnp.broadcast_to(connect_ref[a + u : a + u + 1, lanes], (8, LANES)) for u in range(2)],
                [jnp.zeros((8, LANES), I32)] * 2,
            )
            for u in range(2):
                got_ref[pl.ds(pl.multiple_of(b * 32 + (a + u) * 8, 8), 8)] = found[u]


def spread_matrix(flip):
    shape = (24, 32) if not flip else (32, 24)
    narrow = lax.broadcasted_iota(I32, shape, 1 if flip else 0)
    wide = lax.broadcasted_iota(I32, shape, 0 if flip else 1)
    hit = (narrow // 4 == wide % 8) & (narrow % 4 == wide // 8)
    return jnp.where(hit, 1.0, 0.0).astype(F32)


def dot(a, b):
    return jnp.dot(a, b, precision=lax.Precision.HIGHEST, preferred_element_type=F32)


def main_kernel(
    here_ref,
    recv_ref,
    packed_scale_ref,
    got_ref,
    connect_ref,
    comp_ref,
    dv_ref,
    s_memb_ref,
    s_bend_ref,
    k_memb_ref,
    k_bend_ref,
    stats_ref,
    slope_ref,
    fixed_ref,
    ghost_ref,
    move_ref,
    cost_ref,
    panel_ref,
    fail_ref,
    *,
    own,
    groups,
    domains,
    iface,
    comps,
):
    rows = iface // LANES
    ghosts = len(OFFSETS) * rows
    here = here_ref[0]
    sources = [lax.rem(here + offset + domains, domains) for offset in OFFSETS]

    def x_of(h):
        return recv_ref[sources[h // rows], (h % rows) * 16 : (h % rows) * 16 + 6]

    def y_of(h):
        return recv_ref[sources[h // rows], (h % rows) * 16 + 8 : (h % rows) * 16 + 14]

    x_inv, x_scale = scales_of(x_of, ghosts, DISP_TOP)
    y_inv, y_scale = scales_of(y_of, ghosts, ADJ_TOP)
    gx = pad_rows(x_scale)
    gy = pad_rows(y_scale)
    x_inv = jnp.broadcast_to(x_inv, (6, LANES))
    y_inv = jnp.broadcast_to(y_inv, (6, LANES))
    for h in range(ghosts):

        def store(row, many, value, h=h):
            ghost_ref[h * 8 + row : h * 8 + row + many] = value

        pack_tile(x_of(h), y_of(h), x_inv, y_inv, store)
    ox = packed_scale_ref[0:8]
    oy = packed_scale_ref[8:16]

    @pl.loop(0, groups)
    def _(b):
        lanes = pl.ds(pl.multiple_of(b * LANES, LANES), LANES)
        for a in range(0, 4, 2):
            indices = [jnp.broadcast_to(connect_ref[a + u : a + u + 1, lanes], (8, LANES)) for u in range(2)]
            found = pick_pair(
                lambda h: ghost_ref[h * 8 : h * 8 + 8],
                ghosts,
                own,
                indices,
                [got_ref[pl.ds(pl.multiple_of(b * 32 + (a + u) * 8, 8), 8)] for u in range(2)],
            )
            for u in range(2):
                far = indices[u] >= own * LANES
                x, y = unpack_tile(found[u], jnp.where(far, gx, ox), jnp.where(far, gy, oy))
                move_ref[(a + u) * 8 : (a + u) * 8 + 8, lanes] = x
                cost_ref[(a + u) * 8 : (a + u) * 8 + 8, lanes] = y

    tiles = groups // 8
    panel_ref[...] = jnp.zeros(panel_ref.shape, F32)

    @pl.loop(0, domains)
    def _(s):
        for t in range(0, tiles, 2):
            indices = [dv_ref[(t + u) * 8 : (t + u) * 8 + 8] for u in range(2)]
            lows = [i & 127 for i in indices]
            highs = [(i >> 7) - s * 16 for i in indices]
            found = [panel_ref[(t + u) * 8 : (t + u) * 8 + 8] for u in range(2)]
            for h in range(16):
                row = (h // 4) * 16 + (h % 4 // 2) * 8 + 6 + h % 2
                tile = jnp.broadcast_to(recv_ref[s, row : row + 1], (8, LANES))
                for u in range(2):
                    found[u] = jnp.where(highs[u] == h, lane_pick(tile, lows[u]), found[u])
            for u in range(2):
                panel_ref[(t + u) * 8 : (t + u) * 8 + 8] = found[u]

    wide = spread_matrix(False)
    tall = spread_matrix(True)
    weights = jnp.concatenate(
        [
            dot(s_memb_ref[...], wide),
            dot(s_bend_ref[...], wide),
            dot(tall, dot(k_memb_ref[...], wide)),
            dot(tall, dot(k_bend_ref[...], wide)),
        ],
        axis=0,
    )

    @pl.loop(0, tiles)
    def _(t):
        lanes = pl.ds(pl.multiple_of(t * 8 * LANES, 8 * LANES), 8 * LANES)
        all_parts = dot(weights, move_ref[:, lanes])
        cost = cost_ref[:, lanes]
        for j in range(8):
            part = all_parts[:, j * LANES : (j + 1) * LANES]
            panel = panel_ref[pl.ds(t * 8 + j, 1)]
            bending = part[8:16]
            stress = part[0:8] + panel * bending
            failure = jnp.sum(stress * stress, axis=0, keepdims=True) / 8.0
            slope = jnp.sum(stress * bending, axis=0, keepdims=True) * (2.0 / 8.0)
            stiff = part[16:48] + (3.0 * panel * panel) * part[48:80]
            implicit = jnp.sum(cost[:, j * LANES : (j + 1) * LANES] * stiff, axis=0, keepdims=True)
            fail_ref[pl.ds(t * 8 + j, 1)] = failure
            slope_ref[pl.ds(t * 8 + j, 1)] = slope
            fixed_ref[pl.ds(t * 8 + j, 1)] = implicit

    stats_ref[0] = jnp.zeros((8, LANES), F32)
    names = lax.broadcasted_iota(I32, (LANES, LANES), 0)
    bands = (comps + LANES - 1) // LANES
    diagonal = lax.broadcasted_iota(I32, (LANES, LANES), 0) == lax.broadcasted_iota(I32, (LANES, LANES), 1)

    def to_row(column):
        return jnp.sum(jnp.where(diagonal, column, 0.0), axis=0, keepdims=True)

    for band in range(bands):

        def peak_step(g, best):
            hit = comp_ref[pl.ds(g, 1)] == names + band * LANES
            return jnp.maximum(best, jnp.where(hit, fail_ref[pl.ds(g, 1)], LOW))

        best = lax.fori_loop(0, groups, peak_step, jnp.full((LANES, LANES), LOW, F32))
        stats_ref[0, band : band + 1] = to_row(jnp.max(best, axis=1, keepdims=True))

    for t in range(tiles):
        block = slice(t * 8, t * 8 + 8)
        comp = comp_ref[block]
        low = comp & 127
        high = comp >> 7
        top = jnp.zeros((8, LANES), F32)
        for band in range(bands):
            tile = jnp.broadcast_to(stats_ref[0, band : band + 1], (8, LANES))
            top = jnp.where(high == band, lane_pick(tile, low), top)
        scaled = jnp.exp(SHARP * (fail_ref[block] - top))
        fail_ref[block] = scaled
        slope_ref[block] = slope_ref[block] * scaled

    for band in range(bands):

        def total_step(g, total):
            hit = comp_ref[pl.ds(g, 1)] == names + band * LANES
            return total + jnp.where(hit, fail_ref[pl.ds(g, 1)], 0.0)

        total = lax.fori_loop(0, groups, total_step, jnp.zeros((LANES, LANES), F32))
        stats_ref[0, 4 + band : 5 + band] = to_row(jnp.sum(total, axis=1, keepdims=True))
    mine = stats_ref[0]
    for d in range(1, domains):
        stats_ref[d] = mine


def last_kernel(
    here_ref, stats_ref, mult_ref, comp_ref, dv_ref, slope_ref, fixed_ref, ks_ref, sum_ref, term_ref, *, domains, comps, groups, slots
):
    here = here_ref[0]
    peak = stats_ref[0, 0:4]
    for s in range(1, domains):
        peak = jnp.maximum(peak, stats_ref[s, 0:4])
    total = jnp.zeros_like(peak)
    for s in range(domains):
        total = total + stats_ref[s, 4:8] * jnp.exp(SHARP * (stats_ref[s, 0:4] - peak))
    ks = peak + jnp.log(total) / SHARP
    share = jnp.exp(SHARP * (stats_ref[here, 0:4] - peak)) / total
    bands = (comps + LANES - 1) // LANES
    weights = []
    for band in range(bands):
        many = min(LANES, comps - band * LANES)
        ks_ref[0:1, band * LANES : band * LANES + many] = ks[band : band + 1, 0:many]
        weights.append(jnp.broadcast_to(share[band : band + 1] * mult_ref[band : band + 1], (8, LANES)))
    tiles = groups // 8
    for t in range(tiles):
        block = slice(t * 8, t * 8 + 8)
        comp = comp_ref[block]
        low = comp & 127
        high = comp >> 7
        weight = jnp.zeros((8, LANES), F32)
        for band in range(bands):
            weight = jnp.where(high == band, lane_pick(weights[band], low), weight)
        term_ref[block] = weight * slope_ref[block] + fixed_ref[block]
    sum_ref[...] = jnp.zeros(sum_ref.shape, F32)
    outer = slots // LANES
    outer_ids = lax.broadcasted_iota(I32, (outer, LANES), 0)
    inner_ids = lax.broadcasted_iota(I32, (LANES, LANES), 0)
    zero = jnp.zeros((), F32)

    @pl.loop(0, tiles)
    def _(t):
        highs = []
        lows = []
        for j in range(8):
            place = dv_ref[pl.ds(t * 8 + j, 1)]
            value = term_ref[pl.ds(t * 8 + j, 1)]
            highs.append(jnp.where(outer_ids == (place >> 7), 1.0, zero).astype(jnp.bfloat16))
            rough = value.astype(jnp.bfloat16).astype(F32)
            fine = value - rough
            hit = inner_ids == (place & 127)
            lows.append(
                jnp.concatenate(
                    [
                        jnp.where(hit, rough, 0.0).astype(jnp.bfloat16),
                        jnp.where(hit, fine, 0.0).astype(jnp.bfloat16),
                    ],
                    axis=0,
                )
            )
        both = lax.dot_general(
            jnp.concatenate(highs, axis=1),
            jnp.concatenate(lows, axis=1),
            (((1,), (1,)), ((), ())),
            preferred_element_type=F32,
        )
        sum_ref[...] += both[:, 0:LANES] + both[:, LANES : 2 * LANES]


def vmem():
    return pl.BlockSpec(memory_space=pltpu.VMEM)


def smem():
    return pl.BlockSpec(memory_space=pltpu.SMEM)


def per_device(
    displacement, adjoint, send_list, connect, elem_comp, elem_dv, thickness, multiplier, k_memb, k_bend, s_memb, s_bend
):
    domains = lax.axis_size("dom")
    here = lax.axis_index("dom").astype(I32).reshape(1)
    comps = multiplier.shape[1]
    nodes = displacement.shape[2]
    elems = connect.shape[1]
    iface = send_list.shape[2]
    own = nodes // LANES
    groups = elems // LANES
    slots = thickness.shape[0] * domains
    block = 4 * iface // LANES * 4
    sds = jax.ShapeDtypeStruct

    packed, scale, send = pl.pallas_call(
        functools.partial(send_kernel, chunks=own, domains=domains, iface=iface),
        out_shape=(sds((own * 8, LANES), I32), sds((16, LANES), F32), sds((domains, block, LANES), F32)),
        in_specs=[smem()] + [vmem()] * 4,
        out_specs=(vmem(),) * 3,
        name="send_pick",
    )(here, displacement[0], adjoint[0], send_list[0], thickness.reshape(-1, LANES))
    recv = lax.all_to_all(send, "dom", 0, 0, tiled=True)
    got = pl.pallas_call(
        functools.partial(own_kernel, chunks=own, groups=groups),
        out_shape=sds((groups * 32, LANES), I32),
        in_specs=[vmem()] * 2,
        out_specs=vmem(),
        name="own_pick",
        cost_estimate=pl.CostEstimate(flops=0, transcendentals=0, bytes_accessed=60_000_000),
    )(packed, connect)
    comp = elem_comp.reshape(-1, LANES)
    dv = elem_dv.reshape(-1, LANES)
    stats, slope, fixed = pl.pallas_call(
        functools.partial(main_kernel, own=own, groups=groups, domains=domains, iface=iface, comps=comps),
        out_shape=(sds((domains, 8, LANES), F32), sds((groups, LANES), F32), sds((groups, LANES), F32)),
        in_specs=[smem()] + [vmem()] * 10,
        out_specs=(vmem(),) * 3,
        scratch_shapes=[
            pltpu.VMEM((len(OFFSETS) * iface // LANES * 8, LANES), I32),
            pltpu.VMEM((32, elems), F32),
            pltpu.VMEM((32, elems), F32),
            pltpu.VMEM((groups, LANES), F32),
            pltpu.VMEM((groups, LANES), F32),
        ],
        name="element_work",
    )(here, recv, scale, got, connect, comp, dv, s_memb, s_bend, k_memb, k_bend)
    everyone = lax.all_to_all(stats, "dom", 0, 0, tiled=True)
    mult = jnp.pad(multiplier[0], (0, 4 * LANES - comps)).reshape(4, LANES)
    ks_value, sums = pl.pallas_call(
        functools.partial(last_kernel, domains=domains, comps=comps, groups=groups, slots=slots),
        out_shape=(sds((1, comps), F32), sds((slots // LANES, LANES), F32)),
        in_specs=[smem()] + [vmem()] * 6,
        out_specs=(vmem(),) * 2,
        scratch_shapes=[pltpu.VMEM((groups, LANES), F32)],
        name="weigh_and_sum",
    )(here, everyone, mult, comp, dv, slope, fixed)
    arrived = lax.all_to_all(sums.reshape(domains, -1, LANES), "dom", 0, 0, tiled=True)
    owned = arrived.sum(axis=0)
    sensitivity = from_everyone(owned, "load").sum(axis=0).reshape(-1)
    return ks_value, sensitivity


def solution(mesh):
    in_specs = (
        P("load", None, "dom"),
        P("load", None, "dom"),
        P("dom", None, None),
        P(None, "dom"),
        P("dom"),
        P("dom"),
        P("dom"),
        P("load", None),
        P(),
        P(),
        P(),
        P(),
    )
    return jax.shard_map(
        per_device, mesh=mesh, in_specs=in_specs, out_specs=(P("load", None), P("dom")), check_vma=False
    )
```

```python
import functools

import jax
import jax.numpy as jnp
from jax import lax
from jax.experimental import pallas as pl
from jax.experimental.pallas import tpu as pltpu
from jax.sharding import PartitionSpec as P

NBR = 3
ROWS = 24
HIGHS = 14
SHARP = 50.0
LOW = -1e30
LANES = 128
DISP_TOP = 8388600.0
ADJ_TOP = 131000.0
ADJ_MID = 131072
OFFSETS = tuple(j - NBR if j < NBR else j - NBR + 1 for j in range(2 * NBR))
I32 = jnp.int32
F32 = jnp.float32
BF16 = jnp.bfloat16


def from_everyone(x, axis):
    count = lax.axis_size(axis)
    return lax.all_to_all(jnp.broadcast_to(x[None], (count, *x.shape)), axis, 0, 0, tiled=True)


def lane_pick(table, index):
    return jnp.take_along_axis(table, index, axis=1, mode="promise_in_bounds")


def row_shifts(rows):
    row = lax.broadcasted_iota(I32, (rows, LANES), 0)
    return (row % 3) * 10


def scales_of(x_of, count, top):
    best = jnp.abs(x_of(0))
    for h in range(1, count):
        best = jnp.maximum(best, jnp.abs(x_of(h)))
    most = jnp.maximum(jnp.max(best, axis=1, keepdims=True), 1e-30)
    return top / most, most / top


def pack_tile(x, y, x_inv, y_inv, store):
    q = jnp.floor(x * x_inv + 0.5).astype(I32)
    u = jnp.floor(y * y_inv + 0.5).astype(I32) + ADJ_MID
    store(0, 6, (q << 8) | (u & 255))
    high = (u >> 8) << row_shifts(6)
    store(6, 1, high[0:1] + high[1:2] + high[2:3])
    store(7, 1, high[3:4] + high[4:5] + high[5:6])


def unpack_tile(word, x_scale, y_scale):
    x = (word >> 8).astype(F32) * x_scale
    row = lax.broadcasted_iota(I32, (8, LANES), 0)
    first = jnp.broadcast_to(word[6:7], (8, LANES))
    second = jnp.broadcast_to(word[7:8], (8, LANES))
    high = (jnp.where(row < 3, first, second) >> row_shifts(8)) & 1023
    y = (((high << 8) | (word & 255)) - ADJ_MID).astype(F32) * y_scale
    return x, y


def pad_rows(column):
    return jnp.concatenate([jnp.broadcast_to(column, (6, LANES)), jnp.zeros((2, LANES), F32)], axis=0)


def pick(table_of, count, first_high, indices, starts, by_index):
    lows = [i & 127 for i in indices]
    highs = [(i >> 7) - first_high for i in indices]
    found = list(starts)
    steps = [(u, h) for h in range(count) for u in range(len(indices))]
    if by_index:
        steps = [(u, h) for u in range(len(indices)) for h in range(count)]
    for u, h in steps:
        found[u] = jnp.where(highs[u] == h, lane_pick(table_of(h), lows[u]), found[u])
    return found


def send_kernel(here_ref, disp_ref, adj_ref, list_ref, thick_ref, packed_ref, scale_ref, send_ref, *, chunks, domains, iface):
    rows = iface // LANES
    cut = lambda ref, h: ref[pl.ds(h, 6, stride=chunks)]
    x_inv, x_scale = scales_of(lambda h: cut(disp_ref, h), chunks, DISP_TOP)
    y_inv, y_scale = scales_of(lambda h: cut(adj_ref, h), chunks, ADJ_TOP)
    scale_ref[0:8] = pad_rows(x_scale)
    scale_ref[8:16] = pad_rows(y_scale)
    xs = scale_ref[0:8]
    ys = scale_ref[8:16]
    x_inv = jnp.broadcast_to(x_inv, (6, LANES))
    y_inv = jnp.broadcast_to(y_inv, (6, LANES))
    for h in range(chunks):

        def store(row, many, value, h=h):
            packed_ref[h * 8 + row : h * 8 + row + many] = value

        pack_tile(cut(disp_ref, h), cut(adj_ref, h), x_inv, y_inv, store)

    def thickness_rows(k, half):
        return thick_ref[k * 4 + half * 2 : k * 4 + half * 2 + 2]

    @pl.loop(0, domains)
    def _(d):
        for k in range(rows):
            for half in range(2):
                at = k * 16 + half * 8
                send_ref[d, at : at + 6] = jnp.zeros((6, LANES), F32)
                send_ref[d, at + 6 : at + 8] = thickness_rows(k, half)

    here = here_ref[0]
    row_ids = lax.broadcasted_iota(I32, (8, LANES), 0)
    turns = len(OFFSETS) * rows // 2

    def target_of(turn):
        j = turn // (rows // 2)
        offset = j - NBR + jnp.where(j >= NBR, 1, 0)
        return lax.rem(here - offset + domains, domains)

    def fetch(turn):
        target = target_of(turn)
        base = pl.multiple_of(target // 8 * 8, 8)
        found = []
        for u in range(2):
            k = lax.rem(turn, rows // 2) * 2 + u
            tile = list_ref[0, pl.ds(base, 8), pl.ds(pl.multiple_of(k * LANES, LANES), LANES)]
            row = jnp.sum(jnp.where(row_ids == target - base, tile, 0), axis=0, keepdims=True)
            found.append(jnp.broadcast_to(row, (8, LANES)))
        return tuple(found)

    def body(turn, indices):
        target = target_of(turn)
        picked = pick(
            lambda h: packed_ref[h * 8 : h * 8 + 8], chunks, 0, indices, [jnp.zeros((8, LANES), I32)] * 2, False
        )
        for u in range(2):
            k = lax.rem(turn, rows // 2) * 2 + u
            for half, value in enumerate(unpack_tile(picked[u], xs, ys)):
                at = pl.ds(pl.multiple_of(k * 16 + half * 8, 8), 8)
                send_ref[target, at] = jnp.where(row_ids < 6, value, send_ref[target, at])
        return fetch(jnp.minimum(turn + 1, turns - 1))

    lax.fori_loop(0, turns, body, fetch(jnp.int32(0)))


def own_kernel(
    packed_ref, disp_ref, adj_ref, connect_ref, got_ref, near_x_ref, near_y_ref, wide_ref, table_ref, *, chunks, groups, highs
):
    for high in range(highs):
        for half in range(2):
            lanes = slice(half * LANES, half * LANES + LANES)
            x = disp_ref[pl.ds(high * 2 + half, 6, stride=chunks)]
            y = adj_ref[pl.ds(high * 2 + half, 6, stride=chunks)]
            xh = x.astype(BF16).astype(F32)
            yh = y.astype(BF16).astype(F32)
            xl = x - xh
            yl = y - yh
            pieces = (xh, yh[0:2], yl[4:6], yh[2:6], yl[2:4], xl, yl[0:2])
            at = high * ROWS
            for piece in pieces:
                wide_ref[at : at + piece.shape[0], lanes] = piece
                at += piece.shape[0]
    table_ref[...] = wide_ref[...].astype(BF16)
    row_ids = lax.broadcasted_iota(I32, (8, LANES), 0)
    names = lax.broadcasted_iota(I32, (256, LANES), 0).astype(F32).astype(BF16)
    one = jnp.ones((256, LANES), BF16)
    none = jnp.zeros((256, LANES), BF16)

    def one_hot(index):
        tile = jnp.broadcast_to((index[0:1] & 255).astype(F32), (16, LANES)).astype(BF16)
        return jnp.where(names == jnp.concatenate([tile] * 16, axis=0), one, none)

    def fetch(b):
        rows = connect_ref[:, pl.ds(pl.multiple_of(b * LANES, LANES), LANES)]
        return tuple(jnp.broadcast_to(rows[a : a + 1], (8, LANES)) for a in range(4))

    def body(b, indices):
        hot = jnp.concatenate([one_hot(i) for i in indices], axis=1)
        every = jnp.dot(table_ref[...], hot, preferred_element_type=F32)
        for a in range(4):
            held = [jnp.zeros((8, LANES), F32)] * 3
            for high in range(highs):
                hit = (indices[a] >> 8) == high
                for v in range(3):
                    at = high * ROWS + v * 8
                    held[v] = jnp.where(hit, every[at : at + 8, a * LANES : (a + 1) * LANES], held[v])
            first = held[0] + held[2]
            second = held[1] + jnp.roll(held[1], 4, axis=0)
            at = pl.ds(pl.multiple_of(b * 32 + a * 8, 8), 8)
            near_x_ref[at] = first
            near_y_ref[at] = jnp.where(row_ids < 2, jnp.roll(first, 2, axis=0), second)
        found = pick(
            lambda h: packed_ref[(2 * highs + h) * 8 : (2 * highs + h) * 8 + 8],
            chunks - 2 * highs,
            2 * highs,
            indices,
            [jnp.zeros((8, LANES), I32)] * 4,
            True,
        )
        for a in range(4):
            got_ref[pl.ds(pl.multiple_of(b * 32 + a * 8, 8), 8)] = found[a]
        return fetch(jnp.minimum(b + 1, groups - 1))

    lax.fori_loop(0, groups, body, fetch(jnp.int32(0)))


def spread_matrix(flip):
    shape = (24, 32) if not flip else (32, 24)
    narrow = lax.broadcasted_iota(I32, shape, 1 if flip else 0)
    wide = lax.broadcasted_iota(I32, shape, 0 if flip else 1)
    hit = (narrow // 4 == wide % 8) & (narrow % 4 == wide // 8)
    return jnp.where(hit, 1.0, 0.0).astype(F32)


def three_parts(x):
    parts = []
    for _ in range(3):
        part = x.astype(BF16)
        parts.append(part)
        x = x - part.astype(F32)
    return parts


def dot(a, b):
    return jnp.dot(a, b, precision=lax.Precision.HIGHEST, preferred_element_type=F32)


def main_kernel(
    here_ref,
    recv_ref,
    packed_scale_ref,
    got_ref,
    near_x_ref,
    near_y_ref,
    connect_ref,
    comp_ref,
    dv_ref,
    s_memb_ref,
    s_bend_ref,
    k_memb_ref,
    k_bend_ref,
    stats_ref,
    slope_ref,
    fixed_ref,
    ghost_ref,
    move_ref,
    cost_ref,
    panel_ref,
    fail_ref,
    best_ref,
    *,
    own,
    groups,
    domains,
    iface,
    comps,
    highs,
):
    rows = iface // LANES
    ghosts = len(OFFSETS) * rows
    here = here_ref[0]
    sources = [lax.rem(here + offset + domains, domains) for offset in OFFSETS]

    def x_of(h):
        return recv_ref[sources[h // rows], (h % rows) * 16 : (h % rows) * 16 + 6]

    def y_of(h):
        return recv_ref[sources[h // rows], (h % rows) * 16 + 8 : (h % rows) * 16 + 14]

    x_inv, x_scale = scales_of(x_of, ghosts, DISP_TOP)
    y_inv, y_scale = scales_of(y_of, ghosts, ADJ_TOP)
    gx = pad_rows(x_scale)
    gy = pad_rows(y_scale)
    x_inv = jnp.broadcast_to(x_inv, (6, LANES))
    y_inv = jnp.broadcast_to(y_inv, (6, LANES))
    for h in range(ghosts):

        def store(row, many, value, h=h):
            ghost_ref[h * 8 + row : h * 8 + row + many] = value

        pack_tile(x_of(h), y_of(h), x_inv, y_inv, store)
    ox = packed_scale_ref[0:8]
    oy = packed_scale_ref[8:16]
    tiles = groups // 8
    panel_ref[...] = jnp.zeros(panel_ref.shape, F32)
    span = 8

    @pl.loop(0, tiles // 2 * (domains // span))
    def _(turn):
        first = turn // (tiles // 2) * span
        block = lax.rem(turn, tiles // 2) * 16
        at = [pl.ds(pl.multiple_of(block + u * 8, 8), 8) for u in range(2)]

        def row_of(h):
            k = h % 16
            row = (k // 4) * 16 + (k % 4 // 2) * 8 + 6 + k % 2
            return jnp.broadcast_to(recv_ref[first + h // 16, row : row + 1], (8, LANES))

        found = pick(
            row_of, span * 16, first * 16, [dv_ref[at[u]] for u in range(2)], [panel_ref[at[u]] for u in range(2)], False
        )
        for u in range(2):
            panel_ref[at[u]] = found[u]

    wide = spread_matrix(False)
    tall = spread_matrix(True)
    weights = jnp.concatenate(
        [
            dot(s_memb_ref[...], wide),
            dot(s_bend_ref[...], wide),
            dot(tall, dot(k_memb_ref[...], wide)),
            dot(tall, dot(k_bend_ref[...], wide)),
        ],
        axis=0,
    )
    w = three_parts(weights)
    stacked_weights = jnp.concatenate([w[0], w[0], w[1], w[0], w[1], w[2]], axis=1)
    names = lax.broadcasted_iota(I32, (8, LANES), 0)
    combs = comps // 8
    best_ref[...] = jnp.full(best_ref.shape, LOW, F32)

    def gather(b):
        lanes = pl.ds(pl.multiple_of(b * LANES, LANES), LANES)
        rows = connect_ref[:, lanes]
        indices = [jnp.broadcast_to(rows[a : a + 1], (8, LANES)) for a in range(4)]
        found = pick(
            lambda h: ghost_ref[h * 8 : h * 8 + 8],
            ghosts,
            own,
            indices,
            [got_ref[pl.ds(pl.multiple_of(b * 32 + a * 8, 8), 8)] for a in range(4)],
            True,
        )
        for a in range(4):
            far = indices[a] >= own * LANES
            x, y = unpack_tile(found[a], jnp.where(far, gx, ox), jnp.where(far, gy, oy))
            near = indices[a] < highs * 256
            at = pl.ds(pl.multiple_of(b * 32 + a * 8, 8), 8)
            move_ref[a * 8 : a * 8 + 8] = jnp.where(near, near_x_ref[at], x)
            cost_ref[a * 8 : a * 8 + 8] = jnp.where(near, near_y_ref[at], y)

    def dense(b):
        x = three_parts(move_ref[...])
        part = jnp.dot(
            stacked_weights,
            jnp.concatenate([x[0], x[1], x[0], x[2], x[1], x[0]], axis=0),
            preferred_element_type=F32,
        )
        row = pl.ds(b, 1)
        panel = panel_ref[row]
        bending = part[8:16]
        stress = part[0:8] + panel * bending
        failure = jnp.sum(stress * stress, axis=0, keepdims=True) / 8.0
        slope_ref[row] = jnp.sum(stress * bending, axis=0, keepdims=True) * (2.0 / 8.0)
        stiff = part[16:48] + (3.0 * panel * panel) * part[48:80]
        fixed_ref[row] = jnp.sum(cost_ref[...] * stiff, axis=0, keepdims=True)
        fail_ref[row] = failure
        away = comp_ref[row] - names
        for c in range(combs):
            held = best_ref[c * 8 : c * 8 + 8]
            best_ref[c * 8 : c * 8 + 8] = jnp.maximum(held, jnp.where(away == c * 8, failure, LOW))

    gather(0)

    @pl.loop(1, groups)
    def _(b):
        dense(b - 1)
        gather(b)

    dense(groups - 1)

    stats_ref[0] = jnp.zeros((8, LANES), F32)
    bands = (comps + LANES - 1) // LANES
    diagonal = lax.broadcasted_iota(I32, (LANES, LANES), 0) == lax.broadcasted_iota(I32, (LANES, LANES), 1)

    def to_rows(reduce, start):
        for band in range(bands):
            many = min(LANES, comps - band * LANES)
            column = reduce(best_ref[band * LANES : band * LANES + many], axis=1, keepdims=True)
            row = jnp.sum(jnp.where(diagonal[0:many], column, 0.0), axis=0, keepdims=True)
            stats_ref[0, start + band : start + band + 1] = row

    to_rows(jnp.max, 0)
    for t in range(tiles):
        block = slice(t * 8, t * 8 + 8)
        comp = comp_ref[block]
        low = comp & 127
        high = comp >> 7
        top = jnp.zeros((8, LANES), F32)
        for band in range(bands):
            tile = jnp.broadcast_to(stats_ref[0, band : band + 1], (8, LANES))
            top = jnp.where(high == band, lane_pick(tile, low), top)
        scaled = jnp.exp(SHARP * (fail_ref[block] - top))
        fail_ref[block] = scaled
        slope_ref[block] = slope_ref[block] * scaled

    part_of = combs // 2
    for half in range(2):

        def total_step(step, totals, half=half):
            totals = list(totals)
            for g in range(2):
                row = pl.ds(step * 2 + g, 1)
                away = comp_ref[row] - names
                value = fail_ref[row]
                for c in range(part_of):
                    totals[c] = totals[c] + jnp.where(away == (half * part_of + c) * 8, value, 0.0)
            return tuple(totals)

        totals = lax.fori_loop(0, groups // 2, total_step, (jnp.zeros((8, LANES), F32),) * part_of)
        for c in range(part_of):
            at = (half * part_of + c) * 8
            best_ref[at : at + 8] = totals[c]
    to_rows(jnp.sum, 4)
    mine = stats_ref[0]
    for d in range(1, domains):
        stats_ref[d] = mine


def last_kernel(
    here_ref, stats_ref, mult_ref, comp_ref, dv_ref, slope_ref, fixed_ref, ks_ref, sum_ref, term_ref, *, domains, comps, groups, slots
):
    here = here_ref[0]
    peak = stats_ref[0, 0:4]
    for s in range(1, domains):
        peak = jnp.maximum(peak, stats_ref[s, 0:4])
    total = jnp.zeros_like(peak)
    for s in range(domains):
        total = total + stats_ref[s, 4:8] * jnp.exp(SHARP * (stats_ref[s, 0:4] - peak))
    ks = peak + jnp.log(total) / SHARP
    share = jnp.exp(SHARP * (stats_ref[here, 0:4] - peak)) / total
    bands = (comps + LANES - 1) // LANES
    weights = []
    for band in range(bands):
        many = min(LANES, comps - band * LANES)
        span = slice(band * LANES, band * LANES + many)
        ks_ref[0:1, span] = ks[band : band + 1, 0:many]
        mult = mult_ref[0:1, span]
        if many < LANES:
            mult = jnp.concatenate([mult, jnp.zeros((1, LANES - many), F32)], axis=1)
        weights.append(jnp.broadcast_to(share[band : band + 1] * mult, (8, LANES)))
    tiles = groups // 8
    for t in range(tiles):
        block = slice(t * 8, t * 8 + 8)
        comp = comp_ref[block]
        low = comp & 127
        high = comp >> 7
        weight = jnp.zeros((8, LANES), F32)
        for band in range(bands):
            weight = jnp.where(high == band, lane_pick(weights[band], low), weight)
        term_ref[block] = weight * slope_ref[block] + fixed_ref[block]
    sum_ref[...] = jnp.zeros(sum_ref.shape, F32)
    outer = slots // 256
    outer_ids = lax.broadcasted_iota(I32, (outer, LANES), 0).astype(F32).astype(BF16)
    inner_ids = lax.broadcasted_iota(I32, (256, LANES), 0).astype(F32).astype(BF16)

    def tall(row, many):
        tile = jnp.broadcast_to(row.astype(F32), (16, LANES)).astype(BF16)
        return jnp.concatenate([tile] * (many // 16), axis=0)

    @pl.loop(0, tiles)
    def _(t):
        highs = []
        lows = []
        for j in range(8):
            place = dv_ref[pl.ds(t * 8 + j, 1)]
            value = term_ref[pl.ds(t * 8 + j, 1)]
            rough = value.astype(BF16).astype(F32)
            one = jnp.ones((outer, LANES), BF16)
            highs.append(jnp.where(outer_ids == tall(place >> 8, outer), one, jnp.zeros_like(one)))
            hit = inner_ids == tall(place & 255, 256)
            none = jnp.zeros((256, LANES), BF16)
            lows.append(
                jnp.concatenate(
                    [jnp.where(hit, tall(rough, 256), none), jnp.where(hit, tall(value - rough, 256), none)], axis=0
                )
            )
        both = lax.dot_general(
            jnp.concatenate(highs, axis=1),
            jnp.concatenate(lows, axis=1),
            (((1,), (1,)), ((), ())),
            preferred_element_type=F32,
        )
        sum_ref[...] += both[:, 0:256] + both[:, 256:512]


def vmem():
    return pl.BlockSpec(memory_space=pltpu.VMEM)


def smem():
    return pl.BlockSpec(memory_space=pltpu.SMEM)


def per_device(
    displacement, adjoint, send_list, connect, elem_comp, elem_dv, thickness, multiplier, k_memb, k_bend, s_memb, s_bend
):
    domains = lax.axis_size("dom")
    here = lax.axis_index("dom").astype(I32).reshape(1)
    comps = multiplier.shape[1]
    nodes = displacement.shape[2]
    elems = connect.shape[1]
    iface = send_list.shape[2]
    own = nodes // LANES
    groups = elems // LANES
    slots = thickness.shape[0] * domains
    block = 4 * iface // LANES * 4
    sds = jax.ShapeDtypeStruct

    disp = displacement.reshape(-1, LANES)
    adj = adjoint.reshape(-1, LANES)
    highs = min(HIGHS, own // 2)

    packed, scale, send = pl.pallas_call(
        functools.partial(send_kernel, chunks=own, domains=domains, iface=iface),
        out_shape=(sds((own * 8, LANES), I32), sds((16, LANES), F32), sds((domains, block, LANES), F32)),
        in_specs=[smem()] + [vmem()] * 4,
        out_specs=(vmem(),) * 3,
        name="send_pick",
    )(here, disp, adj, send_list, thickness.reshape(-1, LANES))
    recv = lax.all_to_all(send, "dom", 0, 0, tiled=True)
    got, near_x, near_y = pl.pallas_call(
        functools.partial(own_kernel, chunks=own, groups=groups, highs=highs),
        out_shape=(sds((groups * 32, LANES), I32),) + (sds((groups * 32, LANES), F32),) * 2,
        in_specs=[vmem()] * 4,
        out_specs=(vmem(),) * 3,
        scratch_shapes=[pltpu.VMEM((highs * ROWS, 256), F32), pltpu.VMEM((highs * ROWS, 256), BF16)],
        name="own_pick",
        cost_estimate=pl.CostEstimate(flops=0, transcendentals=0, bytes_accessed=60_000_000),
    )(packed, disp, adj, connect)
    comp = elem_comp.reshape(-1, LANES)
    dv = elem_dv.reshape(-1, LANES)
    stats, slope, fixed = pl.pallas_call(
        functools.partial(main_kernel, own=own, groups=groups, domains=domains, iface=iface, comps=comps, highs=highs),
        out_shape=(sds((domains, 8, LANES), F32), sds((groups, LANES), F32), sds((groups, LANES), F32)),
        in_specs=[smem()] + [vmem()] * 12,
        out_specs=(vmem(),) * 3,
        scratch_shapes=[
            pltpu.VMEM((len(OFFSETS) * iface // LANES * 8, LANES), I32),
            pltpu.VMEM((32, LANES), F32),
            pltpu.VMEM((32, LANES), F32),
            pltpu.VMEM((groups, LANES), F32),
            pltpu.VMEM((groups, LANES), F32),
            pltpu.VMEM((comps, LANES), F32),
        ],
        name="element_work",
    )(here, recv, scale, got, near_x, near_y, connect, comp, dv, s_memb, s_bend, k_memb, k_bend)
    everyone = lax.all_to_all(stats, "dom", 0, 0, tiled=True)
    ks_value, sums = pl.pallas_call(
        functools.partial(last_kernel, domains=domains, comps=comps, groups=groups, slots=slots),
        out_shape=(sds((1, comps), F32), sds((slots // 256, 256), F32)),
        in_specs=[smem()] + [vmem()] * 6,
        out_specs=(vmem(),) * 2,
        scratch_shapes=[pltpu.VMEM((groups, LANES), F32)],
        name="weigh_and_sum",
    )(here, everyone, multiplier, comp, dv, slope, fixed)
    arrived = lax.all_to_all(sums.reshape(domains, -1, 256), "dom", 0, 0, tiled=True)
    owned = arrived.sum(axis=0)
    sensitivity = from_everyone(owned, "load").sum(axis=0).reshape(-1)
    return ks_value, sensitivity


def solution(mesh):
    in_specs = (
        P("load", None, "dom"),
        P("load", None, "dom"),
        P("dom", None, None),
        P(None, "dom"),
        P("dom"),
        P("dom"),
        P("dom"),
        P("load", None),
        P(),
        P(),
        P(),
        P(),
    )
    return jax.shard_map(
        per_device, mesh=mesh, in_specs=in_specs, out_specs=(P("load", None), P("dom")), check_vma=False
    )
```

```python
import functools

import jax
import jax.numpy as jnp
from jax import lax
from jax.experimental import pallas as pl
from jax.experimental.pallas import tpu as pltpu
from jax.sharding import PartitionSpec as P

NBR = 3
ROWS = 24
HIGHS = 14
SLICE = 1024
CAP = 64
SHARP = 50.0
LOW = -1e30
LANES = 128
DISP_TOP = 8388600.0
ADJ_TOP = 131000.0
ADJ_MID = 131072
OFFSETS = tuple(j - NBR if j < NBR else j - NBR + 1 for j in range(2 * NBR))
I32 = jnp.int32
F32 = jnp.float32
BF16 = jnp.bfloat16


def lane_pick(table, index):
    return jnp.take_along_axis(table, index, axis=1, mode="promise_in_bounds")


def row_shifts(rows):
    row = lax.broadcasted_iota(I32, (rows, LANES), 0)
    return (row % 3) * 10


def scales_of(x_of, count, top):
    best = jnp.abs(x_of(0))
    for h in range(1, count):
        best = jnp.maximum(best, jnp.abs(x_of(h)))
    most = jnp.maximum(jnp.max(best, axis=1, keepdims=True), 1e-30)
    return top / most, most / top


def pack_tile(x, y, x_inv, y_inv, store):
    q = jnp.floor(x * x_inv + 0.5).astype(I32)
    u = jnp.floor(y * y_inv + 0.5).astype(I32) + ADJ_MID
    store(0, 6, (q << 8) | (u & 255))
    high = (u >> 8) << row_shifts(6)
    store(6, 1, high[0:1] + high[1:2] + high[2:3])
    store(7, 1, high[3:4] + high[4:5] + high[5:6])


def unpack_tile(word, x_scale, y_scale):
    x = (word >> 8).astype(F32) * x_scale
    row = lax.broadcasted_iota(I32, (8, LANES), 0)
    first = jnp.broadcast_to(word[6:7], (8, LANES))
    second = jnp.broadcast_to(word[7:8], (8, LANES))
    high = (jnp.where(row < 3, first, second) >> row_shifts(8)) & 1023
    y = (((high << 8) | (word & 255)) - ADJ_MID).astype(F32) * y_scale
    return x, y


def pad_rows(column):
    return jnp.concatenate([jnp.broadcast_to(column, (6, LANES)), jnp.zeros((2, LANES), F32)], axis=0)


def pick(table_of, count, first_high, indices, starts, by_index):
    lows = [i & 127 for i in indices]
    highs = [(i >> 7) - first_high for i in indices]
    found = list(starts)
    steps = [(u, h) for h in range(count) for u in range(len(indices))]
    if by_index:
        steps = [(u, h) for u in range(len(indices)) for h in range(count)]
    for u, h in steps:
        found[u] = jnp.where(highs[u] == h, lane_pick(table_of(h), lows[u]), found[u])
    return found


def send_kernel(here_ref, disp_ref, adj_ref, list_ref, thick_ref, packed_ref, scale_ref, send_ref, *, chunks, domains, iface):
    rows = iface // LANES
    cut = lambda ref, h: ref[pl.ds(h, 6, stride=chunks)]
    x_inv, x_scale = scales_of(lambda h: cut(disp_ref, h), chunks, DISP_TOP)
    y_inv, y_scale = scales_of(lambda h: cut(adj_ref, h), chunks, ADJ_TOP)
    scale_ref[0:8] = pad_rows(x_scale)
    scale_ref[8:16] = pad_rows(y_scale)
    xs = scale_ref[0:8]
    ys = scale_ref[8:16]
    x_inv = jnp.broadcast_to(x_inv, (6, LANES))
    y_inv = jnp.broadcast_to(y_inv, (6, LANES))
    for h in range(chunks):

        def store(row, many, value, h=h):
            packed_ref[h * 8 + row : h * 8 + row + many] = value

        pack_tile(cut(disp_ref, h), cut(adj_ref, h), x_inv, y_inv, store)

    def thickness_rows(k, half):
        return thick_ref[k * 4 + half * 2 : k * 4 + half * 2 + 2]

    @pl.loop(0, domains)
    def _(d):
        for k in range(rows):
            for half in range(2):
                at = k * 16 + half * 8
                send_ref[d, at : at + 6] = jnp.zeros((6, LANES), F32)
                send_ref[d, at + 6 : at + 8] = thickness_rows(k, half)

    here = here_ref[0]
    row_ids = lax.broadcasted_iota(I32, (8, LANES), 0)
    turns = len(OFFSETS) * rows // 2

    def target_of(turn):
        j = turn // (rows // 2)
        offset = j - NBR + jnp.where(j >= NBR, 1, 0)
        return lax.rem(here - offset + domains, domains)

    def fetch(turn):
        target = target_of(turn)
        base = pl.multiple_of(target // 8 * 8, 8)
        found = []
        for u in range(2):
            k = lax.rem(turn, rows // 2) * 2 + u
            tile = list_ref[0, pl.ds(base, 8), pl.ds(pl.multiple_of(k * LANES, LANES), LANES)]
            row = jnp.sum(jnp.where(row_ids == target - base, tile, 0), axis=0, keepdims=True)
            found.append(jnp.broadcast_to(row, (8, LANES)))
        return tuple(found)

    def body(turn, indices):
        target = target_of(turn)
        picked = pick(
            lambda h: packed_ref[h * 8 : h * 8 + 8], chunks, 0, indices, [jnp.zeros((8, LANES), I32)] * 2, False
        )
        for u in range(2):
            k = lax.rem(turn, rows // 2) * 2 + u
            for half, value in enumerate(unpack_tile(picked[u], xs, ys)):
                at = pl.ds(pl.multiple_of(k * 16 + half * 8, 8), 8)
                send_ref[target, at] = jnp.where(row_ids < 6, value, send_ref[target, at])
        return fetch(jnp.minimum(turn + 1, turns - 1))

    lax.fori_loop(0, turns, body, fetch(jnp.int32(0)))


def own_kernel(
    packed_ref, disp_ref, adj_ref, connect_ref, got_ref, near_x_ref, near_y_ref, wide_ref, table_ref, *, chunks, groups, highs
):
    for high in range(highs):
        for half in range(2):
            lanes = slice(half * LANES, half * LANES + LANES)
            x = disp_ref[pl.ds(high * 2 + half, 6, stride=chunks)]
            y = adj_ref[pl.ds(high * 2 + half, 6, stride=chunks)]
            xh = x.astype(BF16).astype(F32)
            yh = y.astype(BF16).astype(F32)
            xl = x - xh
            yl = y - yh
            pieces = (xh, yh[0:2], yl[4:6], yh[2:6], yl[2:4], xl, yl[0:2])
            at = high * ROWS
            for piece in pieces:
                wide_ref[at : at + piece.shape[0], lanes] = piece
                at += piece.shape[0]
    table_ref[...] = wide_ref[...].astype(BF16)
    row_ids = lax.broadcasted_iota(I32, (8, LANES), 0)
    names = lax.broadcasted_iota(I32, (256, LANES), 0).astype(F32).astype(BF16)
    one = jnp.ones((256, LANES), BF16)
    none = jnp.zeros((256, LANES), BF16)

    def one_hot(index):
        tile = jnp.broadcast_to((index[0:1] & 255).astype(F32), (16, LANES)).astype(BF16)
        return jnp.where(names == jnp.concatenate([tile] * 16, axis=0), one, none)

    def fetch(b):
        rows = connect_ref[:, pl.ds(pl.multiple_of(b * LANES, LANES), LANES)]
        return tuple(jnp.broadcast_to(rows[a : a + 1], (8, LANES)) for a in range(4))

    def body(b, indices):
        hot = jnp.concatenate([one_hot(i) for i in indices], axis=1)
        every = jnp.dot(table_ref[...], hot, preferred_element_type=F32)
        for a in range(4):
            held = [jnp.zeros((8, LANES), F32)] * 3
            for high in range(highs):
                hit = (indices[a] >> 8) == high
                for v in range(3):
                    at = high * ROWS + v * 8
                    held[v] = jnp.where(hit, every[at : at + 8, a * LANES : (a + 1) * LANES], held[v])
            first = held[0] + held[2]
            second = held[1] + jnp.roll(held[1], 4, axis=0)
            at = pl.ds(pl.multiple_of(b * 32 + a * 8, 8), 8)
            near_x_ref[at] = first
            near_y_ref[at] = jnp.where(row_ids < 2, jnp.roll(first, 2, axis=0), second)
        found = pick(
            lambda h: packed_ref[(2 * highs + h) * 8 : (2 * highs + h) * 8 + 8],
            chunks - 2 * highs,
            2 * highs,
            indices,
            [jnp.zeros((8, LANES), I32)] * 4,
            True,
        )
        for a in range(4):
            got_ref[pl.ds(pl.multiple_of(b * 32 + a * 8, 8), 8)] = found[a]
        return fetch(jnp.minimum(b + 1, groups - 1))

    lax.fori_loop(0, groups, body, fetch(jnp.int32(0)))


def spread_matrix(flip):
    shape = (24, 32) if not flip else (32, 24)
    narrow = lax.broadcasted_iota(I32, shape, 1 if flip else 0)
    wide = lax.broadcasted_iota(I32, shape, 0 if flip else 1)
    hit = (narrow // 4 == wide % 8) & (narrow % 4 == wide // 8)
    return jnp.where(hit, 1.0, 0.0).astype(F32)


def three_parts(x):
    parts = []
    for _ in range(3):
        part = x.astype(BF16)
        parts.append(part)
        x = x - part.astype(F32)
    return parts


def dot(a, b):
    return jnp.dot(a, b, precision=lax.Precision.HIGHEST, preferred_element_type=F32)


def main_kernel(
    here_ref,
    recv_ref,
    packed_scale_ref,
    got_ref,
    near_x_ref,
    near_y_ref,
    connect_ref,
    comp_ref,
    dv_ref,
    s_memb_ref,
    s_bend_ref,
    k_memb_ref,
    k_bend_ref,
    out_ref,
    ghost_ref,
    move_ref,
    cost_ref,
    panel_ref,
    fail_ref,
    best_ref,
    slope_ref,
    fixed_ref,
    stats_ref,
    *,
    own,
    groups,
    domains,
    iface,
    comps,
    highs,
    owned,
    slots,
    cap,
):
    rows = iface // LANES
    ghosts = len(OFFSETS) * rows
    here = here_ref[0]
    sources = [lax.rem(here + offset + domains, domains) for offset in OFFSETS]

    def x_of(h):
        return recv_ref[sources[h // rows], (h % rows) * 16 : (h % rows) * 16 + 6]

    def y_of(h):
        return recv_ref[sources[h // rows], (h % rows) * 16 + 8 : (h % rows) * 16 + 14]

    x_inv, x_scale = scales_of(x_of, ghosts, DISP_TOP)
    y_inv, y_scale = scales_of(y_of, ghosts, ADJ_TOP)
    gx = pad_rows(x_scale)
    gy = pad_rows(y_scale)
    x_inv = jnp.broadcast_to(x_inv, (6, LANES))
    y_inv = jnp.broadcast_to(y_inv, (6, LANES))
    for h in range(ghosts):

        def store(row, many, value, h=h):
            ghost_ref[h * 8 + row : h * 8 + row + many] = value

        pack_tile(x_of(h), y_of(h), x_inv, y_inv, store)
    ox = packed_scale_ref[0:8]
    oy = packed_scale_ref[8:16]
    tiles = groups // 8
    panel_ref[...] = jnp.zeros(panel_ref.shape, F32)
    span = 8

    @pl.loop(0, tiles // 2 * (domains // span))
    def _(turn):
        first = turn // (tiles // 2) * span
        block = lax.rem(turn, tiles // 2) * 16
        at = [pl.ds(pl.multiple_of(block + u * 8, 8), 8) for u in range(2)]

        def row_of(h):
            k = h % 16
            row = (k // 4) * 16 + (k % 4 // 2) * 8 + 6 + k % 2
            return jnp.broadcast_to(recv_ref[first + h // 16, row : row + 1], (8, LANES))

        found = pick(
            row_of, span * 16, first * 16, [dv_ref[at[u]] for u in range(2)], [panel_ref[at[u]] for u in range(2)], False
        )
        for u in range(2):
            panel_ref[at[u]] = found[u]

    wide = spread_matrix(False)
    tall = spread_matrix(True)
    weights = jnp.concatenate(
        [
            dot(s_memb_ref[...], wide),
            dot(s_bend_ref[...], wide),
            dot(tall, dot(k_memb_ref[...], wide)),
            dot(tall, dot(k_bend_ref[...], wide)),
        ],
        axis=0,
    )
    w = three_parts(weights)
    stacked_weights = jnp.concatenate([w[0], w[0], w[1], w[0], w[1], w[2]], axis=1)
    names = lax.broadcasted_iota(I32, (8, LANES), 0)
    combs = comps // 8
    best_ref[...] = jnp.full(best_ref.shape, LOW, F32)

    def gather(b):
        lanes = pl.ds(pl.multiple_of(b * LANES, LANES), LANES)
        rows = connect_ref[:, lanes]
        indices = [jnp.broadcast_to(rows[a : a + 1], (8, LANES)) for a in range(4)]
        found = pick(
            lambda h: ghost_ref[h * 8 : h * 8 + 8],
            ghosts,
            own,
            indices,
            [got_ref[pl.ds(pl.multiple_of(b * 32 + a * 8, 8), 8)] for a in range(4)],
            True,
        )
        for a in range(4):
            far = indices[a] >= own * LANES
            x, y = unpack_tile(found[a], jnp.where(far, gx, ox), jnp.where(far, gy, oy))
            near = indices[a] < highs * 256
            at = pl.ds(pl.multiple_of(b * 32 + a * 8, 8), 8)
            move_ref[a * 8 : a * 8 + 8] = jnp.where(near, near_x_ref[at], x)
            cost_ref[a * 8 : a * 8 + 8] = jnp.where(near, near_y_ref[at], y)

    def dense(b):
        x = three_parts(move_ref[...])
        part = jnp.dot(
            stacked_weights,
            jnp.concatenate([x[0], x[1], x[0], x[2], x[1], x[0]], axis=0),
            preferred_element_type=F32,
        )
        row = pl.ds(b, 1)
        panel = panel_ref[row]
        bending = part[8:16]
        stress = part[0:8] + panel * bending
        failure = jnp.sum(stress * stress, axis=0, keepdims=True) / 8.0
        slope_ref[row] = jnp.sum(stress * bending, axis=0, keepdims=True) * (2.0 / 8.0)
        stiff = part[16:48] + (3.0 * panel * panel) * part[48:80]
        fixed_ref[row] = jnp.sum(cost_ref[...] * stiff, axis=0, keepdims=True)
        fail_ref[row] = failure
        away = comp_ref[row] - names
        for c in range(combs):
            held = best_ref[c * 8 : c * 8 + 8]
            best_ref[c * 8 : c * 8 + 8] = jnp.maximum(held, jnp.where(away == c * 8, failure, LOW))

    gather(0)

    @pl.loop(1, groups)
    def _(b):
        dense(b - 1)
        gather(b)

    dense(groups - 1)

    stats_ref[0] = jnp.zeros((8, LANES), F32)
    bands = (comps + LANES - 1) // LANES
    diagonal = lax.broadcasted_iota(I32, (LANES, LANES), 0) == lax.broadcasted_iota(I32, (LANES, LANES), 1)

    def to_rows(reduce, start):
        for band in range(bands):
            many = min(LANES, comps - band * LANES)
            column = reduce(best_ref[band * LANES : band * LANES + many], axis=1, keepdims=True)
            row = jnp.sum(jnp.where(diagonal[0:many], column, 0.0), axis=0, keepdims=True)
            stats_ref[0, start + band : start + band + 1] = row

    to_rows(jnp.max, 0)
    for t in range(tiles):
        block = slice(t * 8, t * 8 + 8)
        comp = comp_ref[block]
        low = comp & 127
        high = comp >> 7
        top = jnp.zeros((8, LANES), F32)
        for band in range(bands):
            tile = jnp.broadcast_to(stats_ref[0, band : band + 1], (8, LANES))
            top = jnp.where(high == band, lane_pick(tile, low), top)
        scaled = jnp.exp(SHARP * (fail_ref[block] - top))
        fail_ref[block] = scaled
        slope_ref[block] = slope_ref[block] * scaled

    part_of = combs // 2
    for half in range(2):

        def total_step(step, totals, half=half):
            totals = list(totals)
            for g in range(2):
                row = pl.ds(step * 2 + g, 1)
                away = comp_ref[row] - names
                value = fail_ref[row]
                for c in range(part_of):
                    totals[c] = totals[c] + jnp.where(away == (half * part_of + c) * 8, value, 0.0)
            return tuple(totals)

        totals = lax.fori_loop(0, groups // 2, total_step, (jnp.zeros((8, LANES), F32),) * part_of)
        for c in range(part_of):
            at = (half * part_of + c) * 8
            best_ref[at : at + 8] = totals[c]
    to_rows(jnp.sum, 4)

    shift = owned.bit_length() - 1
    owner_ids = lax.broadcasted_iota(I32, (domains, LANES), 0)
    owner_names = owner_ids.astype(F32).astype(BF16)
    rank_names = lax.broadcasted_iota(I32, (cap, LANES), 0).astype(F32).astype(BF16)
    one = jnp.ones((cap, LANES), BF16)
    zero = jnp.zeros((cap, LANES), BF16)
    none = jnp.zeros((domains, LANES), BF16)
    before = lax.broadcasted_iota(I32, (LANES, LANES), 0) < lax.broadcasted_iota(I32, (LANES, LANES), 1)
    before = jnp.concatenate(
        [jnp.where(before, 1.0, 0.0).astype(BF16), jnp.ones((LANES, LANES), BF16)], axis=1
    )
    block_rows = slots // LANES

    @pl.loop(0, groups // (2 * block_rows))
    def _(pair):
        sums = []
        for parity in range(2):
            at = [pair * 2 * block_rows + parity * block_rows + j for j in range(block_rows)]
            places = [dv_ref[pl.ds(r, 1)] for r in at]
            owners = [jnp.where(owner_ids == (place >> shift), 1.0, 0.0) for place in places]
            counts = jnp.dot(
                jnp.concatenate([o.astype(BF16) for o in owners], axis=0), before, preferred_element_type=F32
            )
            base = jnp.zeros((domains, LANES), F32)
            left = []
            right = []
            for j in range(block_rows):
                count = counts[j * domains : (j + 1) * domains]
                rank = jnp.sum(owners[j] * (count[:, 0:LANES] + base), axis=0, keepdims=True)
                base = base + count[:, LANES : 2 * LANES]
                right.append(jnp.where(rank_names == tall_row(rank, cap), one, zero))
                hit = owner_names == tall_row((places[j] >> shift).astype(F32), domains)
                row = pl.ds(at[j], 1)
                values = (
                    fixed_ref[row],
                    slope_ref[row],
                    (places[j] & (owned - 1)).astype(F32),
                    comp_ref[row].astype(F32),
                )
                pieces = []
                for value in values:
                    rough = value.astype(BF16).astype(F32)
                    pieces.append(jnp.where(hit, tall_row(rough, domains), none))
                    pieces.append(jnp.where(hit, tall_row(value - rough, domains), none))
                left.append(jnp.concatenate(pieces, axis=0))
            moved = lax.dot_general(
                jnp.concatenate(left, axis=1),
                jnp.concatenate(right, axis=1),
                (((1,), (1,)), ((), ())),
                preferred_element_type=F32,
            )
            parts = [moved[p * domains : (p + 1) * domains] for p in range(8)]
            sums.append([parts[2 * v] + parts[2 * v + 1] for v in range(4)])
        for v in range(4):
            out_ref[pl.ds(v * 4 + pair, domains, stride=24)] = jnp.concatenate([sums[0][v], sums[1][v]], axis=1)

    mine = stats_ref[0]
    for d in range(domains):
        out_ref[d * 24 + 16 : d * 24 + 24] = mine


def tall_row(row, many):
    tile = jnp.broadcast_to(row, (16, LANES)).astype(BF16)
    return jnp.concatenate([tile] * (many // 16), axis=0)


def last_kernel(recv_ref, mult_ref, ks_ref, sum_ref, fold_ref, *, domains, comps, owned):
    peak = recv_ref[0, 16:20]
    for s in range(1, domains):
        peak = jnp.maximum(peak, recv_ref[s, 16:20])
    total = jnp.zeros_like(peak)
    for s in range(domains):
        total = total + recv_ref[s, 20:24] * jnp.exp(SHARP * (recv_ref[s, 16:20] - peak))
    ks = peak + jnp.log(total) / SHARP
    bands = (comps + LANES - 1) // LANES
    mults = []
    for band in range(bands):
        many = min(LANES, comps - band * LANES)
        span = slice(band * LANES, band * LANES + many)
        ks_ref[0:1, span] = ks[band : band + 1, 0:many]
        mult = mult_ref[0:1, span]
        if many < LANES:
            mult = jnp.concatenate([mult, jnp.zeros((1, LANES - many), F32)], axis=1)
        mults.append(mult)
    factor = jnp.concatenate(mults, axis=0) / total[0:bands]
    half = LANES // 2
    outer = owned // half
    outer_ids = lax.broadcasted_iota(I32, (outer, LANES), 0).astype(F32).astype(BF16)
    inner_ids = lax.broadcasted_iota(I32, (half, LANES), 0).astype(F32).astype(BF16)
    one = jnp.ones((half, LANES), BF16)
    zero = jnp.zeros((half, LANES), BF16)
    none = jnp.zeros((outer, LANES), BF16)

    def part_sum(sources):
        left = []
        right = []
        for s in sources:
            share = jnp.exp(SHARP * (recv_ref[s, 16 : 16 + bands] - peak[0:bands])) * factor
            values = recv_ref[s, 0:8]
            labels = recv_ref[s, 8:16].astype(I32)
            low = labels & 127
            high = labels >> 7
            weight = jnp.zeros((8, LANES), F32)
            for band in range(bands):
                tile = jnp.broadcast_to(share[band : band + 1], (8, LANES))
                weight = jnp.where(high == band, lane_pick(tile, low), weight)
            terms = values + jnp.roll(weight * values, 4, axis=0)
            roughs = terms.astype(BF16).astype(F32)
            fines = terms - roughs
            outers = (labels >> 6).astype(F32)
            inners = (labels & 63).astype(F32)
            for r in range(4):
                row = slice(r, r + 1)
                hit = outer_ids == tall_row(outers[row], outer)
                left.append(
                    jnp.concatenate(
                        [
                            jnp.where(hit, tall_row(roughs[row], outer), none),
                            jnp.where(hit, tall_row(fines[row], outer), none),
                        ],
                        axis=0,
                    )
                )
                right.append(jnp.where(inner_ids == tall_row(inners[row], half), one, zero))
        both = lax.dot_general(
            jnp.concatenate(left, axis=1),
            jnp.concatenate(right, axis=1),
            (((1,), (1,)), ((), ())),
            preferred_element_type=F32,
        )
        return both[0:outer] + both[outer : 2 * outer]

    def step(turn, sums):
        return tuple(sums[m] + part_sum([turn * 4 + m * 2 + j for j in range(2)]) for m in range(2))

    empty = jnp.zeros((outer, half), F32)
    sums = lax.fori_loop(0, domains // 4, step, (empty, empty))
    fold_ref[:, 0:half] = sums[0] + sums[1]
    folded = jnp.concatenate(
        [fold_ref[pl.ds(parity, outer // 2, stride=2)][:, 0:half] for parity in range(2)], axis=1
    )
    for l in range(sum_ref.shape[0]):
        sum_ref[l] = folded


def vmem():
    return pl.BlockSpec(memory_space=pltpu.VMEM)


def smem():
    return pl.BlockSpec(memory_space=pltpu.SMEM)


def per_device(
    displacement, adjoint, send_list, connect, elem_comp, elem_dv, thickness, multiplier, k_memb, k_bend, s_memb, s_bend
):
    domains = lax.axis_size("dom")
    here = lax.axis_index("dom").astype(I32).reshape(1)
    comps = multiplier.shape[1]
    nodes = displacement.shape[2]
    elems = connect.shape[1]
    iface = send_list.shape[2]
    own = nodes // LANES
    groups = elems // LANES
    block = 4 * iface // LANES * 4
    sds = jax.ShapeDtypeStruct

    disp = displacement.reshape(-1, LANES)
    adj = adjoint.reshape(-1, LANES)
    highs = min(HIGHS, own // 2)

    packed, scale, send = pl.pallas_call(
        functools.partial(send_kernel, chunks=own, domains=domains, iface=iface),
        out_shape=(sds((own * 8, LANES), I32), sds((16, LANES), F32), sds((domains, block, LANES), F32)),
        in_specs=[smem()] + [vmem()] * 4,
        out_specs=(vmem(),) * 3,
        name="send_pick",
    )(here, disp, adj, send_list, thickness.reshape(-1, LANES))
    recv = lax.all_to_all(send, "dom", 0, 0, tiled=True)
    got, near_x, near_y = pl.pallas_call(
        functools.partial(own_kernel, chunks=own, groups=groups, highs=highs),
        out_shape=(sds((groups * 32, LANES), I32),) + (sds((groups * 32, LANES), F32),) * 2,
        in_specs=[vmem()] * 4,
        out_specs=(vmem(),) * 3,
        scratch_shapes=[pltpu.VMEM((highs * ROWS, 256), F32), pltpu.VMEM((highs * ROWS, 256), BF16)],
        name="own_pick",
        cost_estimate=pl.CostEstimate(flops=0, transcendentals=0, bytes_accessed=60_000_000),
    )(packed, disp, adj, connect)
    comp = elem_comp.reshape(-1, LANES)
    dv = elem_dv.reshape(-1, LANES)
    owned = thickness.shape[0]
    mine = pl.pallas_call(
        functools.partial(
            main_kernel,
            own=own,
            groups=groups,
            domains=domains,
            iface=iface,
            comps=comps,
            highs=highs,
            owned=owned,
            slots=SLICE,
            cap=CAP,
        ),
        out_shape=sds((domains * 24, LANES), F32),
        in_specs=[smem()] + [vmem()] * 12,
        out_specs=vmem(),
        scratch_shapes=[
            pltpu.VMEM((len(OFFSETS) * iface // LANES * 8, LANES), I32),
            pltpu.VMEM((32, LANES), F32),
            pltpu.VMEM((32, LANES), F32),
            pltpu.VMEM((groups, LANES), F32),
            pltpu.VMEM((groups, LANES), F32),
            pltpu.VMEM((comps, LANES), F32),
            pltpu.VMEM((groups, LANES), F32),
            pltpu.VMEM((groups, LANES), F32),
            pltpu.VMEM((1, 8, LANES), F32),
        ],
        name="element_work",
    )(here, recv, scale, got, near_x, near_y, connect, comp, dv, s_memb, s_bend, k_memb, k_bend)
    everyone = lax.all_to_all(mine.reshape(domains, 24, LANES), "dom", 0, 0, tiled=True)
    loads = lax.axis_size("load")
    ks_value, sums = pl.pallas_call(
        functools.partial(last_kernel, domains=domains, comps=comps, owned=owned),
        out_shape=(sds((1, comps), F32), sds((loads, owned // LANES, LANES), F32)),
        in_specs=[vmem()] * 2,
        out_specs=(vmem(),) * 2,
        scratch_shapes=[pltpu.VMEM((owned * 2 // LANES, LANES), F32)],
        name="weigh_and_sum",
    )(everyone, multiplier)
    sensitivity = lax.all_to_all(sums, "load", 0, 0, tiled=True).sum(axis=0).reshape(-1)
    return ks_value, sensitivity


def solution(mesh):
    in_specs = (
        P("load", None, "dom"),
        P("load", None, "dom"),
        P("dom", None, None),
        P(None, "dom"),
        P("dom"),
        P("dom"),
        P("dom"),
        P("load", None),
        P(),
        P(),
        P(),
        P(),
    )
    return jax.shard_map(
        per_device, mesh=mesh, in_specs=in_specs, out_specs=(P("load", None), P("dom")), check_vma=False
    )
```

```python
import functools

import jax
import jax.numpy as jnp
from jax import lax
from jax.experimental import pallas as pl
from jax.experimental.pallas import tpu as pltpu
from jax.sharding import PartitionSpec as P

NBR = 3
ROWS = 24
HIGHS = 14
GHOST_HIGHS = 6
SLICE = 1024
CAP = 64
SHARP = 50.0
LOW = -1e30
LANES = 128
DISP_TOP = 8388600.0
ADJ_TOP = 131000.0
ADJ_MID = 131072
OFFSETS = tuple(j - NBR if j < NBR else j - NBR + 1 for j in range(2 * NBR))
I32 = jnp.int32
F32 = jnp.float32
BF16 = jnp.bfloat16


def lane_pick(table, index):
    return jnp.take_along_axis(table, index, axis=1, mode="promise_in_bounds")


def row_shifts(rows):
    row = lax.broadcasted_iota(I32, (rows, LANES), 0)
    return (row % 3) * 10


def scales_of(x_of, tiles, top):
    best = jnp.abs(x_of(tiles[0]))
    for h in tiles[1:]:
        best = jnp.maximum(best, jnp.abs(x_of(h)))
    most = jnp.maximum(jnp.max(best, axis=1, keepdims=True), 1e-30)
    return top / most, most / top


def pack_tile(x, y, x_inv, y_inv, store):
    q = jnp.floor(x * x_inv + 0.5).astype(I32)
    u = jnp.floor(y * y_inv + 0.5).astype(I32) + ADJ_MID
    store(0, 6, (q << 8) | (u & 255))
    high = (u >> 8) << row_shifts(6)
    store(6, 1, high[0:1] + high[1:2] + high[2:3])
    store(7, 1, high[3:4] + high[4:5] + high[5:6])


def unpack_tile(word, x_scale, y_scale):
    x = (word >> 8).astype(F32) * x_scale
    row = lax.broadcasted_iota(I32, (8, LANES), 0)
    first = jnp.broadcast_to(word[6:7], (8, LANES))
    second = jnp.broadcast_to(word[7:8], (8, LANES))
    high = (jnp.where(row < 3, first, second) >> row_shifts(8)) & 1023
    y = (((high << 8) | (word & 255)) - ADJ_MID).astype(F32) * y_scale
    return x, y


def pad_rows(column):
    return jnp.concatenate([jnp.broadcast_to(column, (6, LANES)), jnp.zeros((2, LANES), F32)], axis=0)


def pick(table_of, count, first_high, indices, starts, by_index):
    lows = [i & 127 for i in indices]
    highs = [(i >> 7) - first_high for i in indices]
    found = list(starts)
    steps = [(u, h) for h in range(count) for u in range(len(indices))]
    if by_index:
        steps = [(u, h) for u in range(len(indices)) for h in range(count)]
    for u, h in steps:
        found[u] = jnp.where(highs[u] == h, lane_pick(table_of(h), lows[u]), found[u])
    return found


def send_kernel(here_ref, disp_ref, adj_ref, list_ref, thick_ref, packed_ref, scale_ref, send_ref, *, chunks, domains, iface):
    rows = iface // LANES
    cut = lambda ref, h: ref[pl.ds(h, 6, stride=chunks)]
    x_inv, x_scale = scales_of(lambda h: cut(disp_ref, h), range(chunks), DISP_TOP)
    y_inv, y_scale = scales_of(lambda h: cut(adj_ref, h), range(chunks), ADJ_TOP)
    scale_ref[0:8] = pad_rows(x_scale)
    scale_ref[8:16] = pad_rows(y_scale)
    xs = scale_ref[0:8]
    ys = scale_ref[8:16]
    x_inv = jnp.broadcast_to(x_inv, (6, LANES))
    y_inv = jnp.broadcast_to(y_inv, (6, LANES))
    for h in range(chunks):

        def store(row, many, value, h=h):
            packed_ref[h * 8 + row : h * 8 + row + many] = value

        pack_tile(cut(disp_ref, h), cut(adj_ref, h), x_inv, y_inv, store)

    def thickness_rows(k, half):
        return thick_ref[k * 4 + half * 2 : k * 4 + half * 2 + 2]

    @pl.loop(0, domains)
    def _(d):
        for k in range(rows):
            for half in range(2):
                at = k * 16 + half * 8
                send_ref[d, at : at + 6] = jnp.zeros((6, LANES), F32)
                send_ref[d, at + 6 : at + 8] = thickness_rows(k, half)

    here = here_ref[0]
    row_ids = lax.broadcasted_iota(I32, (8, LANES), 0)
    turns = len(OFFSETS) * rows // 2

    def target_of(turn):
        j = turn // (rows // 2)
        offset = j - NBR + jnp.where(j >= NBR, 1, 0)
        return lax.rem(here - offset + domains, domains)

    def fetch(turn):
        target = target_of(turn)
        base = pl.multiple_of(target // 8 * 8, 8)
        found = []
        for u in range(2):
            k = lax.rem(turn, rows // 2) * 2 + u
            tile = list_ref[0, pl.ds(base, 8), pl.ds(pl.multiple_of(k * LANES, LANES), LANES)]
            row = jnp.sum(jnp.where(row_ids == target - base, tile, 0), axis=0, keepdims=True)
            found.append(jnp.broadcast_to(row, (8, LANES)))
        return tuple(found)

    def body(turn, indices):
        target = target_of(turn)
        picked = pick(
            lambda h: packed_ref[h * 8 : h * 8 + 8], chunks, 0, indices, [jnp.zeros((8, LANES), I32)] * 2, False
        )
        for u in range(2):
            k = lax.rem(turn, rows // 2) * 2 + u
            for half, value in enumerate(unpack_tile(picked[u], xs, ys)):
                at = pl.ds(pl.multiple_of(k * 16 + half * 8, 8), 8)
                send_ref[target, at] = jnp.where(row_ids < 6, value, send_ref[target, at])
        return fetch(jnp.minimum(turn + 1, turns - 1))

    lax.fori_loop(0, turns, body, fetch(jnp.int32(0)))


def fill_table(x_of, y_of, highs, wide_ref, table_ref):
    for high in range(highs):
        for half in range(2):
            lanes = slice(half * LANES, half * LANES + LANES)
            x = x_of(high * 2 + half)
            y = y_of(high * 2 + half)
            xh = x.astype(BF16).astype(F32)
            yh = y.astype(BF16).astype(F32)
            xl = x - xh
            yl = y - yh
            at = high * ROWS
            for piece in (xh, yh[0:2], yl[4:6], yh[2:6], yl[2:4], xl, yl[0:2]):
                wide_ref[at : at + piece.shape[0], lanes] = piece
                at += piece.shape[0]
    table_ref[...] = wide_ref[...].astype(BF16)


def matrix_pick(table_ref, indices, highs, first_high):
    row_ids = lax.broadcasted_iota(I32, (8, LANES), 0)
    names = lax.broadcasted_iota(I32, (256, LANES), 0).astype(F32).astype(BF16)
    one = jnp.ones((256, LANES), BF16)
    none = jnp.zeros((256, LANES), BF16)
    hot = [jnp.where(names == tall_row((i[0:1] & 255).astype(F32), 256), one, none) for i in indices]
    every = jnp.dot(table_ref[...], jnp.concatenate(hot, axis=1), preferred_element_type=F32)
    found = []
    for a, index in enumerate(indices):
        held = [jnp.zeros((8, LANES), F32)] * 3
        for high in range(highs):
            hit = (index >> 8) == high + first_high
            for v in range(3):
                at = high * ROWS + v * 8
                held[v] = jnp.where(hit, every[at : at + 8, a * LANES : (a + 1) * LANES], held[v])
        first = held[0] + held[2]
        second = held[1] + jnp.roll(held[1], 4, axis=0)
        found.append((first, jnp.where(row_ids < 2, jnp.roll(first, 2, axis=0), second)))
    return found


def own_kernel(
    packed_ref, scale_ref, disp_ref, adj_ref, connect_ref, own_x_ref, own_y_ref, wide_ref, table_ref, *, chunks, groups, highs
):
    fill_table(
        lambda h: disp_ref[pl.ds(h, 6, stride=chunks)], lambda h: adj_ref[pl.ds(h, 6, stride=chunks)], highs, wide_ref, table_ref
    )
    xs = scale_ref[0:8]
    ys = scale_ref[8:16]

    def fetch(b):
        rows = connect_ref[:, pl.ds(pl.multiple_of(b * LANES, LANES), LANES)]
        return tuple(jnp.broadcast_to(rows[a : a + 1], (8, LANES)) for a in range(4))

    def body(b, indices):
        near = matrix_pick(table_ref, indices, highs, 0)
        found = pick(
            lambda h: packed_ref[(2 * highs + h) * 8 : (2 * highs + h) * 8 + 8],
            chunks - 2 * highs,
            2 * highs,
            indices,
            [jnp.zeros((8, LANES), I32)] * 4,
            True,
        )
        for a in range(4):
            x, y = unpack_tile(found[a], xs, ys)
            first = indices[a] < highs * 256
            at = pl.ds(pl.multiple_of(b * 32 + a * 8, 8), 8)
            own_x_ref[at] = jnp.where(first, near[a][0], x)
            own_y_ref[at] = jnp.where(first, near[a][1], y)
        return fetch(jnp.minimum(b + 1, groups - 1))

    def several(turn, indices):
        for k in range(4):
            indices = body(turn * 4 + k, indices)
        return indices

    lax.fori_loop(0, groups // 4, several, fetch(jnp.int32(0)))


def spread_matrix(flip):
    shape = (24, 32) if not flip else (32, 24)
    narrow = lax.broadcasted_iota(I32, shape, 1 if flip else 0)
    wide = lax.broadcasted_iota(I32, shape, 0 if flip else 1)
    hit = (narrow // 4 == wide % 8) & (narrow % 4 == wide // 8)
    return jnp.where(hit, 1.0, 0.0).astype(F32)


def three_parts(x):
    parts = []
    for _ in range(3):
        part = x.astype(BF16)
        parts.append(part)
        x = x - part.astype(F32)
    return parts


def dot(a, b):
    return jnp.dot(a, b, precision=lax.Precision.HIGHEST, preferred_element_type=F32)


def main_kernel(
    here_ref,
    recv_ref,
    own_x_ref,
    own_y_ref,
    connect_ref,
    comp_ref,
    dv_ref,
    s_memb_ref,
    s_bend_ref,
    k_memb_ref,
    k_bend_ref,
    out_ref,
    ghost_ref,
    wide_ref,
    table_ref,
    move_ref,
    cost_ref,
    panel_ref,
    fail_ref,
    best_ref,
    slope_ref,
    fixed_ref,
    stats_ref,
    *,
    own,
    groups,
    domains,
    iface,
    comps,
    ghost_highs,
    owned,
    slots,
    cap,
):
    rows = iface // LANES
    ghosts = len(OFFSETS) * rows
    here = here_ref[0]
    sources = [lax.rem(here + offset + domains, domains) for offset in OFFSETS]

    def x_of(h):
        return recv_ref[sources[h // rows], (h % rows) * 16 : (h % rows) * 16 + 6]

    def y_of(h):
        return recv_ref[sources[h // rows], (h % rows) * 16 + 8 : (h % rows) * 16 + 14]

    fill_table(x_of, y_of, ghost_highs, wide_ref, table_ref)
    kept = range(2 * ghost_highs, ghosts)
    x_inv, x_scale = scales_of(x_of, kept, DISP_TOP)
    y_inv, y_scale = scales_of(y_of, kept, ADJ_TOP)
    gx = pad_rows(x_scale)
    gy = pad_rows(y_scale)
    x_inv = jnp.broadcast_to(x_inv, (6, LANES))
    y_inv = jnp.broadcast_to(y_inv, (6, LANES))
    for h in kept:

        def store(row, many, value, h=h):
            at = (h - kept[0]) * 8 + row
            ghost_ref[at : at + many] = value

        pack_tile(x_of(h), y_of(h), x_inv, y_inv, store)
    tiles = groups // 8
    panel_ref[...] = jnp.zeros(panel_ref.shape, F32)

    def panel_step(tile, first, span):
        at = pl.ds(pl.multiple_of(tile * 8, 8), 8)

        def row_of(h):
            k = h % 16
            row = (k // 4) * 16 + (k % 4 // 2) * 8 + 6 + k % 2
            return jnp.broadcast_to(recv_ref[first + h // 16, row : row + 1], (8, LANES))

        panel_ref[at] = pick(row_of, span * 16, first * 16, [dv_ref[at]], [panel_ref[at]], True)[0]

    @pl.loop(0, domains // 8)
    def _(turn):
        panel_step(0, turn * 8, 8)

    wide = spread_matrix(False)
    tall = spread_matrix(True)
    weights = jnp.concatenate(
        [
            dot(s_memb_ref[...], wide),
            dot(s_bend_ref[...], wide),
            dot(tall, dot(k_memb_ref[...], wide)),
            dot(tall, dot(k_bend_ref[...], wide)),
        ],
        axis=0,
    )
    w = three_parts(weights)
    stacked_weights = jnp.concatenate([w[0], w[0], w[1], w[0], w[1], w[2]], axis=1)
    names = lax.broadcasted_iota(I32, (8, LANES), 0)
    combs = comps // 8
    best_ref[...] = jnp.full(best_ref.shape, LOW, F32)

    def gather(b):
        lanes = pl.ds(pl.multiple_of(b * LANES, LANES), LANES)
        rows = connect_ref[:, lanes]
        indices = [jnp.broadcast_to(rows[a : a + 1], (8, LANES)) for a in range(4)]
        found = matrix_pick(table_ref, indices, ghost_highs, own // 2)
        words = pick(
            lambda h: ghost_ref[h * 8 : h * 8 + 8],
            len(kept),
            own + kept[0],
            indices,
            [jnp.zeros((8, LANES), I32)] * 4,
            True,
        )
        for a in range(4):
            x, y = unpack_tile(words[a], gx, gy)
            far = indices[a] >= own * LANES
            farther = indices[a] >= (own + kept[0]) * LANES
            at = pl.ds(pl.multiple_of(b * 32 + a * 8, 8), 8)
            move_ref[a * 8 : a * 8 + 8] = jnp.where(farther, x, jnp.where(far, found[a][0], own_x_ref[at]))
            cost_ref[a * 8 : a * 8 + 8] = jnp.where(farther, y, jnp.where(far, found[a][1], own_y_ref[at]))
        panel_step(jnp.minimum(b // 8 + 1, tiles - 1), lax.rem(b, 8) * (domains // 8), domains // 8)

    def dense(b):
        x = three_parts(move_ref[...])
        part = jnp.dot(
            stacked_weights,
            jnp.concatenate([x[0], x[1], x[0], x[2], x[1], x[0]], axis=0),
            preferred_element_type=F32,
        )
        row = pl.ds(b, 1)
        panel = panel_ref[row]
        bending = part[8:16]
        stress = part[0:8] + panel * bending
        failure = jnp.sum(stress * stress, axis=0, keepdims=True) / 8.0
        slope_ref[row] = jnp.sum(stress * bending, axis=0, keepdims=True) * (2.0 / 8.0)
        stiff = part[16:48] + (3.0 * panel * panel) * part[48:80]
        fixed_ref[row] = jnp.sum(cost_ref[...] * stiff, axis=0, keepdims=True)
        fail_ref[row] = failure
        away = comp_ref[row] - names
        for c in range(combs):
            held = best_ref[c * 8 : c * 8 + 8]
            best_ref[c * 8 : c * 8 + 8] = jnp.maximum(held, jnp.where(away == c * 8, failure, LOW))

    gather(jnp.int32(0))

    @pl.loop(0, (groups - 1) // 3)
    def _(turn):
        for k in range(3):
            dense(turn * 3 + k)
            gather(turn * 3 + k + 1)

    dense(groups - 1)

    stats_ref[0] = jnp.zeros((8, LANES), F32)
    bands = (comps + LANES - 1) // LANES
    diagonal = lax.broadcasted_iota(I32, (LANES, LANES), 0) == lax.broadcasted_iota(I32, (LANES, LANES), 1)

    def to_rows(reduce, start):
        for band in range(bands):
            many = min(LANES, comps - band * LANES)
            column = reduce(best_ref[band * LANES : band * LANES + many], axis=1, keepdims=True)
            row = jnp.sum(jnp.where(diagonal[0:many], column, 0.0), axis=0, keepdims=True)
            stats_ref[0, start + band : start + band + 1] = row

    to_rows(jnp.max, 0)
    for t in range(tiles):
        block = slice(t * 8, t * 8 + 8)
        comp = comp_ref[block]
        low = comp & 127
        high = comp >> 7
        top = jnp.zeros((8, LANES), F32)
        for band in range(bands):
            tile = jnp.broadcast_to(stats_ref[0, band : band + 1], (8, LANES))
            top = jnp.where(high == band, lane_pick(tile, low), top)
        scaled = jnp.exp(SHARP * (fail_ref[block] - top))
        fail_ref[block] = scaled
        slope_ref[block] = slope_ref[block] * scaled

    part_of = combs // 2
    for half in range(2):

        def total_step(step, totals, half=half):
            totals = list(totals)
            for g in range(2):
                row = pl.ds(step * 2 + g, 1)
                away = comp_ref[row] - names
                value = fail_ref[row]
                for c in range(part_of):
                    totals[c] = totals[c] + jnp.where(away == (half * part_of + c) * 8, value, 0.0)
            return tuple(totals)

        totals = lax.fori_loop(0, groups // 2, total_step, (jnp.zeros((8, LANES), F32),) * part_of)
        for c in range(part_of):
            at = (half * part_of + c) * 8
            best_ref[at : at + 8] = totals[c]
    to_rows(jnp.sum, 4)

    shift = owned.bit_length() - 1
    owner_ids = lax.broadcasted_iota(I32, (domains, LANES), 0)
    owner_names = owner_ids.astype(F32).astype(BF16)
    rank_names = lax.broadcasted_iota(I32, (cap, LANES), 0).astype(F32).astype(BF16)
    one = jnp.ones((cap, LANES), BF16)
    zero = jnp.zeros((cap, LANES), BF16)
    none = jnp.zeros((domains, LANES), BF16)
    before = lax.broadcasted_iota(I32, (LANES, LANES), 0) < lax.broadcasted_iota(I32, (LANES, LANES), 1)
    before = jnp.concatenate(
        [jnp.where(before, 1.0, 0.0).astype(BF16), jnp.ones((LANES, LANES), BF16)], axis=1
    )
    block_rows = slots // LANES

    @pl.loop(0, groups // (2 * block_rows))
    def _(pair):
        sums = []
        for parity in range(2):
            at = [pair * 2 * block_rows + parity * block_rows + j for j in range(block_rows)]
            places = [dv_ref[pl.ds(r, 1)] for r in at]
            owners = [jnp.where(owner_ids == (place >> shift), 1.0, 0.0) for place in places]
            counts = jnp.dot(
                jnp.concatenate([o.astype(BF16) for o in owners], axis=0), before, preferred_element_type=F32
            )
            base = jnp.zeros((domains, LANES), F32)
            left = []
            right = []
            for j in range(block_rows):
                count = counts[j * domains : (j + 1) * domains]
                rank = jnp.sum(owners[j] * (count[:, 0:LANES] + base), axis=0, keepdims=True)
                base = base + count[:, LANES : 2 * LANES]
                right.append(jnp.where(rank_names == tall_row(rank, cap), one, zero))
                hit = owner_names == tall_row((places[j] >> shift).astype(F32), domains)
                row = pl.ds(at[j], 1)
                values = (
                    fixed_ref[row],
                    slope_ref[row],
                    (places[j] & (owned - 1)).astype(F32),
                    comp_ref[row].astype(F32),
                )
                pieces = []
                for value in values:
                    rough = value.astype(BF16).astype(F32)
                    pieces.append(jnp.where(hit, tall_row(rough, domains), none))
                    pieces.append(jnp.where(hit, tall_row(value - rough, domains), none))
                left.append(jnp.concatenate(pieces, axis=0))
            moved = lax.dot_general(
                jnp.concatenate(left, axis=1),
                jnp.concatenate(right, axis=1),
                (((1,), (1,)), ((), ())),
                preferred_element_type=F32,
            )
            parts = [moved[p * domains : (p + 1) * domains] for p in range(8)]
            sums.append([parts[2 * v] + parts[2 * v + 1] for v in range(4)])
        for v in range(4):
            out_ref[pl.ds(v * 4 + pair, domains, stride=24)] = jnp.concatenate([sums[0][v], sums[1][v]], axis=1)

    mine = stats_ref[0]
    for d in range(domains):
        out_ref[d * 24 + 16 : d * 24 + 24] = mine


def tall_row(row, many):
    tile = jnp.broadcast_to(row, (16, LANES)).astype(BF16)
    return jnp.concatenate([tile] * (many // 16), axis=0)


def last_kernel(recv_ref, mult_ref, ks_ref, sum_ref, fold_ref, *, domains, comps, owned):
    peak = recv_ref[0, 16:20]
    for s in range(1, domains):
        peak = jnp.maximum(peak, recv_ref[s, 16:20])
    total = jnp.zeros_like(peak)
    for s in range(domains):
        total = total + recv_ref[s, 20:24] * jnp.exp(SHARP * (recv_ref[s, 16:20] - peak))
    ks = peak + jnp.log(total) / SHARP
    bands = (comps + LANES - 1) // LANES
    mults = []
    for band in range(bands):
        many = min(LANES, comps - band * LANES)
        span = slice(band * LANES, band * LANES + many)
        ks_ref[0:1, span] = ks[band : band + 1, 0:many]
        mult = mult_ref[0:1, span]
        if many < LANES:
            mult = jnp.concatenate([mult, jnp.zeros((1, LANES - many), F32)], axis=1)
        mults.append(mult)
    factor = jnp.concatenate(mults, axis=0) / total[0:bands]
    half = LANES // 2
    outer = owned // half
    outer_ids = lax.broadcasted_iota(I32, (outer, LANES), 0).astype(F32).astype(BF16)
    inner_ids = lax.broadcasted_iota(I32, (half, LANES), 0).astype(F32).astype(BF16)
    one = jnp.ones((half, LANES), BF16)
    zero = jnp.zeros((half, LANES), BF16)
    none = jnp.zeros((outer, LANES), BF16)

    def part_sum(sources):
        left = []
        right = []
        for s in sources:
            share = jnp.exp(SHARP * (recv_ref[s, 16 : 16 + bands] - peak[0:bands])) * factor
            values = recv_ref[s, 0:8]
            labels = recv_ref[s, 8:16].astype(I32)
            low = labels & 127
            high = labels >> 7
            weight = jnp.zeros((8, LANES), F32)
            for band in range(bands):
                tile = jnp.broadcast_to(share[band : band + 1], (8, LANES))
                weight = jnp.where(high == band, lane_pick(tile, low), weight)
            terms = values + jnp.roll(weight * values, 4, axis=0)
            roughs = terms.astype(BF16).astype(F32)
            fines = terms - roughs
            outers = (labels >> 6).astype(F32)
            inners = (labels & 63).astype(F32)
            for r in range(4):
                row = slice(r, r + 1)
                hit = outer_ids == tall_row(outers[row], outer)
                left.append(
                    jnp.concatenate(
                        [
                            jnp.where(hit, tall_row(roughs[row], outer), none),
                            jnp.where(hit, tall_row(fines[row], outer), none),
                        ],
                        axis=0,
                    )
                )
                right.append(jnp.where(inner_ids == tall_row(inners[row], half), one, zero))
        both = lax.dot_general(
            jnp.concatenate(left, axis=1),
            jnp.concatenate(right, axis=1),
            (((1,), (1,)), ((), ())),
            preferred_element_type=F32,
        )
        return both[0:outer] + both[outer : 2 * outer]

    def step(turn, sums):
        return tuple(sums[m] + part_sum([turn * 4 + m * 2 + j for j in range(2)]) for m in range(2))

    empty = jnp.zeros((outer, half), F32)
    sums = lax.fori_loop(0, domains // 4, step, (empty, empty))
    fold_ref[:, 0:half] = sums[0] + sums[1]
    folded = jnp.concatenate(
        [fold_ref[pl.ds(parity, outer // 2, stride=2)][:, 0:half] for parity in range(2)], axis=1
    )
    for l in range(sum_ref.shape[0]):
        sum_ref[l] = folded


def vmem():
    return pl.BlockSpec(memory_space=pltpu.VMEM)


def smem():
    return pl.BlockSpec(memory_space=pltpu.SMEM)


def per_device(
    displacement, adjoint, send_list, connect, elem_comp, elem_dv, thickness, multiplier, k_memb, k_bend, s_memb, s_bend
):
    domains = lax.axis_size("dom")
    here = lax.axis_index("dom").astype(I32).reshape(1)
    comps = multiplier.shape[1]
    nodes = displacement.shape[2]
    elems = connect.shape[1]
    iface = send_list.shape[2]
    own = nodes // LANES
    groups = elems // LANES
    block = 4 * iface // LANES * 4
    sds = jax.ShapeDtypeStruct

    disp = displacement.reshape(-1, LANES)
    adj = adjoint.reshape(-1, LANES)
    highs = HIGHS
    ghost_highs = GHOST_HIGHS

    packed, scale, send = pl.pallas_call(
        functools.partial(send_kernel, chunks=own, domains=domains, iface=iface),
        out_shape=(sds((own * 8, LANES), I32), sds((16, LANES), F32), sds((domains, block, LANES), F32)),
        in_specs=[smem()] + [vmem()] * 4,
        out_specs=(vmem(),) * 3,
        name="send_pick",
    )(here, disp, adj, send_list, thickness.reshape(-1, LANES))
    recv = lax.all_to_all(send, "dom", 0, 0, tiled=True)
    own_x, own_y = pl.pallas_call(
        functools.partial(own_kernel, chunks=own, groups=groups, highs=highs),
        out_shape=(sds((groups * 32, LANES), F32),) * 2,
        in_specs=[vmem()] * 5,
        out_specs=(vmem(),) * 2,
        scratch_shapes=[pltpu.VMEM((highs * ROWS, 256), F32), pltpu.VMEM((highs * ROWS, 256), BF16)],
        name="own_pick",
        cost_estimate=pl.CostEstimate(flops=0, transcendentals=0, bytes_accessed=60_000_000),
    )(packed, scale, disp, adj, connect)
    comp = elem_comp.reshape(-1, LANES)
    dv = elem_dv.reshape(-1, LANES)
    owned = thickness.shape[0]
    mine = pl.pallas_call(
        functools.partial(
            main_kernel,
            own=own,
            groups=groups,
            domains=domains,
            iface=iface,
            comps=comps,
            ghost_highs=ghost_highs,
            owned=owned,
            slots=SLICE,
            cap=CAP,
        ),
        out_shape=sds((domains * 24, LANES), F32),
        in_specs=[smem()] + [vmem()] * 10,
        out_specs=vmem(),
        scratch_shapes=[
            pltpu.VMEM(((len(OFFSETS) * iface // LANES - 2 * ghost_highs) * 8, LANES), I32),
            pltpu.VMEM((ghost_highs * ROWS, 256), F32),
            pltpu.VMEM((ghost_highs * ROWS, 256), BF16),
            pltpu.VMEM((32, LANES), F32),
            pltpu.VMEM((32, LANES), F32),
            pltpu.VMEM((groups, LANES), F32),
            pltpu.VMEM((groups, LANES), F32),
            pltpu.VMEM((comps, LANES), F32),
            pltpu.VMEM((groups, LANES), F32),
            pltpu.VMEM((groups, LANES), F32),
            pltpu.VMEM((1, 8, LANES), F32),
        ],
        name="element_work",
    )(here, recv, own_x, own_y, connect, comp, dv, s_memb, s_bend, k_memb, k_bend)
    everyone = lax.all_to_all(mine.reshape(domains, 24, LANES), "dom", 0, 0, tiled=True)
    loads = lax.axis_size("load")
    ks_value, sums = pl.pallas_call(
        functools.partial(last_kernel, domains=domains, comps=comps, owned=owned),
        out_shape=(sds((1, comps), F32), sds((loads, owned // LANES, LANES), F32)),
        in_specs=[vmem()] * 2,
        out_specs=(vmem(),) * 2,
        scratch_shapes=[pltpu.VMEM((owned * 2 // LANES, LANES), F32)],
        name="weigh_and_sum",
    )(everyone, multiplier)
    sensitivity = lax.all_to_all(sums, "load", 0, 0, tiled=True).sum(axis=0).reshape(-1)
    return ks_value, sensitivity


def solution(mesh):
    in_specs = (
        P("load", None, "dom"),
        P("load", None, "dom"),
        P("dom", None, None),
        P(None, "dom"),
        P("dom"),
        P("dom"),
        P("dom"),
        P("load", None),
        P(),
        P(),
        P(),
        P(),
    )
    return jax.shard_map(
        per_device, mesh=mesh, in_specs=in_specs, out_specs=(P("load", None), P("dom")), check_vma=False
    )
```

```python
import functools

import jax
import jax.numpy as jnp
from jax import lax
from jax.experimental import pallas as pl
from jax.experimental.pallas import tpu as pltpu
from jax.sharding import PartitionSpec as P

NBR = 3
ROWS = 24
HIGHS = 14
GHOST_HIGHS = 6
SLICE = 1024
CAP = 64
ROOM = 16 * 1024 * 1024
SHARP = 50.0
LOW = -1e30
LANES = 128
DISP_TOP = 8388600.0
ADJ_TOP = 131000.0
ADJ_MID = 131072
OFFSETS = tuple(j - NBR if j < NBR else j - NBR + 1 for j in range(2 * NBR))
I32 = jnp.int32
F32 = jnp.float32
BF16 = jnp.bfloat16


def lane_pick(table, index):
    return jnp.take_along_axis(table, index, axis=1, mode="promise_in_bounds")


def row_shifts(rows):
    row = lax.broadcasted_iota(I32, (rows, LANES), 0)
    return (row % 3) * 10


def scales_of(x_of, tiles, top):
    best = jnp.abs(x_of(tiles[0]))
    for h in tiles[1:]:
        best = jnp.maximum(best, jnp.abs(x_of(h)))
    most = jnp.maximum(jnp.max(best, axis=1, keepdims=True), 1e-30)
    return top / most, most / top


def pack_tile(x, y, x_inv, y_inv, store):
    q = jnp.floor(x * x_inv + 0.5).astype(I32)
    u = jnp.floor(y * y_inv + 0.5).astype(I32) + ADJ_MID
    store(0, 6, (q << 8) | (u & 255))
    high = (u >> 8) << row_shifts(6)
    store(6, 1, high[0:1] + high[1:2] + high[2:3])
    store(7, 1, high[3:4] + high[4:5] + high[5:6])


def unpack_tile(word, x_scale, y_scale):
    x = (word >> 8).astype(F32) * x_scale
    row = lax.broadcasted_iota(I32, (8, LANES), 0)
    first = jnp.broadcast_to(word[6:7], (8, LANES))
    second = jnp.broadcast_to(word[7:8], (8, LANES))
    high = (jnp.where(row < 3, first, second) >> row_shifts(8)) & 1023
    y = (((high << 8) | (word & 255)) - ADJ_MID).astype(F32) * y_scale
    return x, y


def pad_rows(column):
    return jnp.concatenate([jnp.broadcast_to(column, (6, LANES)), jnp.zeros((2, LANES), F32)], axis=0)


def pick(table_of, count, first_high, indices, starts, by_index):
    lows = [i & 127 for i in indices]
    highs = [(i >> 7) - first_high for i in indices]
    found = list(starts)
    steps = [(u, h) for h in range(count) for u in range(len(indices))]
    if by_index:
        steps = [(u, h) for u in range(len(indices)) for h in range(count)]
    for u, h in steps:
        found[u] = jnp.where(highs[u] == h, lane_pick(table_of(h), lows[u]), found[u])
    return found


def send_kernel(here_ref, disp_ref, adj_ref, list_ref, thick_ref, packed_ref, scale_ref, send_ref, *, chunks, domains, iface):
    rows = iface // LANES
    cut = lambda ref, h: ref[pl.ds(h, 6, stride=chunks)]
    x_inv, x_scale = scales_of(lambda h: cut(disp_ref, h), range(chunks), DISP_TOP)
    y_inv, y_scale = scales_of(lambda h: cut(adj_ref, h), range(chunks), ADJ_TOP)
    scale_ref[0:8] = pad_rows(x_scale)
    scale_ref[8:16] = pad_rows(y_scale)
    xs = scale_ref[0:8]
    ys = scale_ref[8:16]
    x_inv = jnp.broadcast_to(x_inv, (6, LANES))
    y_inv = jnp.broadcast_to(y_inv, (6, LANES))
    for h in range(chunks):

        def store(row, many, value, h=h):
            packed_ref[h * 8 + row : h * 8 + row + many] = value

        pack_tile(cut(disp_ref, h), cut(adj_ref, h), x_inv, y_inv, store)

    def thickness_rows(k, half):
        return thick_ref[k * 4 + half * 2 : k * 4 + half * 2 + 2]

    @pl.loop(0, domains)
    def _(d):
        for k in range(rows):
            for half in range(2):
                at = k * 16 + half * 8
                send_ref[d, at : at + 6] = jnp.zeros((6, LANES), F32)
                send_ref[d, at + 6 : at + 8] = thickness_rows(k, half)

    here = here_ref[0]
    row_ids = lax.broadcasted_iota(I32, (8, LANES), 0)
    turns = len(OFFSETS) * rows // 2

    def target_of(turn):
        j = turn // (rows // 2)
        offset = j - NBR + jnp.where(j >= NBR, 1, 0)
        return lax.rem(here - offset + domains, domains)

    def fetch(turn):
        target = target_of(turn)
        base = pl.multiple_of(target // 8 * 8, 8)
        found = []
        for u in range(2):
            k = lax.rem(turn, rows // 2) * 2 + u
            tile = list_ref[0, pl.ds(base, 8), pl.ds(pl.multiple_of(k * LANES, LANES), LANES)]
            row = jnp.sum(jnp.where(row_ids == target - base, tile, 0), axis=0, keepdims=True)
            found.append(jnp.broadcast_to(row, (8, LANES)))
        return tuple(found)

    def body(turn, indices):
        target = target_of(turn)
        picked = pick(
            lambda h: packed_ref[h * 8 : h * 8 + 8], chunks, 0, indices, [jnp.zeros((8, LANES), I32)] * 2, False
        )
        for u in range(2):
            k = lax.rem(turn, rows // 2) * 2 + u
            for half, value in enumerate(unpack_tile(picked[u], xs, ys)):
                at = pl.ds(pl.multiple_of(k * 16 + half * 8, 8), 8)
                send_ref[target, at] = jnp.where(row_ids < 6, value, send_ref[target, at])
        return fetch(jnp.minimum(turn + 1, turns - 1))

    lax.fori_loop(0, turns, body, fetch(jnp.int32(0)))


def fill_table(x_of, y_of, highs, wide_ref, table_ref):
    for high in range(highs):
        for half in range(2):
            lanes = slice(half * LANES, half * LANES + LANES)
            x = x_of(high * 2 + half)
            y = y_of(high * 2 + half)
            xh = x.astype(BF16).astype(F32)
            yh = y.astype(BF16).astype(F32)
            xl = x - xh
            yl = y - yh
            at = high * ROWS
            for piece in (xh, yh[0:2], yl[4:6], yh[2:6], yl[2:4], xl, yl[0:2]):
                wide_ref[at : at + piece.shape[0], lanes] = piece
                at += piece.shape[0]
    table_ref[...] = wide_ref[...].astype(BF16)


def matrix_pick(table_ref, indices, highs, first_high):
    row_ids = lax.broadcasted_iota(I32, (8, LANES), 0)
    names = lax.broadcasted_iota(I32, (256, LANES), 0).astype(F32).astype(BF16)
    one = jnp.ones((256, LANES), BF16)
    none = jnp.zeros((256, LANES), BF16)
    hot = [jnp.where(names == tall_row((i[0:1] & 255).astype(F32), 256), one, none) for i in indices]
    every = jnp.dot(table_ref[...], jnp.concatenate(hot, axis=1), preferred_element_type=F32)
    found = []
    for a, index in enumerate(indices):
        held = [jnp.zeros((8, LANES), F32)] * 3
        for high in range(highs):
            hit = (index >> 8) == high + first_high
            for v in range(3):
                at = high * ROWS + v * 8
                held[v] = jnp.where(hit, every[at : at + 8, a * LANES : (a + 1) * LANES], held[v])
        first = held[0] + held[2]
        second = held[1] + jnp.roll(held[1], 4, axis=0)
        found.append((first, jnp.where(row_ids < 2, jnp.roll(first, 2, axis=0), second)))
    return found


def own_kernel(
    packed_ref, scale_ref, disp_ref, adj_ref, connect_ref, own_x_ref, own_y_ref, wide_ref, table_ref, *, chunks, groups, highs
):
    fill_table(
        lambda h: disp_ref[pl.ds(h, 6, stride=chunks)], lambda h: adj_ref[pl.ds(h, 6, stride=chunks)], highs, wide_ref, table_ref
    )
    xs = scale_ref[0:8]
    ys = scale_ref[8:16]

    def fetch(b):
        rows = connect_ref[:, pl.ds(pl.multiple_of(b * LANES, LANES), LANES)]
        return tuple(jnp.broadcast_to(rows[a : a + 1], (8, LANES)) for a in range(4))

    def body(b, indices):
        near = matrix_pick(table_ref, indices, highs, 0)
        found = pick(
            lambda h: packed_ref[(2 * highs + h) * 8 : (2 * highs + h) * 8 + 8],
            chunks - 2 * highs,
            2 * highs,
            indices,
            [jnp.zeros((8, LANES), I32)] * 4,
            True,
        )
        for a in range(4):
            x, y = unpack_tile(found[a], xs, ys)
            first = indices[a] < highs * 256
            at = pl.ds(pl.multiple_of(b * 32 + a * 8, 8), 8)
            own_x_ref[at] = jnp.where(first, near[a][0], x)
            own_y_ref[at] = jnp.where(first, near[a][1], y)
        return fetch(jnp.minimum(b + 1, groups - 1))

    def several(turn, indices):
        for k in range(4):
            indices = body(turn * 4 + k, indices)
        return indices

    lax.fori_loop(0, groups // 4, several, fetch(jnp.int32(0)))


def spread_matrix(flip):
    shape = (24, 32) if not flip else (32, 24)
    narrow = lax.broadcasted_iota(I32, shape, 1 if flip else 0)
    wide = lax.broadcasted_iota(I32, shape, 0 if flip else 1)
    hit = (narrow // 4 == wide % 8) & (narrow % 4 == wide // 8)
    return jnp.where(hit, 1.0, 0.0).astype(F32)


def three_parts(x):
    parts = []
    for _ in range(3):
        part = x.astype(BF16)
        parts.append(part)
        x = x - part.astype(F32)
    return parts


def dot(a, b):
    return jnp.dot(a, b, precision=lax.Precision.HIGHEST, preferred_element_type=F32)


def main_kernel(
    here_ref,
    recv_ref,
    own_x_ref,
    own_y_ref,
    connect_ref,
    comp_ref,
    dv_ref,
    s_memb_ref,
    s_bend_ref,
    k_memb_ref,
    k_bend_ref,
    out_ref,
    ghost_ref,
    wide_ref,
    table_ref,
    move_ref,
    cost_ref,
    panel_ref,
    fail_ref,
    best_ref,
    slope_ref,
    fixed_ref,
    stats_ref,
    *,
    own,
    groups,
    domains,
    iface,
    comps,
    ghost_highs,
    owned,
    slots,
    cap,
):
    rows = iface // LANES
    ghosts = len(OFFSETS) * rows
    here = here_ref[0]
    sources = [lax.rem(here + offset + domains, domains) for offset in OFFSETS]

    def x_of(h):
        return recv_ref[sources[h // rows], (h % rows) * 16 : (h % rows) * 16 + 6]

    def y_of(h):
        return recv_ref[sources[h // rows], (h % rows) * 16 + 8 : (h % rows) * 16 + 14]

    fill_table(x_of, y_of, ghost_highs, wide_ref, table_ref)
    kept = range(2 * ghost_highs, ghosts)
    x_inv, x_scale = scales_of(x_of, kept, DISP_TOP)
    y_inv, y_scale = scales_of(y_of, kept, ADJ_TOP)
    gx = pad_rows(x_scale)
    gy = pad_rows(y_scale)
    x_inv = jnp.broadcast_to(x_inv, (6, LANES))
    y_inv = jnp.broadcast_to(y_inv, (6, LANES))
    for h in kept:

        def store(row, many, value, h=h):
            at = (h - kept[0]) * 8 + row
            ghost_ref[at : at + many] = value

        pack_tile(x_of(h), y_of(h), x_inv, y_inv, store)
    tiles = groups // 8
    panel_ref[...] = jnp.zeros(panel_ref.shape, F32)

    def panel_step(tile, first, span):
        at = pl.ds(pl.multiple_of(tile * 8, 8), 8)

        def row_of(h):
            k = h % 16
            row = (k // 4) * 16 + (k % 4 // 2) * 8 + 6 + k % 2
            return jnp.broadcast_to(recv_ref[first + h // 16, row : row + 1], (8, LANES))

        panel_ref[at] = pick(row_of, span * 16, first * 16, [dv_ref[at]], [panel_ref[at]], True)[0]

    @pl.loop(0, domains // 8)
    def _(turn):
        panel_step(0, turn * 8, 8)

    wide = spread_matrix(False)
    tall = spread_matrix(True)
    weights = jnp.concatenate(
        [
            dot(s_memb_ref[...], wide),
            dot(s_bend_ref[...], wide),
            dot(tall, dot(k_memb_ref[...], wide)),
            dot(tall, dot(k_bend_ref[...], wide)),
        ],
        axis=0,
    )
    w = three_parts(weights)
    stacked_weights = jnp.concatenate([w[0], w[0], w[1], w[0], w[1], w[2]], axis=1)
    names = lax.broadcasted_iota(I32, (8, LANES), 0)
    combs = comps // 8
    best_ref[...] = jnp.full(best_ref.shape, LOW, F32)

    def gather(b):
        lanes = pl.ds(pl.multiple_of(b * LANES, LANES), LANES)
        rows = connect_ref[:, lanes]
        indices = [jnp.broadcast_to(rows[a : a + 1], (8, LANES)) for a in range(4)]
        found = matrix_pick(table_ref, indices, ghost_highs, own // 2)
        words = pick(
            lambda h: ghost_ref[h * 8 : h * 8 + 8],
            len(kept),
            own + kept[0],
            indices,
            [jnp.zeros((8, LANES), I32)] * 4,
            True,
        )
        for a in range(4):
            x, y = unpack_tile(words[a], gx, gy)
            far = indices[a] >= own * LANES
            farther = indices[a] >= (own + kept[0]) * LANES
            at = pl.ds(pl.multiple_of(b * 32 + a * 8, 8), 8)
            move_ref[a * 8 : a * 8 + 8] = jnp.where(farther, x, jnp.where(far, found[a][0], own_x_ref[at]))
            cost_ref[a * 8 : a * 8 + 8] = jnp.where(farther, y, jnp.where(far, found[a][1], own_y_ref[at]))
        panel_step(jnp.minimum(b // 8 + 1, tiles - 1), lax.rem(b, 8) * (domains // 8), domains // 8)

    def dense(b):
        x = three_parts(move_ref[...])
        part = jnp.dot(
            stacked_weights,
            jnp.concatenate([x[0], x[1], x[0], x[2], x[1], x[0]], axis=0),
            preferred_element_type=F32,
        )
        row = pl.ds(b, 1)
        panel = panel_ref[row]
        bending = part[8:16]
        stress = part[0:8] + panel * bending
        failure = jnp.sum(stress * stress, axis=0, keepdims=True) / 8.0
        slope_ref[row] = jnp.sum(stress * bending, axis=0, keepdims=True) * (2.0 / 8.0)
        stiff = part[16:48] + (3.0 * panel * panel) * part[48:80]
        fixed_ref[row] = jnp.sum(cost_ref[...] * stiff, axis=0, keepdims=True)
        fail_ref[row] = failure
        away = comp_ref[row] - names
        for c in range(combs):
            held = best_ref[c * 8 : c * 8 + 8]
            best_ref[c * 8 : c * 8 + 8] = jnp.maximum(held, jnp.where(away == c * 8, failure, LOW))

    gather(jnp.int32(0))

    @pl.loop(0, (groups - 1) // 3)
    def _(turn):
        for k in range(3):
            dense(turn * 3 + k)
            gather(turn * 3 + k + 1)

    dense(groups - 1)

    stats_ref[0] = jnp.zeros((8, LANES), F32)
    bands = (comps + LANES - 1) // LANES
    diagonal = lax.broadcasted_iota(I32, (LANES, LANES), 0) == lax.broadcasted_iota(I32, (LANES, LANES), 1)

    def to_rows(reduce, start):
        for band in range(bands):
            many = min(LANES, comps - band * LANES)
            column = reduce(best_ref[band * LANES : band * LANES + many], axis=1, keepdims=True)
            row = jnp.sum(jnp.where(diagonal[0:many], column, 0.0), axis=0, keepdims=True)
            stats_ref[0, start + band : start + band + 1] = row

    to_rows(jnp.max, 0)
    for t in range(tiles):
        block = slice(t * 8, t * 8 + 8)
        comp = comp_ref[block]
        low = comp & 127
        high = comp >> 7
        top = jnp.zeros((8, LANES), F32)
        for band in range(bands):
            tile = jnp.broadcast_to(stats_ref[0, band : band + 1], (8, LANES))
            top = jnp.where(high == band, lane_pick(tile, low), top)
        scaled = jnp.exp(SHARP * (fail_ref[block] - top))
        fail_ref[block] = scaled
        slope_ref[block] = slope_ref[block] * scaled

    part_of = combs // 2
    for half in range(2):

        def total_step(step, totals, half=half):
            totals = list(totals)
            for g in range(2):
                row = pl.ds(step * 2 + g, 1)
                away = comp_ref[row] - names
                value = fail_ref[row]
                for c in range(part_of):
                    totals[c] = totals[c] + jnp.where(away == (half * part_of + c) * 8, value, 0.0)
            return tuple(totals)

        totals = lax.fori_loop(0, groups // 2, total_step, (jnp.zeros((8, LANES), F32),) * part_of)
        for c in range(part_of):
            at = (half * part_of + c) * 8
            best_ref[at : at + 8] = totals[c]
    to_rows(jnp.sum, 4)

    shift = owned.bit_length() - 1
    owner_ids = lax.broadcasted_iota(I32, (domains, LANES), 0)
    owner_names = owner_ids.astype(F32).astype(BF16)
    rank_names = lax.broadcasted_iota(I32, (cap, LANES), 0).astype(F32).astype(BF16)
    one = jnp.ones((cap, LANES), BF16)
    zero = jnp.zeros((cap, LANES), BF16)
    none = jnp.zeros((domains, LANES), BF16)
    before = lax.broadcasted_iota(I32, (LANES, LANES), 0) < lax.broadcasted_iota(I32, (LANES, LANES), 1)
    before = jnp.concatenate(
        [jnp.where(before, 1.0, 0.0).astype(BF16), jnp.ones((LANES, LANES), BF16)], axis=1
    )
    block_rows = slots // LANES

    @pl.loop(0, groups // (2 * block_rows))
    def _(pair):
        sums = []
        for parity in range(2):
            at = [pair * 2 * block_rows + parity * block_rows + j for j in range(block_rows)]
            places = [dv_ref[pl.ds(r, 1)] for r in at]
            owners = [jnp.where(owner_ids == (place >> shift), 1.0, 0.0) for place in places]
            counts = jnp.dot(
                jnp.concatenate([o.astype(BF16) for o in owners], axis=0), before, preferred_element_type=F32
            )
            base = jnp.zeros((domains, LANES), F32)
            left = []
            right = []
            for j in range(block_rows):
                count = counts[j * domains : (j + 1) * domains]
                rank = jnp.sum(owners[j] * (count[:, 0:LANES] + base), axis=0, keepdims=True)
                base = base + count[:, LANES : 2 * LANES]
                right.append(jnp.where(rank_names == tall_row(rank, cap), one, zero))
                hit = owner_names == tall_row((places[j] >> shift).astype(F32), domains)
                row = pl.ds(at[j], 1)
                values = (
                    fixed_ref[row],
                    slope_ref[row],
                    (places[j] & (owned - 1)).astype(F32),
                    comp_ref[row].astype(F32),
                )
                pieces = []
                for value in values:
                    rough = value.astype(BF16).astype(F32)
                    pieces.append(jnp.where(hit, tall_row(rough, domains), none))
                    pieces.append(jnp.where(hit, tall_row(value - rough, domains), none))
                left.append(jnp.concatenate(pieces, axis=0))
            moved = lax.dot_general(
                jnp.concatenate(left, axis=1),
                jnp.concatenate(right, axis=1),
                (((1,), (1,)), ((), ())),
                preferred_element_type=F32,
            )
            parts = [moved[p * domains : (p + 1) * domains] for p in range(8)]
            sums.append([parts[2 * v] + parts[2 * v + 1] for v in range(4)])
        for v in range(4):
            out_ref[pl.ds(v * 4 + pair, domains, stride=24)] = jnp.concatenate([sums[0][v], sums[1][v]], axis=1)

    mine = stats_ref[0]
    for d in range(domains):
        out_ref[d * 24 + 16 : d * 24 + 24] = mine


def tall_row(row, many):
    tile = jnp.broadcast_to(row, (16, LANES)).astype(BF16)
    return jnp.concatenate([tile] * (many // 16), axis=0)


def last_kernel(recv_ref, mult_ref, ks_ref, sum_ref, fold_ref, *, domains, comps, owned):
    peak = recv_ref[0, 16:20]
    for s in range(1, domains):
        peak = jnp.maximum(peak, recv_ref[s, 16:20])
    total = jnp.zeros_like(peak)
    for s in range(domains):
        total = total + recv_ref[s, 20:24] * jnp.exp(SHARP * (recv_ref[s, 16:20] - peak))
    ks = peak + jnp.log(total) / SHARP
    bands = (comps + LANES - 1) // LANES
    mults = []
    for band in range(bands):
        many = min(LANES, comps - band * LANES)
        span = slice(band * LANES, band * LANES + many)
        ks_ref[0:1, span] = ks[band : band + 1, 0:many]
        mult = mult_ref[0:1, span]
        if many < LANES:
            mult = jnp.concatenate([mult, jnp.zeros((1, LANES - many), F32)], axis=1)
        mults.append(mult)
    factor = jnp.concatenate(mults, axis=0) / total[0:bands]
    half = LANES // 2
    outer = owned // half
    outer_ids = lax.broadcasted_iota(I32, (outer, LANES), 0).astype(F32).astype(BF16)
    inner_ids = lax.broadcasted_iota(I32, (half, LANES), 0).astype(F32).astype(BF16)
    one = jnp.ones((half, LANES), BF16)
    zero = jnp.zeros((half, LANES), BF16)
    none = jnp.zeros((outer, LANES), BF16)

    def part_sum(sources):
        left = []
        right = []
        for s in sources:
            share = jnp.exp(SHARP * (recv_ref[s, 16 : 16 + bands] - peak[0:bands])) * factor
            values = recv_ref[s, 0:8]
            labels = recv_ref[s, 8:16].astype(I32)
            low = labels & 127
            high = labels >> 7
            weight = jnp.zeros((8, LANES), F32)
            for band in range(bands):
                tile = jnp.broadcast_to(share[band : band + 1], (8, LANES))
                weight = jnp.where(high == band, lane_pick(tile, low), weight)
            terms = values + jnp.roll(weight * values, 4, axis=0)
            roughs = terms.astype(BF16).astype(F32)
            fines = terms - roughs
            outers = (labels >> 6).astype(F32)
            inners = (labels & 63).astype(F32)
            for r in range(4):
                row = slice(r, r + 1)
                hit = outer_ids == tall_row(outers[row], outer)
                left.append(
                    jnp.concatenate(
                        [
                            jnp.where(hit, tall_row(roughs[row], outer), none),
                            jnp.where(hit, tall_row(fines[row], outer), none),
                        ],
                        axis=0,
                    )
                )
                right.append(jnp.where(inner_ids == tall_row(inners[row], half), one, zero))
        both = lax.dot_general(
            jnp.concatenate(left, axis=1),
            jnp.concatenate(right, axis=1),
            (((1,), (1,)), ((), ())),
            preferred_element_type=F32,
        )
        return both[0:outer] + both[outer : 2 * outer]

    def step(turn, sums):
        return tuple(sums[m] + part_sum([turn * 4 + m * 2 + j for j in range(2)]) for m in range(2))

    empty = jnp.zeros((outer, half), F32)
    sums = lax.fori_loop(0, domains // 4, step, (empty, empty))
    fold_ref[:, 0:half] = sums[0] + sums[1]
    folded = jnp.concatenate(
        [fold_ref[pl.ds(parity, outer // 2, stride=2)][:, 0:half] for parity in range(2)], axis=1
    )
    for l in range(sum_ref.shape[0]):
        sum_ref[l] = folded


def vmem():
    return pl.BlockSpec(memory_space=pltpu.VMEM)


def smem():
    return pl.BlockSpec(memory_space=pltpu.SMEM)


def per_device(
    displacement, adjoint, send_list, connect, elem_comp, elem_dv, thickness, multiplier, k_memb, k_bend, s_memb, s_bend
):
    domains = lax.axis_size("dom")
    here = lax.axis_index("dom").astype(I32).reshape(1)
    comps = multiplier.shape[1]
    nodes = displacement.shape[2]
    elems = connect.shape[1]
    iface = send_list.shape[2]
    own = nodes // LANES
    groups = elems // LANES
    block = 4 * iface // LANES * 4
    sds = jax.ShapeDtypeStruct
    near = pltpu.VMEM

    def close(x):
        return pltpu.with_memory_space_constraint(x, pltpu.VMEM)

    def far(x):
        return pltpu.with_memory_space_constraint(x, pltpu.HBM)


    disp = far(displacement.reshape(-1, LANES))
    adj = far(adjoint.reshape(-1, LANES))
    connect = far(connect)
    highs = HIGHS
    ghost_highs = GHOST_HIGHS

    packed, scale, send = pl.pallas_call(
        functools.partial(send_kernel, chunks=own, domains=domains, iface=iface),
        out_shape=(pltpu.HBM((own * 8, LANES), I32), pltpu.HBM((16, LANES), F32), sds((domains, block, LANES), F32)),
        in_specs=[smem()] + [vmem()] * 4,
        out_specs=(vmem(),) * 3,
        compiler_params=pltpu.CompilerParams(vmem_limit_bytes=ROOM),
        name="send_pick",
    )(here, disp, adj, far(send_list), far(thickness.reshape(-1, LANES)))
    recv = lax.all_to_all(send, "dom", 0, 0, tiled=True)
    own_x, own_y = pl.pallas_call(
        functools.partial(own_kernel, chunks=own, groups=groups, highs=highs),
        out_shape=(near((groups * 32, LANES), F32),) * 2,
        in_specs=[vmem()] * 5,
        out_specs=(vmem(),) * 2,
        scratch_shapes=[pltpu.VMEM((highs * ROWS, 256), F32), pltpu.VMEM((highs * ROWS, 256), BF16)],
        compiler_params=pltpu.CompilerParams(vmem_limit_bytes=ROOM),
        name="own_pick",
        cost_estimate=pl.CostEstimate(flops=0, transcendentals=0, bytes_accessed=60_000_000),
    )(far(packed), far(scale), disp, adj, connect)
    comp = far(elem_comp.reshape(-1, LANES))
    dv = far(elem_dv.reshape(-1, LANES))
    owned = thickness.shape[0]
    mine = pl.pallas_call(
        functools.partial(
            main_kernel,
            own=own,
            groups=groups,
            domains=domains,
            iface=iface,
            comps=comps,
            ghost_highs=ghost_highs,
            owned=owned,
            slots=SLICE,
            cap=CAP,
        ),
        out_shape=near((domains * 24, LANES), F32),
        in_specs=[smem()] + [vmem()] * 10,
        out_specs=vmem(),
        scratch_shapes=[
            pltpu.VMEM(((len(OFFSETS) * iface // LANES - 2 * ghost_highs) * 8, LANES), I32),
            pltpu.VMEM((ghost_highs * ROWS, 256), F32),
            pltpu.VMEM((ghost_highs * ROWS, 256), BF16),
            pltpu.VMEM((32, LANES), F32),
            pltpu.VMEM((32, LANES), F32),
            pltpu.VMEM((groups, LANES), F32),
            pltpu.VMEM((groups, LANES), F32),
            pltpu.VMEM((comps, LANES), F32),
            pltpu.VMEM((groups, LANES), F32),
            pltpu.VMEM((groups, LANES), F32),
            pltpu.VMEM((1, 8, LANES), F32),
        ],
        compiler_params=pltpu.CompilerParams(vmem_limit_bytes=ROOM),
        name="element_work",
    )(here, close(recv), close(own_x), close(own_y), connect, comp, dv, far(s_memb), far(s_bend), far(k_memb), far(k_bend))
    everyone = lax.all_to_all(mine.reshape(domains, 24, LANES), "dom", 0, 0, tiled=True)
    loads = lax.axis_size("load")
    ks_value, sums = pl.pallas_call(
        functools.partial(last_kernel, domains=domains, comps=comps, owned=owned),
        out_shape=(sds((1, comps), F32), near((loads, owned // LANES, LANES), F32)),
        in_specs=[vmem()] * 2,
        out_specs=(vmem(),) * 2,
        scratch_shapes=[pltpu.VMEM((owned * 2 // LANES, LANES), F32)],
        compiler_params=pltpu.CompilerParams(vmem_limit_bytes=ROOM),
        name="weigh_and_sum",
    )(close(everyone), far(multiplier))
    sensitivity = lax.all_to_all(sums, "load", 0, 0, tiled=True).sum(axis=0).reshape(-1)
    return ks_value, sensitivity


def solution(mesh):
    in_specs = (
        P("load", None, "dom"),
        P("load", None, "dom"),
        P("dom", None, None),
        P(None, "dom"),
        P("dom"),
        P("dom"),
        P("dom"),
        P("load", None),
        P(),
        P(),
        P(),
        P(),
    )
    return jax.shard_map(
        per_device, mesh=mesh, in_specs=in_specs, out_specs=(P("load", None), P("dom")), check_vma=False
    )
```

```python
import functools

import jax
import jax.numpy as jnp
from jax import lax
from jax.experimental import pallas as pl
from jax.experimental.pallas import tpu as pltpu
from jax.sharding import PartitionSpec as P

NBR = 3
ROWS = 24
HIGHS = 18
GHOST_HIGHS = 6
SLICE = 1024
CAP = 64
ROOM = 16 * 1024 * 1024
SHARP = 50.0
LOW = -1e30
LANES = 128
DISP_TOP = 8388600.0
ADJ_TOP = 131000.0
ADJ_MID = 131072
OFFSETS = tuple(j - NBR if j < NBR else j - NBR + 1 for j in range(2 * NBR))
I32 = jnp.int32
F32 = jnp.float32
BF16 = jnp.bfloat16


def lane_pick(table, index):
    return jnp.take_along_axis(table, index, axis=1, mode="promise_in_bounds")


def row_shifts(rows):
    row = lax.broadcasted_iota(I32, (rows, LANES), 0)
    return (row % 3) * 10


def scales_of(x_of, tiles, top):
    best = jnp.abs(x_of(tiles[0]))
    for h in tiles[1:]:
        best = jnp.maximum(best, jnp.abs(x_of(h)))
    most = jnp.maximum(jnp.max(best, axis=1, keepdims=True), 1e-30)
    return top / most, most / top


def pack_tile(x, y, x_inv, y_inv, store):
    q = jnp.floor(x * x_inv + 0.5).astype(I32)
    u = jnp.floor(y * y_inv + 0.5).astype(I32) + ADJ_MID
    store(0, 6, (q << 8) | (u & 255))
    high = (u >> 8) << row_shifts(6)
    store(6, 1, high[0:1] + high[1:2] + high[2:3])
    store(7, 1, high[3:4] + high[4:5] + high[5:6])


def unpack_tile(word, x_scale, y_scale):
    x = (word >> 8).astype(F32) * x_scale
    row = lax.broadcasted_iota(I32, (8, LANES), 0)
    first = jnp.broadcast_to(word[6:7], (8, LANES))
    second = jnp.broadcast_to(word[7:8], (8, LANES))
    high = (jnp.where(row < 3, first, second) >> row_shifts(8)) & 1023
    y = (((high << 8) | (word & 255)) - ADJ_MID).astype(F32) * y_scale
    return x, y


def pad_rows(column):
    return jnp.concatenate([jnp.broadcast_to(column, (6, LANES)), jnp.zeros((2, LANES), F32)], axis=0)


def pick(table_of, count, first_high, indices, starts, by_index):
    lows = [i & 127 for i in indices]
    highs = [(i >> 7) - first_high for i in indices]
    found = list(starts)
    steps = [(u, h) for h in range(count) for u in range(len(indices))]
    if by_index:
        steps = [(u, h) for u in range(len(indices)) for h in range(count)]
    for u, h in steps:
        found[u] = jnp.where(highs[u] == h, lane_pick(table_of(h), lows[u]), found[u])
    return found


def send_kernel(
    here_ref,
    disp_ref,
    adj_ref,
    list_ref,
    thick_ref,
    packed_ref,
    scale_ref,
    table_ref,
    send_ref,
    wide_ref,
    *,
    chunks,
    domains,
    iface,
    highs,
):
    rows = iface // LANES
    cut = lambda ref, h: ref[pl.ds(h, 6, stride=chunks)]
    x_inv, x_scale = scales_of(lambda h: cut(disp_ref, h), range(chunks), DISP_TOP)
    y_inv, y_scale = scales_of(lambda h: cut(adj_ref, h), range(chunks), ADJ_TOP)
    scale_ref[0:8] = pad_rows(x_scale)
    scale_ref[8:16] = pad_rows(y_scale)
    xs = scale_ref[0:8]
    ys = scale_ref[8:16]
    x_inv = jnp.broadcast_to(x_inv, (6, LANES))
    y_inv = jnp.broadcast_to(y_inv, (6, LANES))
    for h in range(chunks):

        def store(row, many, value, h=h):
            packed_ref[h * 8 + row : h * 8 + row + many] = value

        pack_tile(cut(disp_ref, h), cut(adj_ref, h), x_inv, y_inv, store)

    def thickness_rows(k, half):
        return thick_ref[k * 4 + half * 2 : k * 4 + half * 2 + 2]

    @pl.loop(0, domains)
    def _(d):
        for k in range(rows):
            for half in range(2):
                at = k * 16 + half * 8
                send_ref[d, at : at + 6] = jnp.zeros((6, LANES), F32)
                send_ref[d, at + 6 : at + 8] = thickness_rows(k, half)

    here = here_ref[0]
    row_ids = lax.broadcasted_iota(I32, (8, LANES), 0)
    fill_table(lambda h: cut(disp_ref, h), lambda h: cut(adj_ref, h), highs, wide_ref, table_ref)

    @pl.loop(0, len(OFFSETS) // 3)
    def _(turn):
        for step in range(3):
            j = turn * 3 + step
            offset = j - NBR + jnp.where(j >= NBR, 1, 0)
            target = lax.rem(here - offset + domains, domains)
            base = pl.multiple_of(target // 8 * 8, 8)
            indices = []
            for k in range(rows):
                tile = list_ref[0, pl.ds(base, 8), k * LANES : (k + 1) * LANES]
                row = jnp.sum(jnp.where(row_ids == target - base, tile, 0), axis=0, keepdims=True)
                indices.append(jnp.broadcast_to(row, (8, LANES)))
            found = hybrid_pick(packed_ref, table_ref, indices, chunks, highs, xs, ys)
            for k in range(rows):
                for half in range(2):
                    at = slice(k * 16 + half * 8, k * 16 + half * 8 + 8)
                    send_ref[target, at] = jnp.where(row_ids < 6, found[k][half], send_ref[target, at])


def fill_table(x_of, y_of, highs, wide_ref, table_ref):
    for high in range(highs):
        for half in range(2):
            lanes = slice(half * LANES, half * LANES + LANES)
            x = x_of(high * 2 + half)
            y = y_of(high * 2 + half)
            xh = x.astype(BF16).astype(F32)
            yh = y.astype(BF16).astype(F32)
            xl = x - xh
            yl = y - yh
            at = high * ROWS
            for piece in (xh, yh[0:2], yl[4:6], yh[2:6], yl[2:4], xl, yl[0:2]):
                wide_ref[at : at + piece.shape[0], lanes] = piece
                at += piece.shape[0]
    table_ref[...] = wide_ref[...].astype(BF16)


def matrix_pick(table_ref, indices, highs, first_high):
    row_ids = lax.broadcasted_iota(I32, (8, LANES), 0)
    names = lax.broadcasted_iota(I32, (256, LANES), 0).astype(F32).astype(BF16)
    one = jnp.ones((256, LANES), BF16)
    none = jnp.zeros((256, LANES), BF16)
    hot = [jnp.where(names == tall_row((i[0:1] & 255).astype(F32), 256), one, none) for i in indices]
    every = jnp.dot(table_ref[...], jnp.concatenate(hot, axis=1), preferred_element_type=F32)
    found = []
    for a, index in enumerate(indices):
        held = [jnp.zeros((8, LANES), F32)] * 3
        for high in range(highs):
            hit = (index >> 8) == high + first_high
            for v in range(3):
                at = high * ROWS + v * 8
                held[v] = jnp.where(hit, every[at : at + 8, a * LANES : (a + 1) * LANES], held[v])
        first = held[0] + held[2]
        second = held[1] + jnp.roll(held[1], 4, axis=0)
        found.append((first, jnp.where(row_ids < 2, jnp.roll(first, 2, axis=0), second)))
    return found


def hybrid_pick(packed_ref, table_ref, indices, chunks, highs, xs, ys):
    near = matrix_pick(table_ref, indices, highs, 0)
    words = pick(
        lambda h: packed_ref[(2 * highs + h) * 8 : (2 * highs + h) * 8 + 8],
        chunks - 2 * highs,
        2 * highs,
        indices,
        [jnp.zeros((8, LANES), I32)] * len(indices),
        True,
    )
    found = []
    for a, index in enumerate(indices):
        first = index < highs * 256
        x, y = unpack_tile(words[a], xs, ys)
        found.append((jnp.where(first, near[a][0], x), jnp.where(first, near[a][1], y)))
    return found


def own_kernel(
    packed_ref,
    scale_ref,
    table_ref,
    connect_ref,
    comp_ref,
    dv_ref,
    own_x_ref,
    own_y_ref,
    rank_ref,
    ids_ref,
    *,
    chunks,
    groups,
    highs,
    **sizes,
):
    slot_loop(
        dv_ref,
        lambda row, place: ((place & (sizes["owned"] - 1)).astype(F32), comp_ref[row].astype(F32)),
        None,
        rank_ref,
        ids_ref,
        8,
        groups=groups,
        **sizes,
    )
    xs = scale_ref[0:8]
    ys = scale_ref[8:16]

    def fetch(b):
        rows = connect_ref[:, pl.ds(pl.multiple_of(b * LANES, LANES), LANES)]
        return tuple(jnp.broadcast_to(rows[a : a + 1], (8, LANES)) for a in range(4))

    def body(b, indices):
        found = hybrid_pick(packed_ref, table_ref, indices, chunks, highs, xs, ys)
        for a in range(4):
            at = pl.ds(pl.multiple_of(b * 32 + a * 8, 8), 8)
            own_x_ref[at] = found[a][0]
            own_y_ref[at] = found[a][1]
        return fetch(jnp.minimum(b + 1, groups - 1))

    def several(turn, indices):
        for k in range(4):
            indices = body(turn * 4 + k, indices)
        return indices

    lax.fori_loop(0, groups // 4, several, fetch(jnp.int32(0)))


def slot_loop(dv_ref, values_of, rank_ref, write_rank_ref, out_ref, stride, *, domains, groups, owned, slots, cap):
    shift = owned.bit_length() - 1
    owner_ids = lax.broadcasted_iota(I32, (domains, LANES), 0)
    owner_names = owner_ids.astype(F32).astype(BF16)
    rank_names = lax.broadcasted_iota(I32, (cap, LANES), 0).astype(F32).astype(BF16)
    one = jnp.ones((cap, LANES), BF16)
    zero = jnp.zeros((cap, LANES), BF16)
    none = jnp.zeros((domains, LANES), BF16)
    before = lax.broadcasted_iota(I32, (LANES, LANES), 0) < lax.broadcasted_iota(I32, (LANES, LANES), 1)
    before = jnp.concatenate(
        [jnp.where(before, 1.0, 0.0).astype(BF16), jnp.ones((LANES, LANES), BF16)], axis=1
    )
    block_rows = slots // LANES

    def ranks_of(places):
        owners = [jnp.where(owner_ids == (place >> shift), 1.0, 0.0) for place in places]
        counts = jnp.dot(
            jnp.concatenate([o.astype(BF16) for o in owners], axis=0), before, preferred_element_type=F32
        )
        base = jnp.zeros((domains, LANES), F32)
        ranks = []
        for j in range(block_rows):
            count = counts[j * domains : (j + 1) * domains]
            ranks.append(jnp.sum(owners[j] * (count[:, 0:LANES] + base), axis=0, keepdims=True))
            base = base + count[:, LANES : 2 * LANES]
        return ranks

    @pl.loop(0, groups // (2 * block_rows))
    def _(pair):
        sums = []
        for parity in range(2):
            rows = [pl.ds(pair * 2 * block_rows + parity * block_rows + j, 1) for j in range(block_rows)]
            places = [dv_ref[row] for row in rows]
            ranks = [rank_ref[row] for row in rows] if write_rank_ref is None else ranks_of(places)
            left = []
            right = []
            for row, place, rank in zip(rows, places, ranks):
                if write_rank_ref is not None:
                    write_rank_ref[row] = rank
                right.append(jnp.where(rank_names == tall_row(rank, cap), one, zero))
                hit = owner_names == tall_row((place >> shift).astype(F32), domains)
                pieces = []
                for value in values_of(row, place):
                    rough = value.astype(BF16).astype(F32)
                    pieces.append(jnp.where(hit, tall_row(rough, domains), none))
                    pieces.append(jnp.where(hit, tall_row(value - rough, domains), none))
                left.append(jnp.concatenate(pieces, axis=0))
            moved = lax.dot_general(
                jnp.concatenate(left, axis=1),
                jnp.concatenate(right, axis=1),
                (((1,), (1,)), ((), ())),
                preferred_element_type=F32,
            )
            parts = [moved[p * domains : (p + 1) * domains] for p in range(4)]
            sums.append([parts[2 * v] + parts[2 * v + 1] for v in range(2)])
        for v in range(2):
            out_ref[pl.ds(v * 4 + pair, domains, stride=stride)] = jnp.concatenate([sums[0][v], sums[1][v]], axis=1)


def spread_matrix(flip):
    shape = (24, 32) if not flip else (32, 24)
    narrow = lax.broadcasted_iota(I32, shape, 1 if flip else 0)
    wide = lax.broadcasted_iota(I32, shape, 0 if flip else 1)
    hit = (narrow // 4 == wide % 8) & (narrow % 4 == wide // 8)
    return jnp.where(hit, 1.0, 0.0).astype(F32)


def three_parts(x):
    parts = []
    for _ in range(3):
        part = x.astype(BF16)
        parts.append(part)
        x = x - part.astype(F32)
    return parts


def dot(a, b):
    return jnp.dot(a, b, precision=lax.Precision.HIGHEST, preferred_element_type=F32)


def main_kernel(
    here_ref,
    recv_ref,
    own_x_ref,
    own_y_ref,
    rank_ref,
    ids_ref,
    connect_ref,
    comp_ref,
    dv_ref,
    s_memb_ref,
    s_bend_ref,
    k_memb_ref,
    k_bend_ref,
    out_ref,
    ghost_ref,
    wide_ref,
    table_ref,
    panel_ref,
    fail_ref,
    best_ref,
    slope_ref,
    fixed_ref,
    stats_ref,
    *,
    own,
    groups,
    domains,
    iface,
    comps,
    ghost_highs,
    owned,
    slots,
    cap,
):
    rows = iface // LANES
    ghosts = len(OFFSETS) * rows
    here = here_ref[0]
    sources = [lax.rem(here + offset + domains, domains) for offset in OFFSETS]

    def x_of(h):
        return recv_ref[sources[h // rows], (h % rows) * 16 : (h % rows) * 16 + 6]

    def y_of(h):
        return recv_ref[sources[h // rows], (h % rows) * 16 + 8 : (h % rows) * 16 + 14]

    fill_table(x_of, y_of, ghost_highs, wide_ref, table_ref)
    kept = range(2 * ghost_highs, ghosts)
    x_inv, x_scale = scales_of(x_of, kept, DISP_TOP)
    y_inv, y_scale = scales_of(y_of, kept, ADJ_TOP)
    gx = pad_rows(x_scale)
    gy = pad_rows(y_scale)
    x_inv = jnp.broadcast_to(x_inv, (6, LANES))
    y_inv = jnp.broadcast_to(y_inv, (6, LANES))
    for h in kept:

        def store(row, many, value, h=h):
            at = (h - kept[0]) * 8 + row
            ghost_ref[at : at + many] = value

        pack_tile(x_of(h), y_of(h), x_inv, y_inv, store)
    tiles = groups // 8
    panel_ref[...] = jnp.zeros(panel_ref.shape, F32)

    def panel_step(tile, first, span):
        at = pl.ds(pl.multiple_of(tile * 8, 8), 8)

        def row_of(h):
            k = h % 16
            row = (k // 4) * 16 + (k % 4 // 2) * 8 + 6 + k % 2
            return jnp.broadcast_to(recv_ref[first + h // 16, row : row + 1], (8, LANES))

        panel_ref[at] = pick(row_of, span * 16, first * 16, [dv_ref[at]], [panel_ref[at]], True)[0]

    @pl.loop(0, domains // 8)
    def _(turn):
        panel_step(0, turn * 8, 8)

    wide = spread_matrix(False)
    tall = spread_matrix(True)
    weights = jnp.concatenate(
        [
            dot(s_memb_ref[...], wide),
            dot(s_bend_ref[...], wide),
            dot(tall, dot(k_memb_ref[...], wide)),
            dot(tall, dot(k_bend_ref[...], wide)),
        ],
        axis=0,
    )
    w = three_parts(weights)
    stacked_weights = jnp.concatenate([w[0], w[0], w[1], w[0], w[1], w[2]], axis=1)
    names = lax.broadcasted_iota(I32, (8, LANES), 0)
    combs = comps // 8
    best_ref[...] = jnp.full(best_ref.shape, LOW, F32)

    def gather(b):
        lanes = pl.ds(pl.multiple_of(b * LANES, LANES), LANES)
        rows = connect_ref[:, lanes]
        indices = [jnp.broadcast_to(rows[a : a + 1], (8, LANES)) for a in range(4)]
        found = matrix_pick(table_ref, indices, ghost_highs, own // 2)
        moves = []
        costs = []
        words = pick(
            lambda h: ghost_ref[h * 8 : h * 8 + 8],
            len(kept),
            own + kept[0],
            indices,
            [jnp.zeros((8, LANES), I32)] * 4,
            True,
        )
        for a in range(4):
            x, y = unpack_tile(words[a], gx, gy)
            far = indices[a] >= own * LANES
            farther = indices[a] >= (own + kept[0]) * LANES
            at = pl.ds(pl.multiple_of(b * 32 + a * 8, 8), 8)
            moves.append(jnp.where(farther, x, jnp.where(far, found[a][0], own_x_ref[at])))
            costs.append(jnp.where(farther, y, jnp.where(far, found[a][1], own_y_ref[at])))
        panel_step(jnp.minimum(b // 8 + 1, tiles - 1), lax.rem(b, 8) * (domains // 8), domains // 8)
        return jnp.concatenate(moves, axis=0), jnp.concatenate(costs, axis=0)

    def dense(b, found):
        x = three_parts(found[0])
        part = jnp.dot(
            stacked_weights,
            jnp.concatenate([x[0], x[1], x[0], x[2], x[1], x[0]], axis=0),
            preferred_element_type=F32,
        )
        row = pl.ds(b, 1)
        panel = panel_ref[row]
        bending = part[8:16]
        stress = part[0:8] + panel * bending
        failure = jnp.sum(stress * stress, axis=0, keepdims=True) / 8.0
        slope_ref[row] = jnp.sum(stress * bending, axis=0, keepdims=True) * (2.0 / 8.0)
        stiff = part[16:48] + (3.0 * panel * panel) * part[48:80]
        fixed_ref[row] = jnp.sum(found[1] * stiff, axis=0, keepdims=True)
        fail_ref[row] = failure
        away = comp_ref[row] - names
        for c in range(combs):
            held = best_ref[c * 8 : c * 8 + 8]
            best_ref[c * 8 : c * 8 + 8] = jnp.maximum(held, jnp.where(away == c * 8, failure, LOW))

    def several(turn, found):
        for k in range(3):
            later = gather(turn * 3 + k + 1)
            dense(turn * 3 + k, found)
            found = later
        return found

    dense(groups - 1, lax.fori_loop(0, (groups - 1) // 3, several, gather(jnp.int32(0))))

    stats_ref[0] = jnp.zeros((8, LANES), F32)
    bands = (comps + LANES - 1) // LANES
    diagonal = lax.broadcasted_iota(I32, (LANES, LANES), 0) == lax.broadcasted_iota(I32, (LANES, LANES), 1)

    def to_rows(reduce, start):
        for band in range(bands):
            many = min(LANES, comps - band * LANES)
            column = reduce(best_ref[band * LANES : band * LANES + many], axis=1, keepdims=True)
            row = jnp.sum(jnp.where(diagonal[0:many], column, 0.0), axis=0, keepdims=True)
            stats_ref[0, start + band : start + band + 1] = row

    to_rows(jnp.max, 0)
    for t in range(tiles):
        block = slice(t * 8, t * 8 + 8)
        comp = comp_ref[block]
        low = comp & 127
        high = comp >> 7
        top = jnp.zeros((8, LANES), F32)
        for band in range(bands):
            tile = jnp.broadcast_to(stats_ref[0, band : band + 1], (8, LANES))
            top = jnp.where(high == band, lane_pick(tile, low), top)
        scaled = jnp.exp(SHARP * (fail_ref[block] - top))
        fail_ref[block] = scaled
        slope_ref[block] = slope_ref[block] * scaled

    part_of = combs // 2
    for half in range(2):

        def total_step(step, totals, half=half):
            totals = list(totals)
            for g in range(2):
                row = pl.ds(step * 2 + g, 1)
                away = comp_ref[row] - names
                value = fail_ref[row]
                for c in range(part_of):
                    totals[c] = totals[c] + jnp.where(away == (half * part_of + c) * 8, value, 0.0)
            return tuple(totals)

        totals = lax.fori_loop(0, groups // 2, total_step, (jnp.zeros((8, LANES), F32),) * part_of)
        for c in range(part_of):
            at = (half * part_of + c) * 8
            best_ref[at : at + 8] = totals[c]
    to_rows(jnp.sum, 4)

    slot_loop(
        dv_ref,
        lambda row, place: (fixed_ref[row], slope_ref[row]),
        rank_ref,
        None,
        out_ref,
        24,
        domains=domains,
        groups=groups,
        owned=owned,
        slots=slots,
        cap=cap,
    )
    mine = stats_ref[0]
    for d in range(domains):
        out_ref[d * 24 + 8 : d * 24 + 16] = ids_ref[d * 8 : d * 8 + 8]
        out_ref[d * 24 + 16 : d * 24 + 24] = mine


def tall_row(row, many):
    tile = jnp.broadcast_to(row, (16, LANES)).astype(BF16)
    return jnp.concatenate([tile] * (many // 16), axis=0)


def last_kernel(recv_ref, mult_ref, ks_ref, sum_ref, fold_ref, *, domains, comps, owned):
    peak = recv_ref[0, 16:20]
    for s in range(1, domains):
        peak = jnp.maximum(peak, recv_ref[s, 16:20])
    total = jnp.zeros_like(peak)
    for s in range(domains):
        total = total + recv_ref[s, 20:24] * jnp.exp(SHARP * (recv_ref[s, 16:20] - peak))
    ks = peak + jnp.log(total) / SHARP
    bands = (comps + LANES - 1) // LANES
    mults = []
    for band in range(bands):
        many = min(LANES, comps - band * LANES)
        span = slice(band * LANES, band * LANES + many)
        ks_ref[0:1, span] = ks[band : band + 1, 0:many]
        mult = mult_ref[0:1, span]
        if many < LANES:
            mult = jnp.concatenate([mult, jnp.zeros((1, LANES - many), F32)], axis=1)
        mults.append(mult)
    factor = jnp.concatenate(mults, axis=0) / total[0:bands]
    half = LANES // 2
    outer = owned // half
    outer_ids = lax.broadcasted_iota(I32, (outer, LANES), 0).astype(F32).astype(BF16)
    inner_ids = lax.broadcasted_iota(I32, (half, LANES), 0).astype(F32).astype(BF16)
    one = jnp.ones((half, LANES), BF16)
    zero = jnp.zeros((half, LANES), BF16)
    none = jnp.zeros((outer, LANES), BF16)

    def part_sum(sources):
        left = []
        right = []
        for s in sources:
            share = jnp.exp(SHARP * (recv_ref[s, 16 : 16 + bands] - peak[0:bands])) * factor
            values = recv_ref[s, 0:8]
            labels = recv_ref[s, 8:16].astype(I32)
            low = labels & 127
            high = labels >> 7
            weight = jnp.zeros((8, LANES), F32)
            for band in range(bands):
                tile = jnp.broadcast_to(share[band : band + 1], (8, LANES))
                weight = jnp.where(high == band, lane_pick(tile, low), weight)
            terms = values + jnp.roll(weight * values, 4, axis=0)
            roughs = terms.astype(BF16).astype(F32)
            fines = terms - roughs
            outers = (labels >> 6).astype(F32)
            inners = (labels & 63).astype(F32)
            for r in range(4):
                row = slice(r, r + 1)
                hit = outer_ids == tall_row(outers[row], outer)
                left.append(
                    jnp.concatenate(
                        [
                            jnp.where(hit, tall_row(roughs[row], outer), none),
                            jnp.where(hit, tall_row(fines[row], outer), none),
                        ],
                        axis=0,
                    )
                )
                right.append(jnp.where(inner_ids == tall_row(inners[row], half), one, zero))
        both = lax.dot_general(
            jnp.concatenate(left, axis=1),
            jnp.concatenate(right, axis=1),
            (((1,), (1,)), ((), ())),
            preferred_element_type=F32,
        )
        return both[0:outer] + both[outer : 2 * outer]

    def step(turn, sums):
        return tuple(sums[m] + part_sum([turn * 4 + m * 2 + j for j in range(2)]) for m in range(2))

    empty = jnp.zeros((outer, half), F32)
    sums = lax.fori_loop(0, domains // 4, step, (empty, empty))
    fold_ref[:, 0:half] = sums[0] + sums[1]
    folded = jnp.concatenate(
        [fold_ref[pl.ds(parity, outer // 2, stride=2)][:, 0:half] for parity in range(2)], axis=1
    )
    for l in range(sum_ref.shape[0]):
        sum_ref[l] = folded


def vmem():
    return pl.BlockSpec(memory_space=pltpu.VMEM)


def smem():
    return pl.BlockSpec(memory_space=pltpu.SMEM)


def per_device(
    displacement, adjoint, send_list, connect, elem_comp, elem_dv, thickness, multiplier, k_memb, k_bend, s_memb, s_bend
):
    domains = lax.axis_size("dom")
    here = lax.axis_index("dom").astype(I32).reshape(1)
    comps = multiplier.shape[1]
    nodes = displacement.shape[2]
    elems = connect.shape[1]
    iface = send_list.shape[2]
    own = nodes // LANES
    groups = elems // LANES
    block = 4 * iface // LANES * 4
    sds = jax.ShapeDtypeStruct
    near = pltpu.VMEM

    def close(x):
        return pltpu.with_memory_space_constraint(x, pltpu.VMEM)

    def far(x):
        return pltpu.with_memory_space_constraint(x, pltpu.HBM)


    disp = far(displacement.reshape(-1, LANES))
    adj = far(adjoint.reshape(-1, LANES))
    connect = far(connect)
    highs = HIGHS
    ghost_highs = GHOST_HIGHS

    packed, scale, table, send = pl.pallas_call(
        functools.partial(send_kernel, chunks=own, domains=domains, iface=iface, highs=highs),
        out_shape=(
            pltpu.HBM((own * 8, LANES), I32),
            pltpu.HBM((16, LANES), F32),
            pltpu.HBM((highs * ROWS, 256), BF16),
            sds((domains, block, LANES), F32),
        ),
        in_specs=[smem()] + [vmem()] * 4,
        out_specs=(vmem(),) * 4,
        scratch_shapes=[pltpu.VMEM((highs * ROWS, 256), F32)],
        compiler_params=pltpu.CompilerParams(vmem_limit_bytes=ROOM),
        name="send_pick",
    )(here, disp, adj, far(send_list), far(thickness.reshape(-1, LANES)))
    recv = lax.all_to_all(send, "dom", 0, 0, tiled=True)
    comp = far(elem_comp.reshape(-1, LANES))
    dv = far(elem_dv.reshape(-1, LANES))
    owned = thickness.shape[0]
    own_x, own_y, ranks, ids = pl.pallas_call(
        functools.partial(
            own_kernel, chunks=own, groups=groups, highs=highs, domains=domains, owned=owned, slots=SLICE, cap=CAP
        ),
        out_shape=(near((groups * 32, LANES), F32),) * 2 + (near((groups, LANES), F32), near((domains * 8, LANES), F32)),
        in_specs=[vmem()] * 6,
        out_specs=(vmem(),) * 4,
        compiler_params=pltpu.CompilerParams(vmem_limit_bytes=ROOM),
        name="own_pick",
        cost_estimate=pl.CostEstimate(flops=0, transcendentals=0, bytes_accessed=60_000_000),
    )(far(packed), far(scale), far(table), connect, comp, dv)
    mine = pl.pallas_call(
        functools.partial(
            main_kernel,
            own=own,
            groups=groups,
            domains=domains,
            iface=iface,
            comps=comps,
            ghost_highs=ghost_highs,
            owned=owned,
            slots=SLICE,
            cap=CAP,
        ),
        out_shape=near((domains * 24, LANES), F32),
        in_specs=[smem()] + [vmem()] * 12,
        out_specs=vmem(),
        scratch_shapes=[
            pltpu.VMEM(((len(OFFSETS) * iface // LANES - 2 * ghost_highs) * 8, LANES), I32),
            pltpu.VMEM((ghost_highs * ROWS, 256), F32),
            pltpu.VMEM((ghost_highs * ROWS, 256), BF16),
            pltpu.VMEM((groups, LANES), F32),
            pltpu.VMEM((groups, LANES), F32),
            pltpu.VMEM((comps, LANES), F32),
            pltpu.VMEM((groups, LANES), F32),
            pltpu.VMEM((groups, LANES), F32),
            pltpu.VMEM((1, 8, LANES), F32),
        ],
        compiler_params=pltpu.CompilerParams(vmem_limit_bytes=ROOM),
        name="element_work",
    )(here, close(recv), close(own_x), close(own_y), close(ranks), close(ids), connect, comp, dv, far(s_memb), far(s_bend), far(k_memb), far(k_bend))
    everyone = lax.all_to_all(mine.reshape(domains, 24, LANES), "dom", 0, 0, tiled=True)
    loads = lax.axis_size("load")
    ks_value, sums = pl.pallas_call(
        functools.partial(last_kernel, domains=domains, comps=comps, owned=owned),
        out_shape=(sds((1, comps), F32), near((loads, owned // LANES, LANES), F32)),
        in_specs=[vmem()] * 2,
        out_specs=(vmem(),) * 2,
        scratch_shapes=[pltpu.VMEM((owned * 2 // LANES, LANES), F32)],
        compiler_params=pltpu.CompilerParams(vmem_limit_bytes=ROOM),
        name="weigh_and_sum",
    )(close(everyone), far(multiplier))
    sensitivity = lax.all_to_all(sums, "load", 0, 0, tiled=True).sum(axis=0).reshape(-1)
    return ks_value, sensitivity


def solution(mesh):
    in_specs = (
        P("load", None, "dom"),
        P("load", None, "dom"),
        P("dom", None, None),
        P(None, "dom"),
        P("dom"),
        P("dom"),
        P("dom"),
        P("load", None),
        P(),
        P(),
        P(),
        P(),
    )
    return jax.shard_map(
        per_device, mesh=mesh, in_specs=in_specs, out_specs=(P("load", None), P("dom")), check_vma=False
    )
```

```python
import functools

import jax
import jax.numpy as jnp
from jax import lax
from jax.experimental import pallas as pl
from jax.experimental.pallas import tpu as pltpu
from jax.sharding import PartitionSpec as P

NBR = 3
ROWS = 24
HIGHS = 18
GHOST_HIGHS = 8
SLICE = 1024
CAP = 64
ROOM = 16 * 1024 * 1024
SHARP = 50.0
LOW = -1e30
LANES = 128
DISP_TOP = 8388600.0
ADJ_TOP = 131000.0
ADJ_MID = 131072
OFFSETS = tuple(j - NBR if j < NBR else j - NBR + 1 for j in range(2 * NBR))
I32 = jnp.int32
F32 = jnp.float32
BF16 = jnp.bfloat16


def lane_pick(table, index):
    return jnp.take_along_axis(table, index, axis=1, mode="promise_in_bounds")


def row_shifts(rows):
    row = lax.broadcasted_iota(I32, (rows, LANES), 0)
    return (row % 3) * 10


def scales_of(x_of, tiles, top):
    best = jnp.abs(x_of(tiles[0]))
    for h in tiles[1:]:
        best = jnp.maximum(best, jnp.abs(x_of(h)))
    most = jnp.maximum(jnp.max(best, axis=1, keepdims=True), 1e-30)
    return top / most, most / top


def pack_tile(x, y, x_inv, y_inv, store):
    q = jnp.floor(x * x_inv + 0.5).astype(I32)
    u = jnp.floor(y * y_inv + 0.5).astype(I32) + ADJ_MID
    store(0, 6, (q << 8) | (u & 255))
    high = (u >> 8) << row_shifts(6)
    store(6, 1, high[0:1] + high[1:2] + high[2:3])
    store(7, 1, high[3:4] + high[4:5] + high[5:6])


def unpack_tile(word, x_scale, y_scale):
    x = (word >> 8).astype(F32) * x_scale
    row = lax.broadcasted_iota(I32, (8, LANES), 0)
    first = jnp.broadcast_to(word[6:7], (8, LANES))
    second = jnp.broadcast_to(word[7:8], (8, LANES))
    high = (jnp.where(row < 3, first, second) >> row_shifts(8)) & 1023
    y = (((high << 8) | (word & 255)) - ADJ_MID).astype(F32) * y_scale
    return x, y


def pad_rows(column):
    return jnp.concatenate([jnp.broadcast_to(column, (6, LANES)), jnp.zeros((2, LANES), F32)], axis=0)


def pick(table_of, count, first_high, indices, starts, by_index):
    lows = [i & 127 for i in indices]
    highs = [(i >> 7) - first_high for i in indices]
    found = list(starts)
    steps = [(u, h) for h in range(count) for u in range(len(indices))]
    if by_index:
        steps = [(u, h) for u in range(len(indices)) for h in range(count)]
    for u, h in steps:
        found[u] = jnp.where(highs[u] == h, lane_pick(table_of(h), lows[u]), found[u])
    return found


def send_kernel(
    here_ref,
    disp_ref,
    adj_ref,
    list_ref,
    thick_ref,
    packed_ref,
    scale_ref,
    table_ref,
    send_ref,
    wide_ref,
    *,
    chunks,
    domains,
    iface,
    highs,
):
    rows = iface // LANES
    cut = lambda ref, h: ref[pl.ds(h, 6, stride=chunks)]
    x_inv, x_scale = scales_of(lambda h: cut(disp_ref, h), range(chunks), DISP_TOP)
    y_inv, y_scale = scales_of(lambda h: cut(adj_ref, h), range(chunks), ADJ_TOP)
    scale_ref[0:8] = pad_rows(x_scale)
    scale_ref[8:16] = pad_rows(y_scale)
    xs = scale_ref[0:8]
    ys = scale_ref[8:16]
    x_inv = jnp.broadcast_to(x_inv, (6, LANES))
    y_inv = jnp.broadcast_to(y_inv, (6, LANES))
    for h in range(chunks):

        def store(row, many, value, h=h):
            packed_ref[h * 8 + row : h * 8 + row + many] = value

        pack_tile(cut(disp_ref, h), cut(adj_ref, h), x_inv, y_inv, store)

    def thickness_rows(k, half):
        return thick_ref[k * 4 + half * 2 : k * 4 + half * 2 + 2]

    @pl.loop(0, domains)
    def _(d):
        for k in range(rows):
            for half in range(2):
                at = k * 16 + half * 8
                send_ref[d, at : at + 6] = jnp.zeros((6, LANES), F32)
                send_ref[d, at + 6 : at + 8] = thickness_rows(k, half)

    here = here_ref[0]
    row_ids = lax.broadcasted_iota(I32, (8, LANES), 0)
    fill_table(lambda h: cut(disp_ref, h), lambda h: cut(adj_ref, h), highs, wide_ref, table_ref)

    @pl.loop(0, len(OFFSETS) // 3)
    def _(turn):
        for step in range(3):
            j = turn * 3 + step
            offset = j - NBR + jnp.where(j >= NBR, 1, 0)
            target = lax.rem(here - offset + domains, domains)
            base = pl.multiple_of(target // 8 * 8, 8)
            indices = []
            for k in range(rows):
                tile = list_ref[0, pl.ds(base, 8), k * LANES : (k + 1) * LANES]
                row = jnp.sum(jnp.where(row_ids == target - base, tile, 0), axis=0, keepdims=True)
                indices.append(jnp.broadcast_to(row, (8, LANES)))
            found = hybrid_pick(packed_ref, table_ref, indices, chunks, highs, xs, ys)
            for k in range(rows):
                for half in range(2):
                    at = slice(k * 16 + half * 8, k * 16 + half * 8 + 8)
                    send_ref[target, at] = jnp.where(row_ids < 6, found[k][half], send_ref[target, at])


def fill_table(x_of, y_of, highs, wide_ref, table_ref):
    for high in range(highs):
        for half in range(2):
            lanes = slice(half * LANES, half * LANES + LANES)
            x = x_of(high * 2 + half)
            y = y_of(high * 2 + half)
            xh = x.astype(BF16).astype(F32)
            yh = y.astype(BF16).astype(F32)
            xl = x - xh
            yl = y - yh
            at = high * ROWS
            for piece in (xh, yh[0:2], yl[4:6], yh[2:6], yl[2:4], xl, yl[0:2]):
                wide_ref[at : at + piece.shape[0], lanes] = piece
                at += piece.shape[0]
    table_ref[...] = wide_ref[...].astype(BF16)


def matrix_pick(table_ref, indices, highs, first_high):
    row_ids = lax.broadcasted_iota(I32, (8, LANES), 0)
    names = lax.broadcasted_iota(I32, (256, LANES), 0).astype(F32).astype(BF16)
    one = jnp.ones((256, LANES), BF16)
    none = jnp.zeros((256, LANES), BF16)
    hot = [jnp.where(names == tall_row((i[0:1] & 255).astype(F32), 256), one, none) for i in indices]
    every = jnp.dot(table_ref[...], jnp.concatenate(hot, axis=1), preferred_element_type=F32)
    found = []
    for a, index in enumerate(indices):
        held = [jnp.zeros((8, LANES), F32)] * 3
        for high in range(highs):
            hit = (index >> 8) == high + first_high
            for v in range(3):
                at = high * ROWS + v * 8
                held[v] = jnp.where(hit, every[at : at + 8, a * LANES : (a + 1) * LANES], held[v])
        first = held[0] + held[2]
        second = held[1] + jnp.roll(held[1], 4, axis=0)
        found.append((first, jnp.where(row_ids < 2, jnp.roll(first, 2, axis=0), second)))
    return found


def hybrid_pick(packed_ref, table_ref, indices, chunks, highs, xs, ys):
    near = matrix_pick(table_ref, indices, highs, 0)
    words = pick(
        lambda h: packed_ref[(2 * highs + h) * 8 : (2 * highs + h) * 8 + 8],
        chunks - 2 * highs,
        2 * highs,
        indices,
        [jnp.zeros((8, LANES), I32)] * len(indices),
        True,
    )
    found = []
    for a, index in enumerate(indices):
        first = index < highs * 256
        x, y = unpack_tile(words[a], xs, ys)
        found.append((jnp.where(first, near[a][0], x), jnp.where(first, near[a][1], y)))
    return found


def own_kernel(
    packed_ref,
    scale_ref,
    table_ref,
    connect_ref,
    comp_ref,
    dv_ref,
    own_x_ref,
    own_y_ref,
    rank_ref,
    ids_ref,
    *,
    chunks,
    groups,
    highs,
    **sizes,
):
    slot_loop(
        dv_ref,
        lambda row, place: ((place & (sizes["owned"] - 1)).astype(F32), comp_ref[row].astype(F32)),
        None,
        rank_ref,
        ids_ref,
        8,
        groups=groups,
        **sizes,
    )
    xs = scale_ref[0:8]
    ys = scale_ref[8:16]

    def fetch(b):
        rows = connect_ref[:, pl.ds(pl.multiple_of(b * LANES, LANES), LANES)]
        return tuple(jnp.broadcast_to(rows[a : a + 1], (8, LANES)) for a in range(4))

    def body(b, indices):
        found = hybrid_pick(packed_ref, table_ref, indices, chunks, highs, xs, ys)
        for a in range(4):
            at = pl.ds(pl.multiple_of(b * 32 + a * 8, 8), 8)
            own_x_ref[at] = found[a][0]
            own_y_ref[at] = found[a][1]
        return fetch(jnp.minimum(b + 1, groups - 1))

    def several(turn, indices):
        for k in range(16):
            indices = body(turn * 16 + k, indices)
        return indices

    lax.fori_loop(0, groups // 16, several, fetch(jnp.int32(0)))


def slot_loop(dv_ref, values_of, rank_ref, write_rank_ref, out_ref, stride, *, domains, groups, owned, slots, cap):
    shift = owned.bit_length() - 1
    owner_ids = lax.broadcasted_iota(I32, (domains, LANES), 0)
    owner_names = owner_ids.astype(F32).astype(BF16)
    rank_names = lax.broadcasted_iota(I32, (cap, LANES), 0).astype(F32).astype(BF16)
    one = jnp.ones((cap, LANES), BF16)
    zero = jnp.zeros((cap, LANES), BF16)
    none = jnp.zeros((domains, LANES), BF16)
    before = lax.broadcasted_iota(I32, (LANES, LANES), 0) < lax.broadcasted_iota(I32, (LANES, LANES), 1)
    before = jnp.concatenate(
        [jnp.where(before, 1.0, 0.0).astype(BF16), jnp.ones((LANES, LANES), BF16)], axis=1
    )
    block_rows = slots // LANES

    def ranks_of(places):
        owners = [jnp.where(owner_ids == (place >> shift), 1.0, 0.0) for place in places]
        counts = jnp.dot(
            jnp.concatenate([o.astype(BF16) for o in owners], axis=0), before, preferred_element_type=F32
        )
        base = jnp.zeros((domains, LANES), F32)
        ranks = []
        for j in range(block_rows):
            count = counts[j * domains : (j + 1) * domains]
            ranks.append(jnp.sum(owners[j] * (count[:, 0:LANES] + base), axis=0, keepdims=True))
            base = base + count[:, LANES : 2 * LANES]
        return ranks

    @pl.loop(0, groups // (2 * block_rows))
    def _(pair):
        sums = []
        for parity in range(2):
            rows = [pl.ds(pair * 2 * block_rows + parity * block_rows + j, 1) for j in range(block_rows)]
            places = [dv_ref[row] for row in rows]
            ranks = [rank_ref[row] for row in rows] if write_rank_ref is None else ranks_of(places)
            left = []
            right = []
            for row, place, rank in zip(rows, places, ranks):
                if write_rank_ref is not None:
                    write_rank_ref[row] = rank
                right.append(jnp.where(rank_names == tall_row(rank, cap), one, zero))
                hit = owner_names == tall_row((place >> shift).astype(F32), domains)
                pieces = []
                for value in values_of(row, place):
                    rough = value.astype(BF16).astype(F32)
                    pieces.append(jnp.where(hit, tall_row(rough, domains), none))
                    pieces.append(jnp.where(hit, tall_row(value - rough, domains), none))
                left.append(jnp.concatenate(pieces, axis=0))
            moved = lax.dot_general(
                jnp.concatenate(left, axis=1),
                jnp.concatenate(right, axis=1),
                (((1,), (1,)), ((), ())),
                preferred_element_type=F32,
            )
            parts = [moved[p * domains : (p + 1) * domains] for p in range(4)]
            sums.append([parts[2 * v] + parts[2 * v + 1] for v in range(2)])
        for v in range(2):
            out_ref[pl.ds(v * 4 + pair, domains, stride=stride)] = jnp.concatenate([sums[0][v], sums[1][v]], axis=1)


def spread_matrix(flip):
    shape = (24, 32) if not flip else (32, 24)
    narrow = lax.broadcasted_iota(I32, shape, 1 if flip else 0)
    wide = lax.broadcasted_iota(I32, shape, 0 if flip else 1)
    hit = (narrow // 4 == wide % 8) & (narrow % 4 == wide // 8)
    return jnp.where(hit, 1.0, 0.0).astype(F32)


def three_parts(x):
    parts = []
    for _ in range(3):
        part = x.astype(BF16)
        parts.append(part)
        x = x - part.astype(F32)
    return parts


def dot(a, b):
    return jnp.dot(a, b, precision=lax.Precision.HIGHEST, preferred_element_type=F32)


def main_kernel(
    here_ref,
    recv_ref,
    own_x_ref,
    own_y_ref,
    rank_ref,
    ids_ref,
    connect_ref,
    comp_ref,
    dv_ref,
    s_memb_ref,
    s_bend_ref,
    k_memb_ref,
    k_bend_ref,
    out_ref,
    ghost_ref,
    wide_ref,
    table_ref,
    panel_ref,
    fail_ref,
    best_ref,
    slope_ref,
    fixed_ref,
    stats_ref,
    *,
    own,
    groups,
    domains,
    iface,
    comps,
    ghost_highs,
    owned,
    slots,
    cap,
):
    rows = iface // LANES
    ghosts = len(OFFSETS) * rows
    here = here_ref[0]
    sources = [lax.rem(here + offset + domains, domains) for offset in OFFSETS]

    def x_of(h):
        return recv_ref[sources[h // rows], (h % rows) * 16 : (h % rows) * 16 + 6]

    def y_of(h):
        return recv_ref[sources[h // rows], (h % rows) * 16 + 8 : (h % rows) * 16 + 14]

    fill_table(x_of, y_of, ghost_highs, wide_ref, table_ref)
    kept = range(2 * ghost_highs, ghosts)
    x_inv, x_scale = scales_of(x_of, kept, DISP_TOP)
    y_inv, y_scale = scales_of(y_of, kept, ADJ_TOP)
    gx = pad_rows(x_scale)
    gy = pad_rows(y_scale)
    x_inv = jnp.broadcast_to(x_inv, (6, LANES))
    y_inv = jnp.broadcast_to(y_inv, (6, LANES))
    for h in kept:

        def store(row, many, value, h=h):
            at = (h - kept[0]) * 8 + row
            ghost_ref[at : at + many] = value

        pack_tile(x_of(h), y_of(h), x_inv, y_inv, store)
    tiles = groups // 8
    panel_ref[...] = jnp.zeros(panel_ref.shape, F32)

    def panel_step(tile, first, span):
        at = pl.ds(pl.multiple_of(tile * 8, 8), 8)

        def row_of(h):
            k = h % 16
            row = (k // 4) * 16 + (k % 4 // 2) * 8 + 6 + k % 2
            return jnp.broadcast_to(recv_ref[first + h // 16, row : row + 1], (8, LANES))

        panel_ref[at] = pick(row_of, span * 16, first * 16, [dv_ref[at]], [panel_ref[at]], True)[0]

    @pl.loop(0, domains // 8)
    def _(turn):
        panel_step(0, turn * 8, 8)

    wide = spread_matrix(False)
    tall = spread_matrix(True)
    weights = jnp.concatenate(
        [
            dot(s_memb_ref[...], wide),
            dot(s_bend_ref[...], wide),
            dot(tall, dot(k_memb_ref[...], wide)),
            dot(tall, dot(k_bend_ref[...], wide)),
        ],
        axis=0,
    )
    w = three_parts(weights)
    stacked_weights = jnp.concatenate([w[0], w[0], w[1], w[0], w[1], w[2]], axis=1)
    names = lax.broadcasted_iota(I32, (8, LANES), 0)
    combs = comps // 8
    best_ref[...] = jnp.full(best_ref.shape, LOW, F32)

    def gather(b):
        lanes = pl.ds(pl.multiple_of(b * LANES, LANES), LANES)
        rows = connect_ref[:, lanes]
        indices = [jnp.broadcast_to(rows[a : a + 1], (8, LANES)) for a in range(4)]
        found = matrix_pick(table_ref, indices, ghost_highs, own // 2)
        moves = []
        costs = []
        words = pick(
            lambda h: ghost_ref[h * 8 : h * 8 + 8],
            len(kept),
            own + kept[0],
            indices,
            [jnp.zeros((8, LANES), I32)] * 4,
            True,
        )
        for a in range(4):
            x, y = unpack_tile(words[a], gx, gy)
            far = indices[a] >= own * LANES
            farther = indices[a] >= (own + kept[0]) * LANES
            at = pl.ds(pl.multiple_of(b * 32 + a * 8, 8), 8)
            moves.append(jnp.where(farther, x, jnp.where(far, found[a][0], own_x_ref[at])))
            costs.append(jnp.where(farther, y, jnp.where(far, found[a][1], own_y_ref[at])))
        panel_step(jnp.minimum(b // 8 + 1, tiles - 1), lax.rem(b, 8) * (domains // 8), domains // 8)
        return jnp.concatenate(moves, axis=0), jnp.concatenate(costs, axis=0)

    def dense(b, found):
        x = three_parts(found[0])
        part = jnp.dot(
            stacked_weights,
            jnp.concatenate([x[0], x[1], x[0], x[2], x[1], x[0]], axis=0),
            preferred_element_type=F32,
        )
        row = pl.ds(b, 1)
        panel = panel_ref[row]
        bending = part[8:16]
        stress = part[0:8] + panel * bending
        failure = jnp.sum(stress * stress, axis=0, keepdims=True) / 8.0
        slope_ref[row] = jnp.sum(stress * bending, axis=0, keepdims=True) * (2.0 / 8.0)
        stiff = part[16:48] + (3.0 * panel * panel) * part[48:80]
        fixed_ref[row] = jnp.sum(found[1] * stiff, axis=0, keepdims=True)
        fail_ref[row] = failure
        away = comp_ref[row] - names
        for c in range(combs):
            held = best_ref[c * 8 : c * 8 + 8]
            best_ref[c * 8 : c * 8 + 8] = jnp.maximum(held, jnp.where(away == c * 8, failure, LOW))

    def several(turn, found):
        for k in range(21):
            later = gather(turn * 21 + k + 1)
            dense(turn * 21 + k, found)
            found = later
        return found

    dense(groups - 1, lax.fori_loop(0, (groups - 1) // 21, several, gather(jnp.int32(0))))

    stats_ref[0] = jnp.zeros((8, LANES), F32)
    bands = (comps + LANES - 1) // LANES
    diagonal = lax.broadcasted_iota(I32, (LANES, LANES), 0) == lax.broadcasted_iota(I32, (LANES, LANES), 1)

    def to_rows(reduce, start):
        for band in range(bands):
            many = min(LANES, comps - band * LANES)
            column = reduce(best_ref[band * LANES : band * LANES + many], axis=1, keepdims=True)
            row = jnp.sum(jnp.where(diagonal[0:many], column, 0.0), axis=0, keepdims=True)
            stats_ref[0, start + band : start + band + 1] = row

    to_rows(jnp.max, 0)
    for t in range(tiles):
        block = slice(t * 8, t * 8 + 8)
        comp = comp_ref[block]
        low = comp & 127
        high = comp >> 7
        top = jnp.zeros((8, LANES), F32)
        for band in range(bands):
            tile = jnp.broadcast_to(stats_ref[0, band : band + 1], (8, LANES))
            top = jnp.where(high == band, lane_pick(tile, low), top)
        scaled = jnp.exp(SHARP * (fail_ref[block] - top))
        fail_ref[block] = scaled
        slope_ref[block] = slope_ref[block] * scaled

    part_of = combs // 2
    for half in range(2):

        def total_step(step, totals, half=half):
            totals = list(totals)
            for g in range(4):
                row = pl.ds(step * 4 + g, 1)
                away = comp_ref[row] - names
                value = fail_ref[row]
                for c in range(part_of):
                    totals[c] = totals[c] + jnp.where(away == (half * part_of + c) * 8, value, 0.0)
            return tuple(totals)

        totals = lax.fori_loop(0, groups // 4, total_step, (jnp.zeros((8, LANES), F32),) * part_of)
        for c in range(part_of):
            at = (half * part_of + c) * 8
            best_ref[at : at + 8] = totals[c]
    to_rows(jnp.sum, 4)

    slot_loop(
        dv_ref,
        lambda row, place: (fixed_ref[row], slope_ref[row]),
        rank_ref,
        None,
        out_ref,
        24,
        domains=domains,
        groups=groups,
        owned=owned,
        slots=slots,
        cap=cap,
    )
    mine = stats_ref[0]
    for d in range(domains):
        out_ref[d * 24 + 8 : d * 24 + 16] = ids_ref[d * 8 : d * 8 + 8]
        out_ref[d * 24 + 16 : d * 24 + 24] = mine


def tall_row(row, many):
    tile = jnp.broadcast_to(row, (16, LANES)).astype(BF16)
    return jnp.concatenate([tile] * (many // 16), axis=0)


def last_kernel(recv_ref, mult_ref, ks_ref, sum_ref, fold_ref, *, domains, comps, owned):
    peak = recv_ref[0, 16:20]
    for s in range(1, domains):
        peak = jnp.maximum(peak, recv_ref[s, 16:20])
    total = jnp.zeros_like(peak)
    for s in range(domains):
        total = total + recv_ref[s, 20:24] * jnp.exp(SHARP * (recv_ref[s, 16:20] - peak))
    ks = peak + jnp.log(total) / SHARP
    bands = (comps + LANES - 1) // LANES
    mults = []
    for band in range(bands):
        many = min(LANES, comps - band * LANES)
        span = slice(band * LANES, band * LANES + many)
        ks_ref[0:1, span] = ks[band : band + 1, 0:many]
        mult = mult_ref[0:1, span]
        if many < LANES:
            mult = jnp.concatenate([mult, jnp.zeros((1, LANES - many), F32)], axis=1)
        mults.append(mult)
    factor = jnp.concatenate(mults, axis=0) / total[0:bands]
    half = LANES // 2
    outer = owned // half
    outer_ids = lax.broadcasted_iota(I32, (outer, LANES), 0).astype(F32).astype(BF16)
    inner_ids = lax.broadcasted_iota(I32, (half, LANES), 0).astype(F32).astype(BF16)
    one = jnp.ones((half, LANES), BF16)
    zero = jnp.zeros((half, LANES), BF16)
    none = jnp.zeros((outer, LANES), BF16)

    def part_sum(sources):
        left = []
        right = []
        for s in sources:
            share = jnp.exp(SHARP * (recv_ref[s, 16 : 16 + bands] - peak[0:bands])) * factor
            values = recv_ref[s, 0:8]
            labels = recv_ref[s, 8:16].astype(I32)
            low = labels & 127
            high = labels >> 7
            weight = jnp.zeros((8, LANES), F32)
            for band in range(bands):
                tile = jnp.broadcast_to(share[band : band + 1], (8, LANES))
                weight = jnp.where(high == band, lane_pick(tile, low), weight)
            terms = values + jnp.roll(weight * values, 4, axis=0)
            roughs = terms.astype(BF16).astype(F32)
            fines = terms - roughs
            outers = (labels >> 6).astype(F32)
            inners = (labels & 63).astype(F32)
            for r in range(4):
                row = slice(r, r + 1)
                hit = outer_ids == tall_row(outers[row], outer)
                left.append(
                    jnp.concatenate(
                        [
                            jnp.where(hit, tall_row(roughs[row], outer), none),
                            jnp.where(hit, tall_row(fines[row], outer), none),
                        ],
                        axis=0,
                    )
                )
                right.append(jnp.where(inner_ids == tall_row(inners[row], half), one, zero))
        both = lax.dot_general(
            jnp.concatenate(left, axis=1),
            jnp.concatenate(right, axis=1),
            (((1,), (1,)), ((), ())),
            preferred_element_type=F32,
        )
        return both[0:outer] + both[outer : 2 * outer]

    def step(turn, sums):
        return tuple(sums[m] + part_sum([turn * 8 + m * 2 + j for j in range(2)]) for m in range(4))

    empty = jnp.zeros((outer, half), F32)
    sums = lax.fori_loop(0, domains // 8, step, (empty,) * 4)
    fold_ref[:, 0:half] = (sums[0] + sums[1]) + (sums[2] + sums[3])
    folded = jnp.concatenate(
        [fold_ref[pl.ds(parity, outer // 2, stride=2)][:, 0:half] for parity in range(2)], axis=1
    )
    for l in range(sum_ref.shape[0]):
        sum_ref[l] = folded


def vmem():
    return pl.BlockSpec(memory_space=pltpu.VMEM)


def smem():
    return pl.BlockSpec(memory_space=pltpu.SMEM)


def per_device(
    displacement, adjoint, send_list, connect, elem_comp, elem_dv, thickness, multiplier, k_memb, k_bend, s_memb, s_bend
):
    domains = lax.axis_size("dom")
    here = lax.axis_index("dom").astype(I32).reshape(1)
    comps = multiplier.shape[1]
    nodes = displacement.shape[2]
    elems = connect.shape[1]
    iface = send_list.shape[2]
    own = nodes // LANES
    groups = elems // LANES
    block = 4 * iface // LANES * 4
    sds = jax.ShapeDtypeStruct
    near = pltpu.VMEM

    def close(x):
        return pltpu.with_memory_space_constraint(x, pltpu.VMEM)

    def far(x):
        return pltpu.with_memory_space_constraint(x, pltpu.HBM)


    disp = far(displacement.reshape(-1, LANES))
    adj = far(adjoint.reshape(-1, LANES))
    connect = far(connect)
    highs = HIGHS
    ghost_highs = GHOST_HIGHS

    packed, scale, table, send = pl.pallas_call(
        functools.partial(send_kernel, chunks=own, domains=domains, iface=iface, highs=highs),
        out_shape=(
            pltpu.HBM((own * 8, LANES), I32),
            pltpu.HBM((16, LANES), F32),
            pltpu.HBM((highs * ROWS, 256), BF16),
            sds((domains, block, LANES), F32),
        ),
        in_specs=[smem()] + [vmem()] * 4,
        out_specs=(vmem(),) * 4,
        scratch_shapes=[pltpu.VMEM((highs * ROWS, 256), F32)],
        compiler_params=pltpu.CompilerParams(vmem_limit_bytes=ROOM),
        name="send_pick",
    )(here, disp, adj, far(send_list), far(thickness.reshape(-1, LANES)))
    recv = lax.all_to_all(send, "dom", 0, 0, tiled=True)
    comp = far(elem_comp.reshape(-1, LANES))
    dv = far(elem_dv.reshape(-1, LANES))
    owned = thickness.shape[0]
    own_x, own_y, ranks, ids = pl.pallas_call(
        functools.partial(
            own_kernel, chunks=own, groups=groups, highs=highs, domains=domains, owned=owned, slots=SLICE, cap=CAP
        ),
        out_shape=(near((groups * 32, LANES), F32),) * 2 + (near((groups, LANES), F32), near((domains * 8, LANES), F32)),
        in_specs=[vmem()] * 6,
        out_specs=(vmem(),) * 4,
        compiler_params=pltpu.CompilerParams(vmem_limit_bytes=ROOM),
        name="own_pick",
        cost_estimate=pl.CostEstimate(flops=0, transcendentals=0, bytes_accessed=60_000_000),
    )(far(packed), far(scale), far(table), connect, comp, dv)
    mine = pl.pallas_call(
        functools.partial(
            main_kernel,
            own=own,
            groups=groups,
            domains=domains,
            iface=iface,
            comps=comps,
            ghost_highs=ghost_highs,
            owned=owned,
            slots=SLICE,
            cap=CAP,
        ),
        out_shape=near((domains * 24, LANES), F32),
        in_specs=[smem()] + [vmem()] * 12,
        out_specs=vmem(),
        scratch_shapes=[
            pltpu.VMEM(((len(OFFSETS) * iface // LANES - 2 * ghost_highs) * 8, LANES), I32),
            pltpu.VMEM((ghost_highs * ROWS, 256), F32),
            pltpu.VMEM((ghost_highs * ROWS, 256), BF16),
            pltpu.VMEM((groups, LANES), F32),
            pltpu.VMEM((groups, LANES), F32),
            pltpu.VMEM((comps, LANES), F32),
            pltpu.VMEM((groups, LANES), F32),
            pltpu.VMEM((groups, LANES), F32),
            pltpu.VMEM((1, 8, LANES), F32),
        ],
        compiler_params=pltpu.CompilerParams(vmem_limit_bytes=ROOM),
        name="element_work",
    )(here, close(recv), close(own_x), close(own_y), close(ranks), close(ids), connect, comp, dv, far(s_memb), far(s_bend), far(k_memb), far(k_bend))
    everyone = lax.all_to_all(mine.reshape(domains, 24, LANES), "dom", 0, 0, tiled=True)
    loads = lax.axis_size("load")
    ks_value, sums = pl.pallas_call(
        functools.partial(last_kernel, domains=domains, comps=comps, owned=owned),
        out_shape=(sds((1, comps), F32), near((loads, owned // LANES, LANES), F32)),
        in_specs=[vmem()] * 2,
        out_specs=(vmem(),) * 2,
        scratch_shapes=[pltpu.VMEM((owned * 2 // LANES, LANES), F32)],
        compiler_params=pltpu.CompilerParams(vmem_limit_bytes=ROOM),
        name="weigh_and_sum",
    )(close(everyone), far(multiplier))
    sensitivity = lax.all_to_all(sums, "load", 0, 0, tiled=True).sum(axis=0).reshape(-1)
    return ks_value, sensitivity


def solution(mesh):
    in_specs = (
        P("load", None, "dom"),
        P("load", None, "dom"),
        P("dom", None, None),
        P(None, "dom"),
        P("dom"),
        P("dom"),
        P("dom"),
        P("load", None),
        P(),
        P(),
        P(),
        P(),
    )
    return jax.shard_map(
        per_device, mesh=mesh, in_specs=in_specs, out_specs=(P("load", None), P("dom")), check_vma=False
    )
```

```python
import functools

import jax
import jax.numpy as jnp
from jax import lax
from jax.experimental import pallas as pl
from jax.experimental.pallas import tpu as pltpu
from jax.sharding import PartitionSpec as P

NBR = 3
ROWS = 24
HIGHS = 18
GHOST_HIGHS = 8
SLICE = 1024
CAP = 64
ROOM = 16 * 1024 * 1024
SHARP = 50.0
LOW = -1e30
LANES = 128
DISP_TOP = 8388600.0
ADJ_TOP = 131000.0
ADJ_MID = 131072
OFFSETS = tuple(j - NBR if j < NBR else j - NBR + 1 for j in range(2 * NBR))
I32 = jnp.int32
F32 = jnp.float32
BF16 = jnp.bfloat16


def lane_pick(table, index):
    return jnp.take_along_axis(table, index, axis=1, mode="promise_in_bounds")


def row_shifts(rows):
    row = lax.broadcasted_iota(I32, (rows, LANES), 0)
    return (row % 3) * 10


def scales_of(x_of, tiles, top):
    best = jnp.abs(x_of(tiles[0]))
    for h in tiles[1:]:
        best = jnp.maximum(best, jnp.abs(x_of(h)))
    most = jnp.maximum(jnp.max(best, axis=1, keepdims=True), 1e-30)
    return top / most, most / top


def pack_tile(x, y, x_inv, y_inv, store):
    q = jnp.floor(x * x_inv + 0.5).astype(I32)
    u = jnp.floor(y * y_inv + 0.5).astype(I32) + ADJ_MID
    store(0, 6, (q << 8) | (u & 255))
    high = (u >> 8) << row_shifts(6)
    store(6, 1, high[0:1] + high[1:2] + high[2:3])
    store(7, 1, high[3:4] + high[4:5] + high[5:6])


def unpack_tile(word, x_scale, y_scale):
    x = (word >> 8).astype(F32) * x_scale
    row = lax.broadcasted_iota(I32, (8, LANES), 0)
    first = jnp.broadcast_to(word[6:7], (8, LANES))
    second = jnp.broadcast_to(word[7:8], (8, LANES))
    high = (jnp.where(row < 3, first, second) >> row_shifts(8)) & 1023
    y = (((high << 8) | (word & 255)) - ADJ_MID).astype(F32) * y_scale
    return x, y


def pad_rows(column):
    return jnp.concatenate([jnp.broadcast_to(column, (6, LANES)), jnp.zeros((2, LANES), F32)], axis=0)


def pick(table_of, count, first_high, indices, starts, by_index):
    lows = [i & 127 for i in indices]
    highs = [(i >> 7) - first_high for i in indices]
    found = list(starts)
    steps = [(u, h) for h in range(count) for u in range(len(indices))]
    if by_index:
        steps = [(u, h) for u in range(len(indices)) for h in range(count)]
    for u, h in steps:
        found[u] = jnp.where(highs[u] == h, lane_pick(table_of(h), lows[u]), found[u])
    return found


def send_kernel(
    here_ref,
    disp_ref,
    adj_ref,
    list_ref,
    thick_ref,
    packed_ref,
    scale_ref,
    table_ref,
    send_ref,
    wide_ref,
    *,
    chunks,
    domains,
    iface,
    highs,
):
    rows = iface // LANES
    cut = lambda ref, h: ref[pl.ds(h, 6, stride=chunks)]
    x_inv, x_scale = scales_of(lambda h: cut(disp_ref, h), range(chunks), DISP_TOP)
    y_inv, y_scale = scales_of(lambda h: cut(adj_ref, h), range(chunks), ADJ_TOP)
    scale_ref[0:8] = pad_rows(x_scale)
    scale_ref[8:16] = pad_rows(y_scale)
    xs = scale_ref[0:8]
    ys = scale_ref[8:16]
    x_inv = jnp.broadcast_to(x_inv, (6, LANES))
    y_inv = jnp.broadcast_to(y_inv, (6, LANES))
    for h in range(chunks):

        def store(row, many, value, h=h):
            packed_ref[h * 8 + row : h * 8 + row + many] = value

        pack_tile(cut(disp_ref, h), cut(adj_ref, h), x_inv, y_inv, store)

    def thickness_rows(k, half):
        return thick_ref[k * 4 + half * 2 : k * 4 + half * 2 + 2]

    @pl.loop(0, domains)
    def _(d):
        for k in range(rows):
            for half in range(2):
                at = k * 16 + half * 8
                send_ref[d, at : at + 6] = jnp.zeros((6, LANES), F32)
                send_ref[d, at + 6 : at + 8] = thickness_rows(k, half)

    here = here_ref[0]
    row_ids = lax.broadcasted_iota(I32, (8, LANES), 0)
    fill_table(lambda h: cut(disp_ref, h), lambda h: cut(adj_ref, h), highs, wide_ref, table_ref)

    @pl.loop(0, len(OFFSETS) // 3)
    def _(turn):
        for step in range(3):
            j = turn * 3 + step
            offset = j - NBR + jnp.where(j >= NBR, 1, 0)
            target = lax.rem(here - offset + domains, domains)
            base = pl.multiple_of(target // 8 * 8, 8)
            indices = []
            for k in range(rows):
                tile = list_ref[0, pl.ds(base, 8), k * LANES : (k + 1) * LANES]
                row = jnp.sum(jnp.where(row_ids == target - base, tile, 0), axis=0, keepdims=True)
                indices.append(jnp.broadcast_to(row, (8, LANES)))
            found = hybrid_pick(packed_ref, table_ref, indices, chunks, highs, xs, ys)
            for k in range(rows):
                for half in range(2):
                    at = slice(k * 16 + half * 8, k * 16 + half * 8 + 8)
                    send_ref[target, at] = jnp.where(row_ids < 6, found[k][half], send_ref[target, at])


def fill_table(x_of, y_of, highs, wide_ref, table_ref):
    for high in range(highs):
        for half in range(2):
            lanes = slice(half * LANES, half * LANES + LANES)
            x = x_of(high * 2 + half)
            y = y_of(high * 2 + half)
            xh = x.astype(BF16).astype(F32)
            yh = y.astype(BF16).astype(F32)
            xl = x - xh
            yl = y - yh
            at = high * ROWS
            for piece in (xh, yh[0:2], yl[4:6], yh[2:6], yl[2:4], xl, yl[0:2]):
                wide_ref[at : at + piece.shape[0], lanes] = piece
                at += piece.shape[0]
    table_ref[...] = wide_ref[...].astype(BF16)


def matrix_pick(table_ref, indices, highs, first_high):
    row_ids = lax.broadcasted_iota(I32, (8, LANES), 0)
    names = lax.broadcasted_iota(I32, (256, LANES), 0).astype(F32).astype(BF16)
    one = jnp.ones((256, LANES), BF16)
    none = jnp.zeros((256, LANES), BF16)
    hot = [jnp.where(names == tall_row((i[0:1] & 255).astype(F32), 256), one, none) for i in indices]
    every = jnp.dot(table_ref[...], jnp.concatenate(hot, axis=1), preferred_element_type=F32)
    found = []
    for a, index in enumerate(indices):
        held = [jnp.zeros((8, LANES), F32)] * 3
        for high in range(highs):
            hit = (index >> 8) == high + first_high
            for v in range(3):
                at = high * ROWS + v * 8
                held[v] = jnp.where(hit, every[at : at + 8, a * LANES : (a + 1) * LANES], held[v])
        first = held[0] + held[2]
        second = held[1] + jnp.roll(held[1], 4, axis=0)
        found.append((first, jnp.where(row_ids < 2, jnp.roll(first, 2, axis=0), second)))
    return found


def hybrid_pick(packed_ref, table_ref, indices, chunks, highs, xs, ys):
    near = matrix_pick(table_ref, indices, highs, 0)
    words = pick(
        lambda h: packed_ref[(2 * highs + h) * 8 : (2 * highs + h) * 8 + 8],
        chunks - 2 * highs,
        2 * highs,
        indices,
        [jnp.zeros((8, LANES), I32)] * len(indices),
        True,
    )
    found = []
    for a, index in enumerate(indices):
        first = index < highs * 256
        x, y = unpack_tile(words[a], xs, ys)
        found.append((jnp.where(first, near[a][0], x), jnp.where(first, near[a][1], y)))
    return found


def own_kernel(
    packed_ref,
    scale_ref,
    table_ref,
    connect_ref,
    comp_ref,
    dv_ref,
    s_memb_ref,
    s_bend_ref,
    k_memb_ref,
    k_bend_ref,
    own_x_ref,
    own_y_ref,
    rank_ref,
    ids_ref,
    weight_ref,
    *,
    chunks,
    groups,
    highs,
    **sizes,
):
    wide = spread_matrix(False)
    tall = spread_matrix(True)
    weights = jnp.concatenate(
        [
            dot(s_memb_ref[...], wide),
            dot(s_bend_ref[...], wide),
            dot(tall, dot(k_memb_ref[...], wide)),
            dot(tall, dot(k_bend_ref[...], wide)),
        ],
        axis=0,
    )
    w = three_parts(weights)
    weight_ref[...] = jnp.concatenate([w[0], w[0], w[1], w[0], w[1], w[2]], axis=1)
    slot_loop(
        dv_ref,
        lambda row, place: ((place & (sizes["owned"] - 1)).astype(F32), comp_ref[row].astype(F32)),
        None,
        rank_ref,
        ids_ref,
        8,
        groups=groups,
        **sizes,
    )
    xs = scale_ref[0:8]
    ys = scale_ref[8:16]

    def fetch(b):
        rows = connect_ref[:, pl.ds(pl.multiple_of(b * LANES, LANES), LANES)]
        return tuple(jnp.broadcast_to(rows[a : a + 1], (8, LANES)) for a in range(4))

    def body(b, indices):
        found = hybrid_pick(packed_ref, table_ref, indices, chunks, highs, xs, ys)
        for a in range(4):
            at = pl.ds(pl.multiple_of(b * 32 + a * 8, 8), 8)
            own_x_ref[at] = found[a][0]
            own_y_ref[at] = found[a][1]
        return fetch(jnp.minimum(b + 1, groups - 1))

    def several(turn, indices):
        for k in range(16):
            indices = body(turn * 16 + k, indices)
        return indices

    lax.fori_loop(0, groups // 16, several, fetch(jnp.int32(0)))


def slot_loop(dv_ref, values_of, rank_ref, write_rank_ref, out_ref, stride, *, domains, groups, owned, slots, cap):
    shift = owned.bit_length() - 1
    owner_ids = lax.broadcasted_iota(I32, (domains, LANES), 0)
    owner_names = owner_ids.astype(F32).astype(BF16)
    rank_names = lax.broadcasted_iota(I32, (cap, LANES), 0).astype(F32).astype(BF16)
    one = jnp.ones((cap, LANES), BF16)
    zero = jnp.zeros((cap, LANES), BF16)
    none = jnp.zeros((domains, LANES), BF16)
    before = lax.broadcasted_iota(I32, (LANES, LANES), 0) < lax.broadcasted_iota(I32, (LANES, LANES), 1)
    before = jnp.concatenate(
        [jnp.where(before, 1.0, 0.0).astype(BF16), jnp.ones((LANES, LANES), BF16)], axis=1
    )
    block_rows = slots // LANES

    def ranks_of(places):
        owners = [jnp.where(owner_ids == (place >> shift), 1.0, 0.0) for place in places]
        counts = jnp.dot(
            jnp.concatenate([o.astype(BF16) for o in owners], axis=0), before, preferred_element_type=F32
        )
        base = jnp.zeros((domains, LANES), F32)
        ranks = []
        for j in range(block_rows):
            count = counts[j * domains : (j + 1) * domains]
            ranks.append(jnp.sum(owners[j] * (count[:, 0:LANES] + base), axis=0, keepdims=True))
            base = base + count[:, LANES : 2 * LANES]
        return ranks

    @pl.loop(0, groups // (2 * block_rows))
    def _(pair):
        sums = []
        for parity in range(2):
            rows = [pl.ds(pair * 2 * block_rows + parity * block_rows + j, 1) for j in range(block_rows)]
            places = [dv_ref[row] for row in rows]
            ranks = [rank_ref[row] for row in rows] if write_rank_ref is None else ranks_of(places)
            left = []
            right = []
            for row, place, rank in zip(rows, places, ranks):
                if write_rank_ref is not None:
                    write_rank_ref[row] = rank
                right.append(jnp.where(rank_names == tall_row(rank, cap), one, zero))
                hit = owner_names == tall_row((place >> shift).astype(F32), domains)
                pieces = []
                for value in values_of(row, place):
                    rough = value.astype(BF16).astype(F32)
                    pieces.append(jnp.where(hit, tall_row(rough, domains), none))
                    pieces.append(jnp.where(hit, tall_row(value - rough, domains), none))
                left.append(jnp.concatenate(pieces, axis=0))
            moved = lax.dot_general(
                jnp.concatenate(left, axis=1),
                jnp.concatenate(right, axis=1),
                (((1,), (1,)), ((), ())),
                preferred_element_type=F32,
            )
            parts = [moved[p * domains : (p + 1) * domains] for p in range(4)]
            sums.append([parts[2 * v] + parts[2 * v + 1] for v in range(2)])
        for v in range(2):
            out_ref[pl.ds(v * 4 + pair, domains, stride=stride)] = jnp.concatenate([sums[0][v], sums[1][v]], axis=1)


def spread_matrix(flip):
    shape = (24, 32) if not flip else (32, 24)
    narrow = lax.broadcasted_iota(I32, shape, 1 if flip else 0)
    wide = lax.broadcasted_iota(I32, shape, 0 if flip else 1)
    hit = (narrow // 4 == wide % 8) & (narrow % 4 == wide // 8)
    return jnp.where(hit, 1.0, 0.0).astype(F32)


def three_parts(x):
    parts = []
    for _ in range(3):
        part = x.astype(BF16)
        parts.append(part)
        x = x - part.astype(F32)
    return parts


def dot(a, b):
    return jnp.dot(a, b, precision=lax.Precision.HIGHEST, preferred_element_type=F32)


def main_kernel(
    here_ref,
    recv_ref,
    own_x_ref,
    own_y_ref,
    rank_ref,
    ids_ref,
    connect_ref,
    comp_ref,
    dv_ref,
    weight_ref,
    out_ref,
    ghost_ref,
    wide_ref,
    table_ref,
    panel_ref,
    fail_ref,
    best_ref,
    slope_ref,
    fixed_ref,
    stats_ref,
    *,
    own,
    groups,
    domains,
    iface,
    comps,
    ghost_highs,
    owned,
    slots,
    cap,
):
    rows = iface // LANES
    ghosts = len(OFFSETS) * rows
    here = here_ref[0]
    sources = [lax.rem(here + offset + domains, domains) for offset in OFFSETS]

    def x_of(h):
        return recv_ref[sources[h // rows], (h % rows) * 16 : (h % rows) * 16 + 6]

    def y_of(h):
        return recv_ref[sources[h // rows], (h % rows) * 16 + 8 : (h % rows) * 16 + 14]

    fill_table(x_of, y_of, ghost_highs, wide_ref, table_ref)
    kept = range(2 * ghost_highs, ghosts)
    x_inv, x_scale = scales_of(x_of, kept, DISP_TOP)
    y_inv, y_scale = scales_of(y_of, kept, ADJ_TOP)
    gx = pad_rows(x_scale)
    gy = pad_rows(y_scale)
    x_inv = jnp.broadcast_to(x_inv, (6, LANES))
    y_inv = jnp.broadcast_to(y_inv, (6, LANES))
    for h in kept:

        def store(row, many, value, h=h):
            at = (h - kept[0]) * 8 + row
            ghost_ref[at : at + many] = value

        pack_tile(x_of(h), y_of(h), x_inv, y_inv, store)
    tiles = groups // 8
    panel_ref[...] = jnp.zeros(panel_ref.shape, F32)

    def panel_step(tile, first, span):
        at = pl.ds(pl.multiple_of(tile * 8, 8), 8)

        def row_of(h):
            k = h % 16
            row = (k // 4) * 16 + (k % 4 // 2) * 8 + 6 + k % 2
            return jnp.broadcast_to(recv_ref[first + h // 16, row : row + 1], (8, LANES))

        panel_ref[at] = pick(row_of, span * 16, first * 16, [dv_ref[at]], [panel_ref[at]], True)[0]

    @pl.loop(0, domains // 8)
    def _(turn):
        panel_step(0, turn * 8, 8)

    stacked_weights = weight_ref[...]
    names = lax.broadcasted_iota(I32, (8, LANES), 0)
    combs = comps // 8
    best_ref[...] = jnp.full(best_ref.shape, LOW, F32)

    def gather(b):
        lanes = pl.ds(pl.multiple_of(b * LANES, LANES), LANES)
        rows = connect_ref[:, lanes]
        indices = [jnp.broadcast_to(rows[a : a + 1], (8, LANES)) for a in range(4)]
        found = matrix_pick(table_ref, indices, ghost_highs, own // 2)
        moves = []
        costs = []
        words = pick(
            lambda h: ghost_ref[h * 8 : h * 8 + 8],
            len(kept),
            own + kept[0],
            indices,
            [jnp.zeros((8, LANES), I32)] * 4,
            True,
        )
        for a in range(4):
            x, y = unpack_tile(words[a], gx, gy)
            far = indices[a] >= own * LANES
            farther = indices[a] >= (own + kept[0]) * LANES
            at = pl.ds(pl.multiple_of(b * 32 + a * 8, 8), 8)
            moves.append(jnp.where(farther, x, jnp.where(far, found[a][0], own_x_ref[at])))
            costs.append(jnp.where(farther, y, jnp.where(far, found[a][1], own_y_ref[at])))
        panel_step(jnp.minimum(b // 8 + 1, tiles - 1), lax.rem(b, 8) * (domains // 8), domains // 8)
        return jnp.concatenate(moves, axis=0), jnp.concatenate(costs, axis=0)

    def dense(b, found):
        x = three_parts(found[0])
        part = jnp.dot(
            stacked_weights,
            jnp.concatenate([x[0], x[1], x[0], x[2], x[1], x[0]], axis=0),
            preferred_element_type=F32,
        )
        row = pl.ds(b, 1)
        panel = panel_ref[row]
        bending = part[8:16]
        stress = part[0:8] + panel * bending
        failure = jnp.sum(stress * stress, axis=0, keepdims=True) / 8.0
        slope_ref[row] = jnp.sum(stress * bending, axis=0, keepdims=True) * (2.0 / 8.0)
        stiff = part[16:48] + (3.0 * panel * panel) * part[48:80]
        fixed_ref[row] = jnp.sum(found[1] * stiff, axis=0, keepdims=True)
        fail_ref[row] = failure
        away = comp_ref[row] - names
        for c in range(combs):
            held = best_ref[c * 8 : c * 8 + 8]
            best_ref[c * 8 : c * 8 + 8] = jnp.maximum(held, jnp.where(away == c * 8, failure, LOW))

    def several(turn, found):
        for k in range(21):
            later = gather(turn * 21 + k + 1)
            dense(turn * 21 + k, found)
            found = later
        return found

    dense(groups - 1, lax.fori_loop(0, (groups - 1) // 21, several, gather(jnp.int32(0))))

    stats_ref[0] = jnp.zeros((8, LANES), F32)
    bands = (comps + LANES - 1) // LANES
    diagonal = lax.broadcasted_iota(I32, (LANES, LANES), 0) == lax.broadcasted_iota(I32, (LANES, LANES), 1)

    def to_rows(reduce, start):
        for band in range(bands):
            many = min(LANES, comps - band * LANES)
            column = reduce(best_ref[band * LANES : band * LANES + many], axis=1, keepdims=True)
            row = jnp.sum(jnp.where(diagonal[0:many], column, 0.0), axis=0, keepdims=True)
            stats_ref[0, start + band : start + band + 1] = row

    to_rows(jnp.max, 0)
    for t in range(tiles):
        block = slice(t * 8, t * 8 + 8)
        comp = comp_ref[block]
        low = comp & 127
        high = comp >> 7
        top = jnp.zeros((8, LANES), F32)
        for band in range(bands):
            tile = jnp.broadcast_to(stats_ref[0, band : band + 1], (8, LANES))
            top = jnp.where(high == band, lane_pick(tile, low), top)
        scaled = jnp.exp(SHARP * (fail_ref[block] - top))
        fail_ref[block] = scaled
        slope_ref[block] = slope_ref[block] * scaled

    part_of = combs // 2
    for half in range(2):

        def total_step(step, totals, half=half):
            totals = list(totals)
            for g in range(4):
                row = pl.ds(step * 4 + g, 1)
                away = comp_ref[row] - names
                value = fail_ref[row]
                for c in range(part_of):
                    totals[c] = totals[c] + jnp.where(away == (half * part_of + c) * 8, value, 0.0)
            return tuple(totals)

        totals = lax.fori_loop(0, groups // 4, total_step, (jnp.zeros((8, LANES), F32),) * part_of)
        for c in range(part_of):
            at = (half * part_of + c) * 8
            best_ref[at : at + 8] = totals[c]
    to_rows(jnp.sum, 4)

    slot_loop(
        dv_ref,
        lambda row, place: (fixed_ref[row], slope_ref[row]),
        rank_ref,
        None,
        out_ref,
        24,
        domains=domains,
        groups=groups,
        owned=owned,
        slots=slots,
        cap=cap,
    )
    mine = stats_ref[0]
    for d in range(domains):
        out_ref[d * 24 + 8 : d * 24 + 16] = ids_ref[d * 8 : d * 8 + 8]
        out_ref[d * 24 + 16 : d * 24 + 24] = mine


def tall_row(row, many):
    tile = jnp.broadcast_to(row, (16, LANES)).astype(BF16)
    return jnp.concatenate([tile] * (many // 16), axis=0)


def last_kernel(recv_ref, mult_ref, ks_ref, sum_ref, fold_ref, *, domains, comps, owned):
    peak = recv_ref[0, 16:20]
    for s in range(1, domains):
        peak = jnp.maximum(peak, recv_ref[s, 16:20])
    total = jnp.zeros_like(peak)
    for s in range(domains):
        total = total + recv_ref[s, 20:24] * jnp.exp(SHARP * (recv_ref[s, 16:20] - peak))
    ks = peak + jnp.log(total) / SHARP
    bands = (comps + LANES - 1) // LANES
    mults = []
    for band in range(bands):
        many = min(LANES, comps - band * LANES)
        span = slice(band * LANES, band * LANES + many)
        ks_ref[0:1, span] = ks[band : band + 1, 0:many]
        mult = mult_ref[0:1, span]
        if many < LANES:
            mult = jnp.concatenate([mult, jnp.zeros((1, LANES - many), F32)], axis=1)
        mults.append(mult)
    factor = jnp.concatenate(mults, axis=0) / total[0:bands]
    half = LANES // 2
    outer = owned // half
    outer_ids = lax.broadcasted_iota(I32, (outer, LANES), 0).astype(F32).astype(BF16)
    inner_ids = lax.broadcasted_iota(I32, (half, LANES), 0).astype(F32).astype(BF16)
    one = jnp.ones((half, LANES), BF16)
    zero = jnp.zeros((half, LANES), BF16)
    none = jnp.zeros((outer, LANES), BF16)

    def part_sum(sources):
        left = []
        right = []
        for s in sources:
            share = jnp.exp(SHARP * (recv_ref[s, 16 : 16 + bands] - peak[0:bands])) * factor
            values = recv_ref[s, 0:8]
            labels = recv_ref[s, 8:16].astype(I32)
            low = labels & 127
            high = labels >> 7
            weight = jnp.zeros((8, LANES), F32)
            for band in range(bands):
                tile = jnp.broadcast_to(share[band : band + 1], (8, LANES))
                weight = jnp.where(high == band, lane_pick(tile, low), weight)
            terms = values + jnp.roll(weight * values, 4, axis=0)
            roughs = terms.astype(BF16).astype(F32)
            fines = terms - roughs
            outers = (labels >> 6).astype(F32)
            inners = (labels & 63).astype(F32)
            for r in range(4):
                row = slice(r, r + 1)
                hit = outer_ids == tall_row(outers[row], outer)
                left.append(
                    jnp.concatenate(
                        [
                            jnp.where(hit, tall_row(roughs[row], outer), none),
                            jnp.where(hit, tall_row(fines[row], outer), none),
                        ],
                        axis=0,
                    )
                )
                right.append(jnp.where(inner_ids == tall_row(inners[row], half), one, zero))
        both = lax.dot_general(
            jnp.concatenate(left, axis=1),
            jnp.concatenate(right, axis=1),
            (((1,), (1,)), ((), ())),
            preferred_element_type=F32,
        )
        return both[0:outer] + both[outer : 2 * outer]

    def step(turn, sums):
        return tuple(sums[m] + part_sum([turn * 8 + m * 2 + j for j in range(2)]) for m in range(4))

    empty = jnp.zeros((outer, half), F32)
    sums = lax.fori_loop(0, domains // 8, step, (empty,) * 4)
    fold_ref[:, 0:half] = (sums[0] + sums[1]) + (sums[2] + sums[3])
    folded = jnp.concatenate(
        [fold_ref[pl.ds(parity, outer // 2, stride=2)][:, 0:half] for parity in range(2)], axis=1
    )
    for l in range(sum_ref.shape[0]):
        sum_ref[l] = folded


def vmem():
    return pl.BlockSpec(memory_space=pltpu.VMEM)


def smem():
    return pl.BlockSpec(memory_space=pltpu.SMEM)


def per_device(
    displacement, adjoint, send_list, connect, elem_comp, elem_dv, thickness, multiplier, k_memb, k_bend, s_memb, s_bend
):
    domains = lax.axis_size("dom")
    here = lax.axis_index("dom").astype(I32).reshape(1)
    comps = multiplier.shape[1]
    nodes = displacement.shape[2]
    elems = connect.shape[1]
    iface = send_list.shape[2]
    own = nodes // LANES
    groups = elems // LANES
    block = 4 * iface // LANES * 4
    sds = jax.ShapeDtypeStruct
    near = pltpu.VMEM

    def close(x):
        return pltpu.with_memory_space_constraint(x, pltpu.VMEM)

    def far(x):
        return pltpu.with_memory_space_constraint(x, pltpu.HBM)


    disp = far(displacement.reshape(-1, LANES))
    adj = far(adjoint.reshape(-1, LANES))
    connect = far(connect)
    highs = HIGHS
    ghost_highs = GHOST_HIGHS

    packed, scale, table, send = pl.pallas_call(
        functools.partial(send_kernel, chunks=own, domains=domains, iface=iface, highs=highs),
        out_shape=(
            pltpu.HBM((own * 8, LANES), I32),
            pltpu.HBM((16, LANES), F32),
            pltpu.HBM((highs * ROWS, 256), BF16),
            sds((domains, block, LANES), F32),
        ),
        in_specs=[smem()] + [vmem()] * 4,
        out_specs=(vmem(),) * 4,
        scratch_shapes=[pltpu.VMEM((highs * ROWS, 256), F32)],
        compiler_params=pltpu.CompilerParams(vmem_limit_bytes=ROOM),
        name="send_pick",
    )(here, disp, adj, far(send_list), far(thickness.reshape(-1, LANES)))
    recv = lax.all_to_all(send, "dom", 0, 0, tiled=True)
    comp = far(elem_comp.reshape(-1, LANES))
    dv = far(elem_dv.reshape(-1, LANES))
    owned = thickness.shape[0]
    own_x, own_y, ranks, ids, weights = pl.pallas_call(
        functools.partial(
            own_kernel, chunks=own, groups=groups, highs=highs, domains=domains, owned=owned, slots=SLICE, cap=CAP
        ),
        out_shape=(near((groups * 32, LANES), F32),) * 2 + (near((groups, LANES), F32), near((domains * 8, LANES), F32), near((80, 192), BF16)),
        in_specs=[vmem()] * 10,
        out_specs=(vmem(),) * 5,
        compiler_params=pltpu.CompilerParams(vmem_limit_bytes=ROOM),
        name="own_pick",
        cost_estimate=pl.CostEstimate(flops=0, transcendentals=0, bytes_accessed=60_000_000),
    )(far(packed), far(scale), far(table), connect, comp, dv, far(s_memb), far(s_bend), far(k_memb), far(k_bend))
    mine = pl.pallas_call(
        functools.partial(
            main_kernel,
            own=own,
            groups=groups,
            domains=domains,
            iface=iface,
            comps=comps,
            ghost_highs=ghost_highs,
            owned=owned,
            slots=SLICE,
            cap=CAP,
        ),
        out_shape=near((domains * 24, LANES), F32),
        in_specs=[smem()] + [vmem()] * 9,
        out_specs=vmem(),
        scratch_shapes=[
            pltpu.VMEM(((len(OFFSETS) * iface // LANES - 2 * ghost_highs) * 8, LANES), I32),
            pltpu.VMEM((ghost_highs * ROWS, 256), F32),
            pltpu.VMEM((ghost_highs * ROWS, 256), BF16),
            pltpu.VMEM((groups, LANES), F32),
            pltpu.VMEM((groups, LANES), F32),
            pltpu.VMEM((comps, LANES), F32),
            pltpu.VMEM((groups, LANES), F32),
            pltpu.VMEM((groups, LANES), F32),
            pltpu.VMEM((1, 8, LANES), F32),
        ],
        compiler_params=pltpu.CompilerParams(vmem_limit_bytes=ROOM),
        name="element_work",
    )(here, close(recv), close(own_x), close(own_y), close(ranks), close(ids), connect, comp, dv, close(weights))
    everyone = lax.all_to_all(mine.reshape(domains, 24, LANES), "dom", 0, 0, tiled=True)
    loads = lax.axis_size("load")
    ks_value, sums = pl.pallas_call(
        functools.partial(last_kernel, domains=domains, comps=comps, owned=owned),
        out_shape=(sds((1, comps), F32), near((loads, owned // LANES, LANES), F32)),
        in_specs=[vmem()] * 2,
        out_specs=(vmem(),) * 2,
        scratch_shapes=[pltpu.VMEM((owned * 2 // LANES, LANES), F32)],
        compiler_params=pltpu.CompilerParams(vmem_limit_bytes=ROOM),
        name="weigh_and_sum",
    )(close(everyone), far(multiplier))
    sensitivity = lax.all_to_all(sums, "load", 0, 0, tiled=True).sum(axis=0).reshape(-1)
    return ks_value, sensitivity


def solution(mesh):
    in_specs = (
        P("load", None, "dom"),
        P("load", None, "dom"),
        P("dom", None, None),
        P(None, "dom"),
        P("dom"),
        P("dom"),
        P("dom"),
        P("load", None),
        P(),
        P(),
        P(),
        P(),
    )
    return jax.shard_map(
        per_device, mesh=mesh, in_specs=in_specs, out_specs=(P("load", None), P("dom")), check_vma=False
    )
```
